32 devices in a mesh: dp: 4 (over z), ctx: 2 (over x), tensor: 4 (over y, core).
Axes of the slice: x: 2, y: 2, z: 4, core: 2. Of those that a mesh axis runs over, the one named last changes fastest.
Arguments:
- layer_input: bfloat16 [8, 2048, 1024], P('dp', 'ctx'), may hold values from -6 to 6
- cotangent: bfloat16 [8, 2048, 1024], P('dp', 'ctx'), may hold values from -6 to 6
- attn_gain: bfloat16 [1024], P('dp'), may hold values from 0.5 to 1.5
- query_weight: bfloat16 [1024, 1024], P('dp', 'tensor'), may hold values from -0.1875 to 0.1875
- key_weight: bfloat16 [1024, 512], P('dp', 'tensor'), may hold values from -0.1875 to 0.1875
- value_weight: bfloat16 [1024, 512], P('dp', 'tensor'), may hold values from -0.1875 to 0.1875
- query_gain: bfloat16 [64], P('dp'), may hold values from 1 to 2
- key_gain: bfloat16 [64], P('dp'), may hold values from 0.5 to 1.5
- out_weight: bfloat16 [1024, 1024], P('tensor', 'dp'), may hold values from -1.5 to 1.5
- ffn_gain: bfloat16 [1024], P('dp'), may hold values from 0.5 to 1.5
- gate_weight: bfloat16 [1024, 4608], P('dp', 'tensor'), may hold values from -0.1875 to 0.1875
- up_weight: bfloat16 [1024, 4608], P('dp', 'tensor'), may hold values from -0.1875 to 0.1875
- down_weight: bfloat16 [4608, 1024], P('tensor', 'dp'), may hold values from -0.09375 to 0.09375
Outputs:
- layer_output: bfloat16 [8, 2048, 1024], P('dp', 'ctx')
- input_grad: float32 [8, 2048, 1024], P('dp', 'ctx')
- attn_gain_grad: float32 [1024], P('dp')
- query_weight_grad: float32 [1024, 1024], P('dp', 'tensor')
- key_weight_grad: float32 [1024, 512], P('dp', 'tensor')
- value_weight_grad: float32 [1024, 512], P('dp', 'tensor')
- query_gain_grad: float32 [64], P('dp')
- key_gain_grad: float32 [64], P('dp')
- out_weight_grad: float32 [1024, 1024], P('tensor', 'dp')
- ffn_gain_grad: float32 [1024], P('dp')
- gate_weight_grad: float32 [1024, 4608], P('dp', 'tensor')
- up_weight_grad: float32 [1024, 4608], P('dp', 'tensor')
- down_weight_grad: float32 [4608, 1024], P('tensor', 'dp')
The draws below stay inside these ranges and needn't reach their ends.
All inputs are finite; a program needn't handle non-finite values.
Results may differ from the reference program's by a relative error of at most 0.024.
Values may be sent and summed in bfloat16 or wider, within the bound.
No kernel may reach another device: no remote copies, remote signals or barrier semaphores. Data moves between devices by JAX's collectives and lax.ppermute only.
A program may use at most 320 MiB of HBM per device.

```python
import math
import jax
import jax.numpy as jnp
from jax import lax

D = 1024
H = 16
KV = 8
HD = 64
FF = 4608
SEQ_LEN = 2048
NSEQ = 8


def level_of(rng, extent, cuts, smallest, top_value):
    level, own = 1.0, jax.random.fold_in(rng, 6)
    for position, parts in cuts:
        steps = jnp.exp(jax.random.uniform(jax.random.fold_in(own, position), (parts,), jnp.float32, smallest / len(cuts), top_value / len(cuts)))
        level = level * jnp.repeat(steps, extent[position] // parts).reshape([-1 if axis == position else 1 for axis in range(len(extent))])
    return level


def normal_values(key, dims, scale, most, split=(), held_as=jnp.bfloat16):
    level = level_of(key, dims, split, -0.22, 0.18) if split else 1.0
    entries = jax.random.normal(key, dims, jnp.float32) * scale * level
    return jnp.minimum(jnp.maximum(entries, -most), most).astype(held_as)


def setup_inputs(seed: int = 0) -> dict:
    keys = jax.random.split(jax.random.key(seed), 14)
    layer_input = normal_values(keys[0], (NSEQ, SEQ_LEN, D), 1.0, 6.0, ((0, 4), (1, 2)))
    cotangent = normal_values(keys[1], (NSEQ, SEQ_LEN, D), 1.0, 6.0, ((0, 4), (1, 2)))
    attn_gain = jnp.clip(1.0 + 0.1 * jax.random.normal(keys[2], (D,), jnp.float32), 0.5, 1.5).astype(jnp.bfloat16)
    query_weight = normal_values(keys[3], (D, H * HD), D ** -0.5, 0.1875, ((0, 4), (1, 4)))
    key_weight = normal_values(keys[4], (D, KV * HD), D ** -0.5, 0.1875, ((0, 4), (1, 4)))
    value_weight = normal_values(keys[5], (D, KV * HD), D ** -0.5, 0.1875, ((0, 4), (1, 4)))
    query_gain = jnp.clip(jnp.exp(math.log(2.0) - 0.6931472 * jax.random.uniform(keys[6], (HD,), jnp.float32) ** level_of(keys[6], (HD,), ((0, 4),), -0.2, 0.2)), 1.0, 2.0).astype(jnp.bfloat16)
    key_gain = jnp.clip(1.0 + 0.1 * jax.random.normal(keys[7], (HD,), jnp.float32), 0.5, 1.5).astype(jnp.bfloat16)
    out_weight = normal_values(keys[8], (H * HD, D), (H * HD // 64) ** -0.5, 1.5, ((0, 4), (1, 4)))
    ffn_gain = jnp.clip(1.0 + 0.1 * jax.random.normal(keys[9], (D,), jnp.float32), 0.5, 1.5).astype(jnp.bfloat16)
    gate_weight = normal_values(keys[10], (D, FF), D ** -0.5, 0.1875, ((0, 4), (1, 4)))
    up_weight = normal_values(keys[11], (D, FF), D ** -0.5, 0.1875, ((0, 4), (1, 4)))
    down_weight = normal_values(keys[12], (FF, D), FF ** -0.5, 0.09375, ((0, 4), (1, 4)))
    return {"layer_input": layer_input, "cotangent": cotangent, "attn_gain": attn_gain, "query_weight": query_weight, "key_weight": key_weight, "value_weight": value_weight, "query_gain": query_gain, "key_gain": key_gain, "out_weight": out_weight, "ffn_gain": ffn_gain, "gate_weight": gate_weight, "up_weight": up_weight, "down_weight": down_weight}


eps_norm = 1e-05
rope_base = 1000000.0

@jax.custom_vjp
def low(v):
    return lax.optimization_barrier(v.astype(jnp.bfloat16)).astype(jnp.float32)

@jax.custom_vjp
def low_back(v):
    return v

def low_keep(v):
    return (low(v), None)

def low_pass(kept, grad):
    return (grad,)

def back_keep(v):
    return (v, None)

def back_low(kept, grad):
    return (low(grad),)
low.defvjp(low_keep, low_pass)
low_back.defvjp(back_keep, back_low)

def rms_scale(field, norm_gain):
    return field * lax.rsqrt(lax.optimization_barrier(jnp.mean(field * field, axis=-1, keepdims=True)) + eps_norm) * norm_gain

def rope_tables(positions, head_width):
    frequency = rope_base ** (-jnp.arange(0, head_width, 2).astype(jnp.float32) / head_width)
    angles = positions.astype(jnp.float32)[:, None] * frequency[None, :]
    angles = jnp.concatenate([angles, angles], axis=-1)
    return (jnp.cos(angles), jnp.sin(angles))

def rotate(field, cosine_table, sine_table):
    half_width = field.shape[-1] // 2
    turned = jnp.concatenate([-field[..., half_width:], field[..., :half_width]], axis=-1)
    return field * cosine_table + turned * sine_table

def attention(queries, keys_rot, values):
    length = queries.shape[0]
    block_rows = min(512, length)
    starts = jnp.arange(0, length, block_rows).astype(jnp.int32)
    blocks = queries.reshape(length // block_rows, block_rows, KV, H // KV, HD)
    key_place = jnp.arange(length).astype(jnp.int32)
    highest = lax.Precision.HIGHEST

    def one_block(inputs):
        first_row, query_block = inputs
        raw_scores = jnp.einsum('qkgd,nkd->kgqn', query_block, keys_rot, precision=highest)
        scores = low_back(raw_scores) * HD ** (-0.5)
        query_place = first_row + jnp.arange(block_rows).astype(jnp.int32)
        causal_mask = key_place[None, :] <= query_place[:, None]
        scores = jnp.where(causal_mask, scores, -1e+30)
        weights = low(jax.nn.softmax(scores, axis=-1))
        return jnp.einsum('kgqn,nkd->qkgd', weights, values, precision=highest)
    attended = lax.map(jax.checkpoint(one_block), (starts, blocks))
    return attended.reshape(length, H * HD)

def layer(inputs, attn_gain, query_weight, key_weight, value_weight, query_gain, key_gain, out_weight, ffn_gain, gate_weight, up_weight, down_weight):
    length = inputs.shape[0]
    highest = lax.Precision.HIGHEST
    normed = low(rms_scale(inputs, attn_gain))
    queries = low_back(jnp.dot(normed, query_weight, precision=highest)).reshape(length, H, HD)
    key_proj = low_back(jnp.dot(normed, key_weight, precision=highest)).reshape(length, KV, HD)
    values = low(low_back(jnp.dot(normed, value_weight, precision=highest))).reshape(length, KV, HD)
    cosine_table, sine_table = rope_tables(jnp.arange(length), HD)
    cosine_table = cosine_table[:, None, :]
    sine_table = sine_table[:, None, :]
    query_rot = low(rotate(rms_scale(queries, query_gain), cosine_table, sine_table))
    key_rot = low(rotate(rms_scale(key_proj, key_gain), cosine_table, sine_table))
    attended = attention(query_rot.reshape(length, KV, H // KV, HD), key_rot, values)
    attended = low_back(low(attended))
    hidden = inputs + low_back(jnp.dot(attended, out_weight, precision=highest))
    normed_ffn = low(rms_scale(hidden, ffn_gain))
    gate_proj = low_back(jnp.dot(normed_ffn, gate_weight, precision=highest))
    up_proj = low_back(jnp.dot(normed_ffn, up_weight, precision=highest))
    activated = low(jax.nn.silu(gate_proj) * up_proj)
    return hidden + jnp.dot(activated, down_weight, precision=highest)

def reference(layer_input, cotangent, attn_gain, query_weight, key_weight, value_weight, query_gain, key_gain, out_weight, ffn_gain, gate_weight, up_weight, down_weight):
    params = (attn_gain.astype(jnp.float32), query_weight.astype(jnp.float32), key_weight.astype(jnp.float32), value_weight.astype(jnp.float32), query_gain.astype(jnp.float32), key_gain.astype(jnp.float32), out_weight.astype(jnp.float32), ffn_gain.astype(jnp.float32), gate_weight.astype(jnp.float32), up_weight.astype(jnp.float32), down_weight.astype(jnp.float32))

    def one_sequence(running, seq_pair):
        sequence, seq_cot = seq_pair
        output, backward = jax.vjp(layer, sequence.astype(jnp.float32), *params)
        gradients = backward(seq_cot.astype(jnp.float32))
        running = tuple((earlier + later for earlier, later in zip(running, gradients[1:])))
        return (running, (output.astype(jnp.bfloat16), gradients[0]))
    zeros_init = tuple((jnp.zeros_like(weight_item) for weight_item in params))
    totals, (outputs, input_grads) = lax.scan(one_sequence, zeros_init, (layer_input, cotangent))
    return (outputs, input_grads, totals[0], totals[1], totals[2], totals[3], totals[4], totals[5], totals[6], totals[7], totals[8], totals[9], totals[10])
```

```python
import functools
import math

import jax
import jax.numpy as jnp
from jax import lax
from jax.experimental import pallas as pl
from jax.experimental.pallas import tpu as pltpu
from jax.sharding import PartitionSpec as P

HD = 64
LANES = 128
EPS = 1e-05
ROPE_BASE = 1000000.0
BF = jnp.bfloat16
F32 = jnp.float32
NT = (((1,), (1,)), ((), ()))
TN = (((0,), (0,)), ((), ()))
NN = (((1,), (0,)), ((), ()))
SCALE = HD ** (-0.5)
SCORE_SCALE = SCALE * math.log2(math.e)
VMEM_LIMIT = 56 * 1024 * 1024


def mm(a, b, dims=NN):
    return lax.dot_general(a, b, dims, preferred_element_type=F32)


def low_half(shape):
    return lax.broadcasted_iota(jnp.int32, shape, 1) % HD < HD // 2


def left_head(shape):
    return lax.broadcasted_iota(jnp.int32, shape, 1) < HD


def partner(x):
    return jnp.where(low_half(x.shape), pltpu.roll(x, LANES - HD // 2, 1), pltpu.roll(x, HD // 2, 1))


def head_mean(x):
    rows = lax.broadcasted_iota(jnp.int32, (LANES, LANES), 0) // HD
    cols = lax.broadcasted_iota(jnp.int32, (LANES, LANES), 1) // HD
    ones = jnp.where(rows == cols, 1.0 / HD, 0.0).astype(BF)
    high = x.astype(BF)
    rest = (x - high.astype(F32)).astype(BF)
    return mm(high, ones) + mm(rest, ones)


def project_kernel(x_ref, gain_ref, w_ref, cos_ref, sin_ref, qg_ref, kg_ref,
                   normed_ref, z_ref, q_ref, k_ref, v_ref):
    x = x_ref[...].astype(F32)
    scale = lax.rsqrt(jnp.mean(x * x, axis=-1, keepdims=True) + EPS)
    normed = (x * scale * gain_ref[...]).astype(BF)
    normed_ref[...] = normed
    out = mm(normed, w_ref[...])
    n_q = q_ref.shape[1] // LANES
    n_k = k_ref.shape[1] // (2 * LANES)
    cos, sin = cos_ref[...], sin_ref[...]
    for block in range(n_q + n_k):
        z = out[:, block * LANES:(block + 1) * LANES]
        z_ref[:, block * LANES:(block + 1) * LANES] = z
        gain = qg_ref[...] if block < n_q else kg_ref[...]
        n = z * lax.rsqrt(head_mean(z * z) + EPS) * gain
        turned = n * cos + partner(n) * sin
        if block < n_q:
            q_ref[:, block * LANES:(block + 1) * LANES] = turned.astype(BF)
        else:
            both(turned, k_ref, block - n_q)
    for block in range(n_k):
        at = (n_q + n_k + block) * LANES
        both(out[:, at:at + LANES], v_ref, block)


def both(pair, ref, block):
    swapped = pltpu.roll(pair, HD, 1)
    left = left_head(pair.shape)
    at = 2 * block * LANES
    ref[:, at:at + LANES] = jnp.where(left, pair, swapped).astype(BF)
    ref[:, at + LANES:at + 2 * LANES] = jnp.where(left, swapped, pair).astype(BF)


def project(xs, gain, w_all, cos, sin, qgain, kgain, n_qcols, n_kcols, tb):
    tokens, width = xs.shape
    cols = w_all.shape[1]
    row = lambda b: (b, 0)
    fixed = lambda b: (0, 0)
    return pl.pallas_call(
        project_kernel,
        grid=(tokens // tb,),
        in_specs=[
            pl.BlockSpec((tb, width), row),
            pl.BlockSpec((1, width), fixed),
            pl.BlockSpec((width, cols), fixed),
            pl.BlockSpec((tb, LANES), row),
            pl.BlockSpec((tb, LANES), row),
            pl.BlockSpec((1, LANES), fixed),
            pl.BlockSpec((1, LANES), fixed),
        ],
        out_specs=[
            pl.BlockSpec((tb, width), row),
            pl.BlockSpec((tb, n_qcols + n_kcols), row),
            pl.BlockSpec((tb, n_qcols), row),
            pl.BlockSpec((tb, 2 * n_kcols), row),
            pl.BlockSpec((tb, 2 * n_kcols), row),
        ],
        out_shape=[
            jax.ShapeDtypeStruct((tokens, width), BF),
            jax.ShapeDtypeStruct((tokens, n_qcols + n_kcols), F32),
            jax.ShapeDtypeStruct((tokens, n_qcols), BF),
            jax.ShapeDtypeStruct((tokens, 2 * n_kcols), BF),
            jax.ShapeDtypeStruct((tokens, 2 * n_kcols), BF),
        ],
        cost_estimate=pl.CostEstimate(flops=2 * tokens * width * cols, bytes_accessed=tokens * 14000, transcendentals=0),
        compiler_params=pltpu.CompilerParams(vmem_limit_bytes=VMEM_LIMIT),
        name="project",
    )(xs, gain, w_all, cos, sin, qgain, kgain)


def attend_kernel(ids, q_ref, k_ref, v_ref, o_ref, lse_ref, acc_a, acc_b):
    chunk = q_ref.shape[0]
    own = ids[pl.program_id(1)]
    left = left_head(q_ref.shape)
    q = q_ref[...]
    zero = jnp.zeros_like(q)
    q_a, q_b = jnp.where(left, q, zero), jnp.where(left, zero, q)
    acc_a[...] = jnp.zeros_like(acc_a)
    acc_b[...] = jnp.zeros_like(acc_b)

    def block(at, masked):
        rows = pl.ds(pl.multiple_of(at * chunk, chunk), chunk)
        k, v = k_ref[rows, :], v_ref[rows, :]
        one = jnp.ones_like(v)
        for q_one, v_one, acc in ((q_a, jnp.where(left, v, one), acc_a), (q_b, jnp.where(left, one, v), acc_b)):
            p = jnp.exp2(mm(q_one, k, NT) * SCORE_SCALE)
            if masked:
                allowed = lax.broadcasted_iota(jnp.int32, p.shape, 1) <= lax.broadcasted_iota(jnp.int32, p.shape, 0)
                p = jnp.where(allowed, p, 0.0)
            acc[...] += mm(p.astype(BF), v_one)

    @pl.loop(0, own)
    def _(at):
        block(at, False)

    block(own, True)
    a, b = acc_a[...], acc_b[...]
    total = pltpu.roll(jnp.where(left, b, a), HD, 1)
    o_ref[...] = (jnp.where(left, a, b) / total).astype(BF)
    rows = jnp.transpose(jnp.log2(total))
    lse_ref[0:1, :] = rows[0:1, :]
    lse_ref[1:2, :] = rows[HD:HD + 1, :]


def attend(ids, q, k, v, chunk):
    tokens, cols = q.shape
    pairs = cols // LANES
    return pl.pallas_call(
        attend_kernel,
        grid_spec=pltpu.PrefetchScalarGridSpec(
            num_scalar_prefetch=1,
            grid=(pairs, 2),
            in_specs=[
                pl.BlockSpec((chunk, LANES), lambda j, c, ids: (ids[c], j)),
                pl.BlockSpec((tokens, LANES), lambda j, c, ids: (0, j)),
                pl.BlockSpec((tokens, LANES), lambda j, c, ids: (0, j)),
            ],
            out_specs=[
                pl.BlockSpec((chunk, LANES), lambda j, c, ids: (c, j)),
                pl.BlockSpec((8, chunk), lambda j, c, ids: (j, c)),
            ],
            scratch_shapes=[pltpu.VMEM((chunk, LANES), F32)] * 2,
        ),
        out_shape=[
            jax.ShapeDtypeStruct((2 * chunk, cols), BF),
            jax.ShapeDtypeStruct((8 * pairs, 2 * chunk), F32),
        ],
        cost_estimate=pl.CostEstimate(
            flops=pairs * 2 * 4 * LANES * chunk * (tokens + chunk), bytes_accessed=6 * tokens * cols,
            transcendentals=pairs * 2 * chunk * (tokens + chunk)),
        compiler_params=pltpu.CompilerParams(vmem_limit_bytes=VMEM_LIMIT),
        name="attend",
    )(ids, q, k, v)


def attend_back_kernel(ids, q_ref, k_ref, v_ref, o_ref, do_ref, lse_ref, dq_ref, dk_ref, dv_ref):
    chunk = q_ref.shape[0]
    own = ids[pl.program_id(1)]
    left = left_head(q_ref.shape)
    q, do = q_ref[...], do_ref[...]
    zero = jnp.zeros_like(q)
    q_a, q_b = jnp.where(left, q, zero), jnp.where(left, zero, q)
    do_a, do_b = jnp.where(left, do, zero), jnp.where(left, zero, do)
    prod = jnp.transpose(do.astype(F32) * o_ref[...].astype(F32))
    delta_a = jnp.sum(prod[:HD], axis=0, keepdims=True)
    delta_b = jnp.sum(prod[HD:], axis=0, keepdims=True)
    lse_a, lse_b = lse_ref[0:1, :], lse_ref[1:2, :]
    dq_ref[...] = jnp.zeros_like(dq_ref)

    @pl.when(pl.program_id(1) == 0)
    def _():
        dk_ref[...] = jnp.zeros_like(dk_ref)
        dv_ref[...] = jnp.zeros_like(dv_ref)

    def block(at, masked):
        rows = pl.ds(pl.multiple_of(at * chunk, chunk), chunk)
        k, v = k_ref[rows, :], v_ref[rows, :]
        k_a, k_b = jnp.where(left, k, zero), jnp.where(left, zero, k)
        for q_one, do_one, k_one, lse, delta in ((q_a, do_a, k_a, lse_a, delta_a), (q_b, do_b, k_b, lse_b, delta_b)):
            p = jnp.exp2(mm(k, q_one, NT) * SCORE_SCALE - lse)
            if masked:
                allowed = lax.broadcasted_iota(jnp.int32, p.shape, 0) <= lax.broadcasted_iota(jnp.int32, p.shape, 1)
                p = jnp.where(allowed, p, 0.0)
            ds = (p * (mm(v, do_one, NT) - delta)).astype(BF)
            dv_ref[rows, :] += mm(p.astype(BF), do_one)
            dk_ref[rows, :] += mm(ds, q_one)
            dq_ref[...] += mm(ds, k_one, TN)

    @pl.loop(0, own)
    def _(at):
        block(at, False)

    block(own, True)


def attend_back(ids, q, k, v, o, do, lse, chunk):
    tokens, cols = q.shape
    pairs = cols // LANES
    whole = pl.BlockSpec((tokens, LANES), lambda j, c, ids: (0, j))
    mine = pl.BlockSpec((chunk, LANES), lambda j, c, ids: (c, j))
    natural = pl.BlockSpec((chunk, LANES), lambda j, c, ids: (ids[c], j))
    return pl.pallas_call(
        attend_back_kernel,
        grid_spec=pltpu.PrefetchScalarGridSpec(
            num_scalar_prefetch=1,
            grid=(pairs, 2),
            in_specs=[natural, whole, whole, mine, mine, pl.BlockSpec((8, chunk), lambda j, c, ids: (j, c))],
            out_specs=[natural, whole, whole],
        ),
        out_shape=[jax.ShapeDtypeStruct((tokens, cols), F32)] * 3,
        cost_estimate=pl.CostEstimate(
            flops=pairs * 2 * 10 * LANES * chunk * (tokens + chunk), bytes_accessed=18 * tokens * cols,
            transcendentals=pairs * 2 * chunk * (tokens + chunk)),
        compiler_params=pltpu.CompilerParams(vmem_limit_bytes=VMEM_LIMIT),
        name="attend_back",
    )(ids, q, k, v, o, do, lse)


def turn_back_kernel(ids, z_ref, dq_ref, dk_ref, dv_ref, cos_ref, sin_ref, qg_ref, kg_ref, out_ref, gain_ref, *, per_chunk):
    step = pl.program_id(0)
    n_q = dq_ref.shape[1] // LANES
    n_k = dk_ref.shape[1] // (2 * LANES)
    cos, sin = cos_ref[...], sin_ref[...]

    @pl.when(step == 0)
    def _():
        gain_ref[...] = jnp.zeros_like(gain_ref)

    def back(block, d, gain, row):
        z = z_ref[:, block * LANES:(block + 1) * LANES]
        scale = lax.rsqrt(head_mean(z * z) + EPS)
        d = d * SCALE
        dn = d * cos - partner(d) * sin
        zr = z * scale
        gain_ref[row:row + 1, :] += jnp.sum(dn * zr, axis=0, keepdims=True)
        gdn = gain * dn
        out_ref[:, block * LANES:(block + 1) * LANES] = (scale * (gdn - zr * head_mean(zr * gdn))).astype(BF)

    own = jnp.logical_or(step // per_chunk == ids[0], step // per_chunk == ids[1])

    @pl.when(own)
    def _():
        for block in range(n_q):
            back(block, dq_ref[:, block * LANES:(block + 1) * LANES], qg_ref[...], 0)

    @pl.when(jnp.logical_not(own))
    def _():
        out_ref[:, :n_q * LANES] = jnp.zeros((out_ref.shape[0], n_q * LANES), BF)

    def folded(ref, block):
        at = 2 * block * LANES
        one, two = ref[:, at:at + LANES], ref[:, at + LANES:at + 2 * LANES]
        one, two = one + pltpu.roll(one, HD, 1), two + pltpu.roll(two, HD, 1)
        return jnp.where(left_head(one.shape), one, two)

    for block in range(n_k):
        back(n_q + block, folded(dk_ref, block), kg_ref[...], 1)
        at = (n_q + n_k + block) * LANES
        out_ref[:, at:at + LANES] = folded(dv_ref, block).astype(BF)


def turn_back(ids, z, dq, dk, dv, cos, sin, qgain, kgain, tb, chunk):
    tokens = z.shape[0]
    n_q, n_k = dq.shape[1], dk.shape[1] // 2
    row = lambda b, ids: (b, 0)
    fixed = lambda b, ids: (0, 0)
    return pl.pallas_call(
        functools.partial(turn_back_kernel, per_chunk=chunk // tb),
        grid_spec=pltpu.PrefetchScalarGridSpec(
            num_scalar_prefetch=1,
            grid=(tokens // tb,),
            in_specs=[
                pl.BlockSpec((tb, n_q + n_k), row),
                pl.BlockSpec((tb, n_q), row),
                pl.BlockSpec((tb, 2 * n_k), row),
                pl.BlockSpec((tb, 2 * n_k), row),
                pl.BlockSpec((tb, LANES), row),
                pl.BlockSpec((tb, LANES), row),
                pl.BlockSpec((1, LANES), fixed),
                pl.BlockSpec((1, LANES), fixed),
            ],
            out_specs=[pl.BlockSpec((tb, n_q + 2 * n_k), row), pl.BlockSpec((8, LANES), fixed)],
        ),
        out_shape=[
            jax.ShapeDtypeStruct((tokens, n_q + 2 * n_k), BF),
            jax.ShapeDtypeStruct((8, LANES), F32),
        ],
        cost_estimate=pl.CostEstimate(flops=tokens * 200000, bytes_accessed=tokens * 12000, transcendentals=0),
        compiler_params=pltpu.CompilerParams(vmem_limit_bytes=VMEM_LIMIT),
        name="turn_back",
    )(ids, z, dq, dk, dv, cos, sin, qgain, kgain)


def feed_kernel(hn_ref, dy_ref, wg_ref, wu_ref, wd_ref, act_ref, dg_ref, du_ref, out_ref, dhn_ref):
    hn, dy = hn_ref[...], dy_ref[...]
    parts, _, part = wd_ref.shape
    gate = mm(hn, wg_ref[...])
    up = mm(hn, wu_ref[...])
    dact = mm(dy[:, :part], wd_ref[0], NT)
    for i in range(1, parts):
        dact += mm(dy[:, i * part:(i + 1) * part], wd_ref[i], NT)
    sig = 1.0 / (1.0 + jnp.exp(-gate))
    silu = gate * sig
    act = (silu * up).astype(BF)
    dg = (dact * up * (sig + silu * (1.0 - sig))).astype(BF)
    du = (dact * silu).astype(BF)
    act_ref[...] = act
    dg_ref[...] = dg
    du_ref[...] = du
    dhn_ref[...] = (mm(dg, wg_ref[...], NT) + mm(du, wu_ref[...], NT)).astype(BF)
    for i in range(parts):
        out_ref[:, i * part:(i + 1) * part] = mm(act, wd_ref[i]).astype(BF)


def feed(hn, dy, wg, wu, wd, tb):
    tokens, width = hn.shape
    units = wg.shape[1]
    row = lambda b: (b, 0)
    fixed = lambda b: (0, 0)
    once = pl.Buffered(1)
    return pl.pallas_call(
        feed_kernel,
        grid=(tokens // tb,),
        in_specs=[
            pl.BlockSpec((tb, width), row),
            pl.BlockSpec((tb, width), row),
            pl.BlockSpec((width, units), fixed, pipeline_mode=once),
            pl.BlockSpec((width, units), fixed, pipeline_mode=once),
            pl.BlockSpec(wd.shape, lambda b: (0, 0, 0), pipeline_mode=once),
        ],
        out_specs=[pl.BlockSpec((tb, units), row)] * 3 + [pl.BlockSpec((tb, width), row)] * 2,
        out_shape=[jax.ShapeDtypeStruct((tokens, units), BF)] * 3 + [jax.ShapeDtypeStruct((tokens, width), BF)] * 2,
        cost_estimate=pl.CostEstimate(flops=12 * tokens * width * units, bytes_accessed=6 * width * units + tokens * 15000,
                                      transcendentals=tokens * units),
        compiler_params=pltpu.CompilerParams(vmem_limit_bytes=VMEM_LIMIT),
        name="feed",
    )(hn, dy, wg, wu, wd)


def rope_tables(length):
    positions = lax.optimization_barrier(jnp.arange(length, dtype=jnp.int32))
    frequency = ROPE_BASE ** (-jnp.arange(0, HD, 2).astype(F32) / HD)
    angles = positions.astype(F32)[:, None] * frequency[None, :]
    cos, sin = jnp.cos(angles), jnp.sin(angles)
    return jnp.concatenate([cos] * 4, axis=1), jnp.concatenate([-sin, sin] * 2, axis=1)


def rms(z):
    return lax.rsqrt(jnp.mean(z * z, axis=-1, keepdims=True) + EPS)


def norm_back(z, scale, gain, dn):
    zr = z * scale
    gdn = gain * dn
    dz = scale * (gdn - zr * jnp.mean(zr * gdn, axis=-1, keepdims=True))
    return dz, jnp.sum(dn * zr, axis=0)


def on_device(layer_input, cotangent, attn_gain, query_weight, key_weight, value_weight, query_gain, key_gain,
              out_weight, ffn_gain, gate_weight, up_weight, down_weight):
    n_dp, n_ctx, n_tensor = (lax.axis_size(a) for a in ("dp", "ctx", "tensor"))
    seqs, local_len, width = layer_input.shape
    assert seqs == 2 and n_tensor == 4
    chunk = local_len // 2
    length = local_len * n_ctx
    t = lax.axis_index("tensor")
    seq, core = t // 2, t % 2
    ctx = lax.axis_index("ctx")

    def own_chunk(place, which):
        return jnp.where(place % 2 == which, place, 2 * n_ctx - 1 - place)

    id_here, id_there = own_chunk(ctx, core), own_chunk(ctx, 1 - core)
    ids = jnp.stack([id_here, id_there]).astype(jnp.int32)

    def swap_core(x):
        return lax.ppermute(x, "tensor", [(i, i ^ 1) for i in range(n_tensor)])

    def swap_seq(x):
        return lax.ppermute(x, "tensor", [(i, i ^ 2) for i in range(n_tensor)])

    def swap_ctx(x):
        return lax.ppermute(x, "ctx", [(0, 1), (1, 0)])

    homes = []
    for place in range(n_ctx):
        for i in range(n_tensor):
            which = place if place % 2 == i % 2 else 2 * n_ctx - 1 - place
            homes.append((place * n_tensor + i, (which // 2) * n_tensor + i))

    def send_home(x):
        return lax.ppermute(x, ("ctx", "tensor"), homes)

    def fetch_from_home(x):
        return lax.ppermute(x, ("ctx", "tensor"), [(b, a) for a, b in homes])

    def ctx_pair(x, axis):
        if n_ctx != 2:
            return lax.all_gather(x, "ctx", axis=axis, tiled=False)
        other = swap_ctx(x)
        return jnp.where(ctx == 0, jnp.stack([x, other], axis), jnp.stack([other, x], axis))

    x_here = lax.dynamic_index_in_dim(layer_input, seq, 0, keepdims=False)
    if n_ctx == 2:
        half = lax.dynamic_slice_in_dim(x_here, core * chunk, chunk, 0)
        first = swap_ctx(half)
        second = swap_core(first)
        xs = jnp.zeros((length, width), BF)
        xs = lax.dynamic_update_slice(xs, x_here, (ctx * local_len, 0))
        xs = lax.dynamic_update_slice(xs, first, ((1 - ctx) * local_len + core * chunk, 0))
        xs = lax.dynamic_update_slice(xs, second, ((1 - ctx) * local_len + (1 - core) * chunk, 0))
    else:
        xs = lax.all_gather(x_here, "ctx", axis=0, tiled=True)

    gains = lax.all_gather(jnp.concatenate([attn_gain, ffn_gain, query_gain, key_gain]), "dp", axis=0, tiled=False)
    d_part, h_part = attn_gain.shape[0], query_gain.shape[0]
    gain_a = gains[:, :d_part].reshape(1, width).astype(F32)
    gain_f = gains[:, d_part:2 * d_part].reshape(1, width).astype(F32)
    gain_q = jnp.tile(gains[:, 2 * d_part:2 * d_part + h_part].reshape(1, HD).astype(F32), (1, 2))
    gain_k = jnp.tile(gains[:, 2 * d_part + h_part:].reshape(1, HD).astype(F32), (1, 2))

    nq, nk = query_weight.shape[1], key_weight.shape[1]
    qkv_mine = lax.all_gather(jnp.concatenate([query_weight, key_weight, value_weight], axis=1), "dp", axis=0, tiled=True)
    qkv_theirs = swap_seq(qkv_mine)

    def interleave(a, b):
        pieces = []
        for lo, hi in ((0, nq), (nq, nq + nk), (nq + nk, nq + 2 * nk)):
            pieces += [a[:, lo:hi], b[:, lo:hi]]
        return jnp.concatenate(pieces, axis=1)

    w_all = interleave(qkv_mine, qkv_theirs)
    out_mine = lax.all_gather(out_weight, "dp", axis=0, tiled=False).transpose(1, 0, 2).reshape(out_weight.shape[0], width)
    w_out = jnp.concatenate([out_mine, swap_seq(out_mine)], axis=0)

    def gather_ffn(w):
        if n_ctx != 2:
            return lax.all_gather(w, "dp", axis=0, tiled=False)
        rows = w.shape[0] // 2
        mine = lax.dynamic_slice_in_dim(w, ctx * rows, rows, 0)
        got = lax.all_gather(mine, "dp", axis=0, tiled=False)
        return ctx_pair(got, 1).reshape(n_dp, w.shape[0], w.shape[1])

    w_gate = gather_ffn(gate_weight).reshape(width, -1)
    w_up = gather_ffn(up_weight).reshape(width, -1)
    w_down = gather_ffn(down_weight)

    cot_home = lax.dynamic_slice(cotangent, (seq, core * chunk, 0), (1, chunk, width))[0]
    dy_0 = fetch_from_home(cot_home)
    dy_2 = swap_seq(dy_0)
    dy_02 = jnp.stack([dy_0, dy_2])
    dy_13 = swap_core(dy_02)
    dy_own = jnp.concatenate([dy_0, dy_13[0]], axis=0)
    dy_other = jnp.concatenate([dy_2, dy_13[1]], axis=0)

    tb = min(256, chunk)
    cos, sin = rope_tables(length)
    normed, z, q, k, v = project(xs, gain_a, w_all, cos, sin, gain_q, gain_k, 2 * nq, 2 * nk, tb)
    o, lse = attend(ids, q, k, v, chunk)
    attn = mm(o, w_out)
    got = swap_core(attn[chunk:].astype(BF))
    x_0 = lax.dynamic_slice_in_dim(xs, id_here * chunk, chunk, 0).astype(F32)
    hidden = x_0 + (attn[:chunk] + got.astype(F32))
    h_scale = rms(hidden)
    hn_0 = (hidden * h_scale * gain_f).astype(BF)
    hn_1 = swap_core(hn_0)
    hn_2 = swap_seq(hn_0)
    hn_3 = swap_core(hn_2)
    hn_own = jnp.concatenate([hn_0, hn_1], axis=0)
    hn_other = jnp.concatenate([hn_2, hn_3], axis=0)

    act_o, dg_o, du_o, y_o, dhn_o = feed(hn_own, dy_own, w_gate, w_up, w_down, tb)
    act_t, dg_t, du_t, y_t, dhn_t = feed(hn_other, dy_other, w_gate, w_up, w_down, tb)

    def sum_tensor(mine, theirs):
        for_seq = theirs[:chunk].astype(F32) + swap_core(theirs[chunk:]).astype(F32)
        here = mine[:chunk].astype(F32) + swap_core(mine[chunk:]).astype(F32)
        return here + swap_seq(for_seq.astype(BF)).astype(F32)

    dhn = sum_tensor(dhn_o, dhn_t)
    d_norm, ffn_gain_part = norm_back(hidden, h_scale, gain_f, dhn)
    dhidden = dy_0.astype(F32) + d_norm
    dhr_0 = dhidden.astype(BF)
    dhr = jnp.concatenate([dhr_0, swap_core(dhr_0)], axis=0)

    def join(piece, kind):
        p_core = swap_core(piece)
        p_seq = swap_seq(piece)
        p_both = swap_core(p_seq)
        out = jnp.zeros((2, 2, chunk, width), kind)
        for value, s, c in ((piece, seq, core), (p_core, seq, 1 - core), (p_seq, 1 - seq, core), (p_both, 1 - seq, 1 - core)):
            out = lax.dynamic_update_slice(out, value.astype(kind)[None, None], (s, c, 0, 0))
        return out.reshape(2, local_len, width)

    total = (hidden + sum_tensor(y_o, y_t)).astype(BF)
    layer_output = join(send_home(total), BF)

    def weight_sum(a_own, b_own, a_other, b_other):
        return (mm(a_own, b_own, TN) + mm(a_other, b_other, TN)).astype(BF)

    def scatter(g):
        mine = lax.psum_scatter(g, ("dp", "ctx"), scatter_dimension=0, tiled=True)
        return ctx_pair(mine, 0).reshape(g.shape[0] // n_dp, g.shape[1])

    gate_grad = scatter(weight_sum(hn_own, dg_o, hn_other, dg_t)).astype(F32)
    up_grad = scatter(weight_sum(hn_own, du_o, hn_other, du_t)).astype(F32)
    down_grad = scatter(weight_sum(dy_own, act_o, dy_other, act_t)).T.astype(F32)

    do = mm(dhr, w_out, NT).astype(BF)
    dq, dk, dv = attend_back(ids, q, k, v, o, do, lse, chunk)
    dqkv, gain_parts = turn_back(ids, z, dq, dk, dv, cos, sin, gain_q, gain_k, tb, chunk)
    dn = mm(dqkv, w_all, NT).astype(BF).reshape(n_ctx, 2, chunk, width)
    keep = lax.dynamic_index_in_dim(dn, core, 1, keepdims=False)
    give = lax.dynamic_index_in_dim(dn, 1 - core, 1, keepdims=False)
    dn = keep.astype(F32) + swap_core(give).astype(F32)
    x_kept = lax.dynamic_index_in_dim(xs.reshape(n_ctx, 2, chunk, width), core, 1, keepdims=False).astype(F32)
    dz, attn_gain_part = norm_back(x_kept, rms(x_kept), gain_a, dn.reshape(n_ctx, chunk, width))
    attn_gain_part = jnp.sum(attn_gain_part, axis=0)
    at_home = lax.dynamic_index_in_dim(dz, id_here // 2, 0, keepdims=True) + dhidden[None]
    dz = lax.dynamic_update_slice(dz, at_home, (id_here // 2, 0, 0)).astype(BF)
    if n_ctx == 2:
        mine = lax.dynamic_index_in_dim(dz, ctx, 0, keepdims=False)
        got = swap_ctx(lax.dynamic_index_in_dim(dz, 1 - ctx, 0, keepdims=False))
        dx = (mine.astype(F32) + got.astype(F32)).astype(BF)
    else:
        dx = lax.psum_scatter(dz, "ctx", scatter_dimension=0, tiled=False)
    input_grad = join(dx, F32)

    g_all = mm(normed, dqkv, TN).astype(BF)
    g_out = mm(dhr, o, TN).astype(BF)
    c1, c2 = 2 * nq, 2 * nq + 2 * nk
    h_out = out_weight.shape[0]
    g_mine = jnp.concatenate([g_all[:, :nq], g_all[:, c1:c1 + nk], g_all[:, c2:c2 + nk], g_out[:, :h_out]], axis=1)
    g_theirs = jnp.concatenate([g_all[:, nq:c1], g_all[:, c1 + nk:c2], g_all[:, c2 + nk:], g_out[:, h_out:]], axis=1)
    g = scatter((g_mine.astype(F32) + swap_seq(g_theirs).astype(F32)).astype(BF)).astype(F32)
    query_grad, key_grad, value_grad = g[:, :nq], g[:, nq:nq + nk], g[:, nq + nk:nq + 2 * nk]
    out_grad = g[:, nq + 2 * nk:].T

    fold = gain_parts[:2, :HD] + gain_parts[:2, HD:]
    small = lax.psum(jnp.concatenate([attn_gain_part, ffn_gain_part, fold.reshape(-1)]), ("dp", "ctx", "tensor"))
    dp = lax.axis_index("dp")
    attn_gain_grad = lax.dynamic_slice_in_dim(small, dp * d_part, d_part)
    ffn_gain_grad = lax.dynamic_slice_in_dim(small, width + dp * d_part, d_part)
    qgain_grad = lax.dynamic_slice_in_dim(small, 2 * width + dp * h_part, h_part)
    kgain_grad = lax.dynamic_slice_in_dim(small, 2 * width + HD + dp * h_part, h_part)

    return (layer_output, input_grad, attn_gain_grad, query_grad, key_grad, value_grad, qgain_grad, kgain_grad,
            out_grad, ffn_gain_grad, gate_grad, up_grad, down_grad)


def solution(mesh):
    token = P("dp", "ctx", None)
    into, out_of, vector = P("dp", "tensor"), P("tensor", "dp"), P("dp")
    return jax.shard_map(
        on_device,
        mesh=mesh,
        in_specs=(token, token, vector, into, into, into, vector, vector, out_of, vector, into, into, out_of),
        out_specs=(token, token, vector, into, into, into, vector, vector, out_of, vector, into, into, out_of),
        check_vma=False,
    )
```

```python
import functools
import math

import jax
import jax.numpy as jnp
from jax import lax
from jax.experimental import pallas as pl
from jax.experimental.pallas import tpu as pltpu
from jax.sharding import PartitionSpec as P

HD = 64
LANES = 128
EPS = 1e-05
ROPE_BASE = 1000000.0
BF = jnp.bfloat16
F32 = jnp.float32
NT = (((1,), (1,)), ((), ()))
TN = (((0,), (0,)), ((), ()))
NN = (((1,), (0,)), ((), ()))
SCALE = HD ** (-0.5)
SCORE_SCALE = SCALE * math.log2(math.e)
VMEM_LIMIT = 56 * 1024 * 1024
COST_PART = 1000


def cost(flops, bytes_accessed, transcendentals):
    return pl.CostEstimate(flops=flops // COST_PART, bytes_accessed=bytes_accessed // COST_PART,
                           transcendentals=transcendentals // COST_PART)


def mm(a, b, dims=NN):
    return lax.dot_general(a, b, dims, preferred_element_type=F32)


def low_half(shape):
    return lax.broadcasted_iota(jnp.int32, shape, 1) % HD < HD // 2


def left_head(shape):
    return lax.broadcasted_iota(jnp.int32, shape, 1) < HD


def partner(x):
    return jnp.where(low_half(x.shape), pltpu.roll(x, LANES - HD // 2, 1), pltpu.roll(x, HD // 2, 1))


def head_mean(x):
    rows = lax.broadcasted_iota(jnp.int32, (LANES, LANES), 0) // HD
    cols = lax.broadcasted_iota(jnp.int32, (LANES, LANES), 1) // HD
    ones = jnp.where(rows == cols, 1.0 / HD, 0.0).astype(BF)
    high = x.astype(BF)
    rest = (x - high.astype(F32)).astype(BF)
    return mm(high, ones) + mm(rest, ones)


def project_kernel(x_ref, gain_ref, w_ref, cos_ref, sin_ref, qg_ref, kg_ref,
                   normed_ref, z_ref, q_ref, k_ref, v_ref):
    x = x_ref[...].astype(F32)
    scale = lax.rsqrt(jnp.mean(x * x, axis=-1, keepdims=True) + EPS)
    normed = (x * scale * gain_ref[...]).astype(BF)
    normed_ref[...] = normed
    out = mm(normed, w_ref[...])
    cos, sin = cos_ref[...], sin_ref[...]
    for kind, block, at in column_blocks(q_ref.shape[1], k_ref.shape[1]):
        z = out[:, at * LANES:(at + 1) * LANES]
        if kind == "v":
            both(z, v_ref, block)
            continue
        z_ref[:, at * LANES:(at + 1) * LANES] = z
        gain = qg_ref[...] if kind == "q" else kg_ref[...]
        n = z * lax.rsqrt(head_mean(z * z) + EPS) * gain
        turned = n * cos + partner(n) * sin
        if kind == "q":
            q_ref[:, block * LANES:(block + 1) * LANES] = turned.astype(BF)
        else:
            both(turned, k_ref, block)


def column_blocks(n_q, n_k_twice):
    n_q, n_k = n_q // (2 * LANES), n_k_twice // (4 * LANES)
    blocks, at = [], 0
    for shard in range(2):
        for kind, count in (("q", n_q), ("k", n_k), ("v", n_k)):
            for i in range(count):
                blocks.append((kind, shard * count + i, at))
                at += 1
    return blocks


def both(pair, ref, block):
    swapped = pltpu.roll(pair, HD, 1)
    left = left_head(pair.shape)
    at = 2 * block * LANES
    ref[:, at:at + LANES] = jnp.where(left, pair, swapped).astype(BF)
    ref[:, at + LANES:at + 2 * LANES] = jnp.where(left, swapped, pair).astype(BF)


def project(xs, gain, w_all, cos, sin, qgain, kgain, n_qcols, n_kcols, tb):
    tokens, width = xs.shape
    cols = w_all.shape[1]
    row = lambda b: (b, 0)
    fixed = lambda b: (0, 0)
    return pl.pallas_call(
        project_kernel,
        grid=(tokens // tb,),
        in_specs=[
            pl.BlockSpec((tb, width), row),
            pl.BlockSpec((1, width), fixed),
            pl.BlockSpec((width, cols), fixed),
            pl.BlockSpec((tb, LANES), row),
            pl.BlockSpec((tb, LANES), row),
            pl.BlockSpec((1, LANES), fixed),
            pl.BlockSpec((1, LANES), fixed),
        ],
        out_specs=[
            pl.BlockSpec((tb, width), row),
            pl.BlockSpec((tb, cols), row),
            pl.BlockSpec((tb, n_qcols), row),
            pl.BlockSpec((tb, 2 * n_kcols), row),
            pl.BlockSpec((tb, 2 * n_kcols), row),
        ],
        out_shape=[
            jax.ShapeDtypeStruct((tokens, width), BF),
            jax.ShapeDtypeStruct((tokens, cols), F32),
            jax.ShapeDtypeStruct((tokens, n_qcols), BF),
            jax.ShapeDtypeStruct((tokens, 2 * n_kcols), BF),
            jax.ShapeDtypeStruct((tokens, 2 * n_kcols), BF),
        ],
        cost_estimate=cost(flops=2 * tokens * width * cols, bytes_accessed=tokens * 14000, transcendentals=0),
        compiler_params=pltpu.CompilerParams(vmem_limit_bytes=VMEM_LIMIT),
        name="project",
    )(xs, gain, w_all, cos, sin, qgain, kgain)


def attend_kernel(ids, q_ref, k_ref, v_ref, o_ref, lse_ref, acc_a, acc_b):
    chunk = q_ref.shape[0]
    own = ids[pl.program_id(1)]
    left = left_head(q_ref.shape)
    q = q_ref[...]
    zero = jnp.zeros_like(q)
    q_a, q_b = jnp.where(left, q, zero), jnp.where(left, zero, q)
    acc_a[...] = jnp.zeros_like(acc_a)
    acc_b[...] = jnp.zeros_like(acc_b)

    def block(at, masked):
        rows = pl.ds(pl.multiple_of(at * chunk, chunk), chunk)
        k, v = k_ref[rows, :], v_ref[rows, :]
        one = jnp.ones_like(v)
        for q_one, v_one, acc in ((q_a, jnp.where(left, v, one), acc_a), (q_b, jnp.where(left, one, v), acc_b)):
            p = jnp.exp2(mm(q_one, k, NT) * SCORE_SCALE)
            if masked:
                allowed = lax.broadcasted_iota(jnp.int32, p.shape, 1) <= lax.broadcasted_iota(jnp.int32, p.shape, 0)
                p = jnp.where(allowed, p, 0.0)
            acc[...] += mm(p.astype(BF), v_one)

    @pl.loop(0, own)
    def _(at):
        block(at, False)

    block(own, True)
    a, b = acc_a[...], acc_b[...]
    total = pltpu.roll(jnp.where(left, b, a), HD, 1)
    o_ref[...] = (jnp.where(left, a, b) / total).astype(BF)
    rows = jnp.transpose(jnp.log2(total))
    lse_ref[0:1, :] = rows[0:1, :]
    lse_ref[1:2, :] = rows[HD:HD + 1, :]


def attend(ids, q, k, v, chunk):
    tokens, cols = q.shape
    pairs = cols // LANES
    return pl.pallas_call(
        attend_kernel,
        grid_spec=pltpu.PrefetchScalarGridSpec(
            num_scalar_prefetch=1,
            grid=(pairs, 2),
            in_specs=[
                pl.BlockSpec((chunk, LANES), lambda j, c, ids: (ids[c], j)),
                pl.BlockSpec((tokens, LANES), lambda j, c, ids: (0, j)),
                pl.BlockSpec((tokens, LANES), lambda j, c, ids: (0, j)),
            ],
            out_specs=[
                pl.BlockSpec((chunk, LANES), lambda j, c, ids: (c, j)),
                pl.BlockSpec((8, chunk), lambda j, c, ids: (j, c)),
            ],
            scratch_shapes=[pltpu.VMEM((chunk, LANES), F32)] * 2,
        ),
        out_shape=[
            jax.ShapeDtypeStruct((2 * chunk, cols), BF),
            jax.ShapeDtypeStruct((8 * pairs, 2 * chunk), F32),
        ],
        cost_estimate=cost(
            flops=pairs * 2 * 4 * LANES * chunk * (tokens + chunk), bytes_accessed=6 * tokens * cols,
            transcendentals=pairs * 2 * chunk * (tokens + chunk)),
        compiler_params=pltpu.CompilerParams(vmem_limit_bytes=VMEM_LIMIT),
        name="attend",
    )(ids, q, k, v)


def attend_back_kernel(ids, q_ref, k_ref, v_ref, o_ref, do_ref, lse_ref, dq_ref, dk_ref, dv_ref):
    chunk = q_ref.shape[0]
    own = ids[pl.program_id(1)]
    left = left_head(q_ref.shape)
    q, do = q_ref[...], do_ref[...]
    zero = jnp.zeros_like(q)
    q_a, q_b = jnp.where(left, q, zero), jnp.where(left, zero, q)
    do_a, do_b = jnp.where(left, do, zero), jnp.where(left, zero, do)
    prod = jnp.transpose(do.astype(F32) * o_ref[...].astype(F32))
    delta_a = jnp.sum(prod[:HD], axis=0, keepdims=True)
    delta_b = jnp.sum(prod[HD:], axis=0, keepdims=True)
    lse_a, lse_b = lse_ref[0:1, :], lse_ref[1:2, :]
    dq_ref[...] = jnp.zeros_like(dq_ref)

    @pl.when(pl.program_id(1) == 0)
    def _():
        dk_ref[...] = jnp.zeros_like(dk_ref)
        dv_ref[...] = jnp.zeros_like(dv_ref)

    def block(at, masked):
        rows = pl.ds(pl.multiple_of(at * chunk, chunk), chunk)
        k, v = k_ref[rows, :], v_ref[rows, :]
        k_a, k_b = jnp.where(left, k, zero), jnp.where(left, zero, k)
        for q_one, do_one, k_one, lse, delta in ((q_a, do_a, k_a, lse_a, delta_a), (q_b, do_b, k_b, lse_b, delta_b)):
            p = jnp.exp2(mm(k, q_one, NT) * SCORE_SCALE - lse)
            if masked:
                allowed = lax.broadcasted_iota(jnp.int32, p.shape, 0) <= lax.broadcasted_iota(jnp.int32, p.shape, 1)
                p = jnp.where(allowed, p, 0.0)
            ds = (p * (mm(v, do_one, NT) - delta)).astype(BF)
            dv_ref[rows, :] += mm(p.astype(BF), do_one)
            dk_ref[rows, :] += mm(ds, q_one)
            dq_ref[...] += mm(ds, k_one, TN)

    @pl.loop(0, own)
    def _(at):
        block(at, False)

    block(own, True)


def attend_back(ids, q, k, v, o, do, lse, chunk, group):
    tokens, cols = q.shape
    pairs = cols // LANES // 2
    first = group * pairs
    whole = pl.BlockSpec((tokens, LANES), lambda j, c, ids: (0, first + j))
    mine = pl.BlockSpec((chunk, LANES), lambda j, c, ids: (c, first + j))
    natural = pl.BlockSpec((chunk, LANES), lambda j, c, ids: (ids[c], first + j))
    total = pl.BlockSpec((tokens, LANES), lambda j, c, ids: (0, j))
    return pl.pallas_call(
        attend_back_kernel,
        grid_spec=pltpu.PrefetchScalarGridSpec(
            num_scalar_prefetch=1,
            grid=(pairs, 2),
            in_specs=[natural, whole, whole, mine, mine, pl.BlockSpec((8, chunk), lambda j, c, ids: (first + j, c))],
            out_specs=[pl.BlockSpec((chunk, LANES), lambda j, c, ids: (ids[c], j)), total, total],
        ),
        out_shape=[jax.ShapeDtypeStruct((tokens, cols // 2), F32)] * 3,
        cost_estimate=cost(
            flops=pairs * 2 * 10 * LANES * chunk * (tokens + chunk), bytes_accessed=9 * tokens * cols,
            transcendentals=pairs * 2 * chunk * (tokens + chunk)),
        compiler_params=pltpu.CompilerParams(vmem_limit_bytes=VMEM_LIMIT),
        name="attend_back",
    )(ids, q, k, v, o, do, lse)


def turn_back_kernel(ids, z_ref, dq_ref, dk_ref, dv_ref, cos_ref, sin_ref, qg_ref, kg_ref, out_ref, gain_ref, *, per_chunk):
    step = pl.program_id(0)
    blocks = column_blocks(2 * dq_ref.shape[1], 2 * dk_ref.shape[1])
    blocks = blocks[:len(blocks) // 2]
    cos, sin = cos_ref[...], sin_ref[...]

    @pl.when(step == 0)
    def _():
        gain_ref[...] = jnp.zeros_like(gain_ref)

    def back(block, d, gain, row):
        z = z_ref[:, block * LANES:(block + 1) * LANES]
        scale = lax.rsqrt(head_mean(z * z) + EPS)
        d = d * SCALE
        dn = d * cos - partner(d) * sin
        zr = z * scale
        gain_ref[row:row + 1, :] += jnp.sum(dn * zr, axis=0, keepdims=True)
        gdn = gain * dn
        out_ref[:, block * LANES:(block + 1) * LANES] = (scale * (gdn - zr * head_mean(zr * gdn))).astype(BF)

    own = jnp.logical_or(step // per_chunk == ids[0], step // per_chunk == ids[1])

    @pl.when(own)
    def _():
        for kind, block, at in blocks:
            if kind == "q":
                back(at, dq_ref[:, block * LANES:(block + 1) * LANES], qg_ref[...], 0)

    @pl.when(jnp.logical_not(own))
    def _():
        for kind, _, at in blocks:
            if kind == "q":
                out_ref[:, at * LANES:(at + 1) * LANES] = jnp.zeros((out_ref.shape[0], LANES), BF)

    def folded(ref, block):
        at = 2 * block * LANES
        one, two = ref[:, at:at + LANES], ref[:, at + LANES:at + 2 * LANES]
        one, two = one + pltpu.roll(one, HD, 1), two + pltpu.roll(two, HD, 1)
        return jnp.where(left_head(one.shape), one, two)

    for kind, block, at in blocks:
        if kind == "k":
            back(at, folded(dk_ref, block), kg_ref[...], 1)
        if kind == "v":
            out_ref[:, at * LANES:(at + 1) * LANES] = folded(dv_ref, block).astype(BF)


def turn_back(ids, z, dq, dk, dv, cos, sin, qgain, kgain, tb, chunk, group):
    tokens = z.shape[0]
    n_q, n_k = dq.shape[1], dk.shape[1] // 2
    row = lambda b, ids: (b, 0)
    fixed = lambda b, ids: (0, 0)
    return pl.pallas_call(
        functools.partial(turn_back_kernel, per_chunk=chunk // tb),
        grid_spec=pltpu.PrefetchScalarGridSpec(
            num_scalar_prefetch=1,
            grid=(tokens // tb,),
            in_specs=[
                pl.BlockSpec((tb, n_q + 2 * n_k), lambda b, ids: (b, group)),
                pl.BlockSpec((tb, n_q), row),
                pl.BlockSpec((tb, 2 * n_k), row),
                pl.BlockSpec((tb, 2 * n_k), row),
                pl.BlockSpec((tb, LANES), row),
                pl.BlockSpec((tb, LANES), row),
                pl.BlockSpec((1, LANES), fixed),
                pl.BlockSpec((1, LANES), fixed),
            ],
            out_specs=[pl.BlockSpec((tb, n_q + 2 * n_k), row), pl.BlockSpec((8, LANES), fixed)],
        ),
        out_shape=[
            jax.ShapeDtypeStruct((tokens, n_q + 2 * n_k), BF),
            jax.ShapeDtypeStruct((8, LANES), F32),
        ],
        cost_estimate=cost(flops=tokens * 200000, bytes_accessed=tokens * 12000, transcendentals=0),
        compiler_params=pltpu.CompilerParams(vmem_limit_bytes=VMEM_LIMIT),
        name="turn_back",
    )(ids, z, dq, dk, dv, cos, sin, qgain, kgain)


def feed_kernel(place, *refs, n_pieces):
    hn_a, hn_b, dy_a, dy_b = refs[:4]
    pieces, rest = [], refs[4:]
    for count in n_pieces:
        pieces.append(rest[:count])
        rest = rest[count:]
    act_ref, dg_ref, du_ref, out_a, out_b, dhn_a, dhn_b, wg_ref, wu_ref, wd_ref, sems = rest
    step, steps = pl.program_id(0), pl.num_programs(0)
    early = step < steps // 2
    n_dp = wd_ref.shape[0]
    part = wd_ref.shape[2]

    def copies(weight):
        made = []
        for half, source in enumerate(pieces[weight]):
            rows = source.shape[1]
            offset = (place[0] if half == 0 else 1 - place[0]) * rows if n_pieces[weight] == 2 else 0
            for i in range(n_dp):
                if weight < 2:
                    target = (wg_ref, wu_ref)[weight]
                    window = target.at[pl.ds(pl.multiple_of(i * n_pieces[weight] * rows + offset, rows), rows), :]
                else:
                    window = wd_ref.at[i, pl.ds(pl.multiple_of(offset, rows), rows), :]
                made.append(pltpu.make_async_copy(source.at[i], window, sems.at[weight, half, i]))
        return made

    @pl.when(step == 0)
    def _():
        for weight in range(3):
            for copy in copies(weight):
                copy.start()
        for weight in range(3):
            for copy in copies(weight):
                copy.wait()

    hn = jnp.where(early, hn_a[...], hn_b[...])
    dy = jnp.where(early, dy_a[...], dy_b[...])
    gate = mm(hn, wg_ref[...])
    up = mm(hn, wu_ref[...])
    dact = mm(dy[:, :part], wd_ref[0], NT)
    for i in range(1, n_dp):
        dact += mm(dy[:, i * part:(i + 1) * part], wd_ref[i], NT)
    sig = 1.0 / (1.0 + jnp.exp(-gate))
    silu = gate * sig
    act = (silu * up).astype(BF)
    dg = (dact * up * (sig + silu * (1.0 - sig))).astype(BF)
    du = (dact * silu).astype(BF)
    act_ref[...] = act
    dg_ref[...] = dg
    du_ref[...] = du
    dhn = (mm(dg, wg_ref[...], NT) + mm(du, wu_ref[...], NT)).astype(BF)
    out = [mm(act, wd_ref[i]).astype(BF) for i in range(n_dp)]

    def store(dhn_ref, out_ref):
        dhn_ref[...] = dhn
        for i in range(n_dp):
            out_ref[:, i * part:(i + 1) * part] = out[i]

    @pl.when(early)
    def _():
        store(dhn_a, out_a)

    @pl.when(jnp.logical_not(early))
    def _():
        store(dhn_b, out_b)


def feed(place, hn, dy, gate, up, down, tb):
    chunk, width = hn[0].shape
    n_dp, _, units = gate[0].shape
    n_pieces = (len(gate), len(up), len(down))
    steps = 2 * chunk // tb
    row = lambda b, p: (b, 0)
    a = pl.BlockSpec((tb, width), lambda b, p: (jnp.minimum(b, steps // 2 - 1), 0))
    b = pl.BlockSpec((tb, width), lambda b, p: (jnp.maximum(b - steps // 2, 0), 0))
    anywhere = pl.BlockSpec(memory_space=pl.ANY)
    return pl.pallas_call(
        functools.partial(feed_kernel, n_pieces=n_pieces),
        grid_spec=pltpu.PrefetchScalarGridSpec(
            num_scalar_prefetch=1,
            grid=(steps,),
            in_specs=[a, b, a, b] + [anywhere] * sum(n_pieces),
            out_specs=[pl.BlockSpec((tb, units), row)] * 3 + [a, b, a, b],
            scratch_shapes=[
                pltpu.VMEM((width, units), BF),
                pltpu.VMEM((width, units), BF),
                pltpu.VMEM((n_dp, units, width // n_dp), BF),
                pltpu.SemaphoreType.DMA((3, 2, n_dp)),
            ],
        ),
        out_shape=[jax.ShapeDtypeStruct((2 * chunk, units), BF)] * 3 + [jax.ShapeDtypeStruct((chunk, width), BF)] * 4,
        cost_estimate=cost(flops=24 * chunk * width * units, bytes_accessed=6 * width * units + chunk * 30000,
                           transcendentals=2 * chunk * units),
        compiler_params=pltpu.CompilerParams(vmem_limit_bytes=VMEM_LIMIT),
        name="feed",
    )(place, *hn, *dy, *gate, *up, *down)


def weight_grad_kernel(place, *refs, n_left, n_right, n_dp):
    lefts, rights, give_ref, keep_ref = refs[:n_left * n_dp], refs[n_left * n_dp:-2], refs[-2], refs[-1]
    total, right, at = None, 0, 0
    for i in range(n_left):
        tall = jnp.concatenate([lefts[i * n_dp + j][...] for j in range(n_dp)], axis=1)
        tokens = tall.shape[0]
        term = mm(tall, rights[right][at:at + tokens, :], TN)
        total = term if total is None else total + term
        at += tokens
        if at == rights[right].shape[0]:
            right, at = right + 1, 0
    total = total.astype(BF).reshape(give_ref.shape)

    @pl.when(pl.program_id(0) == 0)
    def _():
        give_ref[...] = total

    @pl.when(pl.program_id(0) == 1)
    def _():
        keep_ref[...] = total


def weight_grad(place, lefts, rights, n_dp):
    width, units = lefts[0].shape[1], rights[0].shape[1]
    rows = width // (2 * n_dp)
    tokens = sum(left.shape[0] for left in lefts)

    def column(left, i):
        return pl.BlockSpec((left.shape[0], rows), lambda h, p: (0, 2 * i + jnp.where(h == 0, 1 - p[0], p[0])))

    return pl.pallas_call(
        functools.partial(weight_grad_kernel, n_left=len(lefts), n_right=len(rights), n_dp=n_dp),
        grid_spec=pltpu.PrefetchScalarGridSpec(
            num_scalar_prefetch=1,
            grid=(2,),
            in_specs=[column(left, i) for left in lefts for i in range(n_dp)]
            + [pl.BlockSpec(right.shape, lambda h, p: (0, 0), pipeline_mode=pl.Buffered(1)) for right in rights],
            out_specs=[pl.BlockSpec((n_dp, rows, units), lambda h, p: (0, 0, 0))] * 2,
        ),
        out_shape=[jax.ShapeDtypeStruct((n_dp, rows, units), BF)] * 2,
        cost_estimate=cost(flops=2 * tokens * width * units, bytes_accessed=2 * tokens * (width + units), transcendentals=0),
        compiler_params=pltpu.CompilerParams(vmem_limit_bytes=VMEM_LIMIT),
        name="weight_grad",
    )(place, *[left for left in lefts for _ in range(n_dp)], *rights)


def put_kernel(where, a_ref, b_ref, *refs):
    out_ref = refs[-1]

    @pl.when(pl.program_id(0) == 0)
    def _():
        out_ref[...] = a_ref[...].astype(out_ref.dtype)

    @pl.when(pl.program_id(0) == 1)
    def _():
        out_ref[...] = b_ref[...].astype(out_ref.dtype)


def put(where, a, b, into, kind):
    chunk, width = a.shape
    tb = min(256, chunk)
    per = chunk // tb
    more = () if into is None else (into,)
    return pl.pallas_call(
        put_kernel,
        grid_spec=pltpu.PrefetchScalarGridSpec(
            num_scalar_prefetch=1,
            grid=(2, per),
            in_specs=[
                pl.BlockSpec((tb, width), lambda i, r, w: (jnp.where(i == 0, r, per - 1), 0)),
                pl.BlockSpec((tb, width), lambda i, r, w: (jnp.where(i == 1, r, 0), 0)),
            ] + [pl.BlockSpec(memory_space=pl.ANY)] * len(more),
            out_specs=pl.BlockSpec((tb, width), lambda i, r, w: (jnp.where(i == 0, w[0], w[1]) * per + r, 0)),
        ),
        out_shape=jax.ShapeDtypeStruct((4 * chunk, width), kind),
        input_output_aliases={3: 0} if more else {},
        cost_estimate=cost(flops=chunk, bytes_accessed=12 * chunk * width, transcendentals=0),
        compiler_params=pltpu.CompilerParams(vmem_limit_bytes=VMEM_LIMIT),
        name="put",
    )(where, a, b, *more)


def unproject_kernel(parity, a_ref, b_ref, w_ref, out_ref):
    half = a_ref.shape[1]
    out = mm(a_ref[...], w_ref[:, :half], NT) + mm(b_ref[...], w_ref[:, half:], NT)
    out_ref[...] = out.astype(BF)


def unproject(parity, a, b, w, tb, chunk):
    tokens, half = a.shape
    width = w.shape[0]
    per = chunk // tb
    natural = lambda r, p: ((2 * (r // per) + p[0]) * per + r % per, 0)
    return pl.pallas_call(
        unproject_kernel,
        grid_spec=pltpu.PrefetchScalarGridSpec(
            num_scalar_prefetch=1,
            grid=(tokens // 2 // tb,),
            in_specs=[pl.BlockSpec((tb, half), natural), pl.BlockSpec((tb, half), natural),
                      pl.BlockSpec(w.shape, lambda r, p: (0, 0))],
            out_specs=pl.BlockSpec((tb, width), lambda r, p: (r, 0)),
        ),
        out_shape=jax.ShapeDtypeStruct((tokens // 2, width), BF),
        cost_estimate=cost(flops=2 * tokens * width * half, bytes_accessed=4 * tokens * width, transcendentals=0),
        compiler_params=pltpu.CompilerParams(vmem_limit_bytes=VMEM_LIMIT),
        name="unproject",
    )(parity, a, b, w)


def close_kernel(where, a_ref, b_ref, w_ref, got_ref, x_ref, gain_ref, dhidden_ref, dz_ref, *, per):
    step = pl.program_id(0)
    half = a_ref.shape[1]
    dn = mm(a_ref[...], w_ref[:, :half], NT) + mm(b_ref[...], w_ref[:, half:], NT) + got_ref[...].astype(F32)
    x = x_ref[...].astype(F32)
    scale = lax.rsqrt(jnp.mean(x * x, axis=-1, keepdims=True) + EPS)
    zr = x * scale
    gdn = gain_ref[...] * dn
    dz = scale * (gdn - zr * jnp.mean(zr * gdn, axis=-1, keepdims=True))
    dz += jnp.where(step // per == where[1], dhidden_ref[...], 0.0)
    dz_ref[...] = dz.astype(BF)


def close(where, a, b, w, got, xs, gain, dhidden, tb, chunk):
    tokens, width = got.shape
    half = a.shape[1]
    per = chunk // tb
    row = lambda r, p: (r, 0)
    fixed = lambda r, p: (0, 0)
    natural = lambda r, p: ((2 * (r // per) + p[0]) * per + r % per, 0)
    return pl.pallas_call(
        functools.partial(close_kernel, per=per),
        grid_spec=pltpu.PrefetchScalarGridSpec(
            num_scalar_prefetch=1,
            grid=(tokens // tb,),
            in_specs=[
                pl.BlockSpec((tb, half), natural),
                pl.BlockSpec((tb, half), natural),
                pl.BlockSpec(w.shape, fixed),
                pl.BlockSpec((tb, width), row),
                pl.BlockSpec((tb, width), natural),
                pl.BlockSpec((1, width), fixed),
                pl.BlockSpec((tb, width), lambda r, p: (r % per, 0)),
            ],
            out_specs=pl.BlockSpec((tb, width), row),
        ),
        out_shape=jax.ShapeDtypeStruct((tokens, width), BF),
        cost_estimate=cost(flops=4 * tokens * width * half, bytes_accessed=10 * tokens * width, transcendentals=0),
        compiler_params=pltpu.CompilerParams(vmem_limit_bytes=VMEM_LIMIT),
        name="close",
    )(where, a, b, w, got, xs, gain, dhidden)


def rope_tables(length):
    positions = lax.optimization_barrier(jnp.arange(length, dtype=jnp.int32))
    frequency = ROPE_BASE ** (-jnp.arange(0, HD, 2).astype(F32) / HD)
    angles = positions.astype(F32)[:, None] * frequency[None, :]
    cos, sin = jnp.cos(angles), jnp.sin(angles)
    return jnp.concatenate([cos] * 4, axis=1), jnp.concatenate([-sin, sin] * 2, axis=1)


def tie(*values):
    return lax.optimization_barrier(values)


def rms(z):
    return lax.rsqrt(jnp.mean(z * z, axis=-1, keepdims=True) + EPS)


def norm_back(z, scale, gain, dn):
    zr = z * scale
    gdn = gain * dn
    return scale * (gdn - zr * jnp.mean(zr * gdn, axis=-1, keepdims=True))


def on_device(layer_input, cotangent, attn_gain, query_weight, key_weight, value_weight, query_gain, key_gain,
              out_weight, ffn_gain, gate_weight, up_weight, down_weight):
    n_dp, n_ctx, n_tensor = (lax.axis_size(a) for a in ("dp", "ctx", "tensor"))
    seqs, local_len, width = layer_input.shape
    assert seqs == 2 and n_tensor == 4
    chunk = local_len // 2
    length = local_len * n_ctx
    t = lax.axis_index("tensor")
    seq, core = t // 2, t % 2
    ctx = lax.axis_index("ctx")

    def own_chunk(place, which):
        return jnp.where(place % 2 == which, place, 2 * n_ctx - 1 - place)

    id_here, id_there = own_chunk(ctx, core), own_chunk(ctx, 1 - core)
    ids = jnp.stack([id_here, id_there]).astype(jnp.int32)

    def swap_core(x):
        return lax.ppermute(x, "tensor", [(i, i ^ 1) for i in range(n_tensor)])

    def swap_seq(x):
        return lax.ppermute(x, "tensor", [(i, i ^ 2) for i in range(n_tensor)])

    def swap_ctx(x):
        return lax.ppermute(x, "ctx", [(0, 1), (1, 0)])

    homes = []
    for place in range(n_ctx):
        for i in range(n_tensor):
            which = place if place % 2 == i % 2 else 2 * n_ctx - 1 - place
            homes.append((place * n_tensor + i, (which // 2) * n_tensor + i))

    def send_home(x):
        return lax.ppermute(x, ("ctx", "tensor"), homes)

    def fetch_from_home(x):
        return lax.ppermute(x, ("ctx", "tensor"), [(b, a) for a, b in homes])

    def ctx_pair(x, axis):
        if n_ctx != 2:
            return lax.all_gather(x, "ctx", axis=axis, tiled=False)
        other = swap_ctx(x)
        return jnp.where(ctx == 0, jnp.stack([x, other], axis), jnp.stack([other, x], axis))

    x_here = lax.dynamic_index_in_dim(layer_input, seq, 0, keepdims=False)
    if n_ctx == 2:
        first = swap_ctx(lax.dynamic_slice(layer_input, (seq, core * chunk, 0), (1, chunk, width))[0])
        second = swap_core(first)
        xs = jnp.zeros((length, width), BF)
        xs = lax.dynamic_update_slice(xs, x_here, (ctx * local_len, 0))
        xs = lax.dynamic_update_slice(xs, first, ((1 - ctx) * local_len + core * chunk, 0))
        xs = lax.dynamic_update_slice(xs, second, ((1 - ctx) * local_len + (1 - core) * chunk, 0))
    else:
        xs = lax.all_gather(x_here, "ctx", axis=0, tiled=True)

    d_part, h_part = attn_gain.shape[0], query_gain.shape[0]
    nq, nk = query_weight.shape[1], key_weight.shape[1]
    n_qkv = nq + 2 * nk
    gains = jnp.concatenate([attn_gain, ffn_gain, query_gain, key_gain])
    gain_rows = -(-gains.shape[0] // LANES)
    gains = jnp.pad(gains, (0, gain_rows * LANES - gains.shape[0])).reshape(gain_rows, LANES)
    gains = jnp.pad(gains, ((0, d_part - gain_rows), (0, 0)))
    piece = jnp.concatenate([query_weight, key_weight, value_weight, gains], axis=1)
    dp = lax.axis_index("dp")
    w_all = jnp.zeros((width, 2 * n_qkv), BF)
    gains = jnp.zeros((n_dp, gain_rows, LANES), BF)
    for hop in range(n_dp):
        owner = (dp + n_dp - hop) % n_dp
        w_all = lax.dynamic_update_slice(w_all, piece[:, :n_qkv], (owner * d_part, 0))
        w_all = lax.dynamic_update_slice(w_all, swap_seq(piece[:, :n_qkv]), (owner * d_part, n_qkv))
        gains = lax.dynamic_update_slice(gains, piece[None, :gain_rows, n_qkv:], (owner, 0, 0))
        if hop < n_dp - 1:
            piece = lax.ppermute(piece, "dp", [(i, (i + 1) % n_dp) for i in range(n_dp)])
    gains = gains.reshape(n_dp, gain_rows * LANES)
    gain_a = gains[:, :d_part].reshape(1, width).astype(F32)
    gain_f = gains[:, d_part:2 * d_part].reshape(1, width).astype(F32)
    gain_q = jnp.tile(gains[:, 2 * d_part:2 * d_part + h_part].reshape(1, HD).astype(F32), (1, 2))
    gain_k = jnp.tile(gains[:, 2 * d_part + h_part:2 * d_part + 2 * h_part].reshape(1, HD).astype(F32), (1, 2))

    def half_rows(w):
        rows = w.shape[0] // 2
        return lax.dynamic_slice_in_dim(w, ctx * rows, rows, 0) if n_ctx == 2 else w

    def gather_dp(w):
        return lax.all_gather(w, "dp", axis=0, tiled=False)

    h_out = out_weight.shape[0]
    got = gather_dp(jnp.concatenate([out_weight, half_rows(down_weight)], axis=0))
    out_mine = got[:, :h_out].transpose(1, 0, 2).reshape(h_out, width)
    out_theirs = swap_seq(out_mine)
    down = [got[:, h_out:]]
    gate = [gather_dp(half_rows(gate_weight))]
    up = [gather_dp(up_weight)]
    if n_ctx == 2:
        down.append(swap_ctx(down[0]))

    cot_home = lax.dynamic_slice(cotangent, (seq, core * chunk, 0), (1, chunk, width))[0]
    dy_0 = fetch_from_home(cot_home)
    dy_2 = swap_seq(dy_0)
    dy_02 = jnp.stack([dy_0, dy_2])
    dy_13 = swap_core(dy_02)
    dy_own, dy_other = [dy_0, dy_13[0]], [dy_2, dy_13[1]]

    tb = min(256, chunk)
    cos, sin = rope_tables(length)
    normed, z, q, k, v = project(xs, gain_a, w_all, cos, sin, gain_q, gain_k, 2 * nq, 2 * nk, tb)
    if n_ctx == 2:
        q, down[1], gate[0] = tie(q, down[1], gate[0])
        gate.append(swap_ctx(gate[0]))
    o, lse = attend(ids, q, k, v, chunk)
    if n_ctx == 2:
        o, gate[1] = tie(o, gate[1])
    w_out = jnp.concatenate([out_mine, out_theirs], axis=0)
    attn = mm(o, w_out)
    got = swap_core(attn[chunk:].astype(BF))
    x_0 = lax.dynamic_slice_in_dim(xs, id_here * chunk, chunk, 0).astype(F32)
    hidden = x_0 + (attn[:chunk] + got.astype(F32))
    h_scale = rms(hidden)
    hn_0 = (hidden * h_scale * gain_f).astype(BF)
    hn_1 = swap_core(hn_0)
    hn_2 = swap_seq(hn_0)

    place = jnp.reshape(ctx, (1,)).astype(jnp.int32)

    def added(a, b):
        return (a.astype(F32) + b.astype(F32)).astype(BF)

    act_o, dg_o, du_o, y_0, y_1, dhn_0, dhn_1 = feed(place, [hn_0, hn_1], dy_own, gate, up, down, tb)
    act_o, hn_2 = tie(act_o, hn_2)
    hn_3 = swap_core(hn_2)
    act_t, dg_t, du_t, y_2, y_3, dhn_2, dhn_3 = feed(place, [hn_2, hn_3], dy_other, gate, up, down, tb)
    dhn_send = added(dhn_2, swap_core(dhn_3))
    dhn_got = swap_seq(dhn_send)

    def weight_sum(lefts, rights):
        if n_ctx == 2:
            return weight_grad(place, lefts, rights, n_dp)
        return None, mm(jnp.concatenate(lefts, axis=0), jnp.concatenate(rights, axis=0), TN).astype(BF)

    def to_ctx(give, keep):
        return swap_ctx(give) if n_ctx == 2 else keep[:1]

    def ctx_sum(keep, got):
        return added(keep, got) if n_ctx == 2 else keep

    def scatter(half):
        if n_ctx == 2:
            return lax.psum_scatter(half, "dp", scatter_dimension=0, tiled=False)
        return lax.psum_scatter(half, ("dp", "ctx"), scatter_dimension=0, tiled=True)

    def gather_rows(mine):
        return ctx_pair(mine, 0).reshape(width // n_dp, mine.shape[1])

    hn_all, dy_all = [hn_0, hn_1, hn_2, hn_3], dy_own + dy_other
    act_t, dg_t, du_t, dhn_send = tie(act_t, dg_t, du_t, dhn_send)
    give, g_gate = weight_sum(hn_all, [dg_o, dg_t])
    gate_got = to_ctx(give, g_gate)
    du_o, g_gate = tie(du_o, g_gate)
    give, g_up = weight_sum(hn_all, [du_o, du_t])
    up_got = to_ctx(give, g_up)
    act_o, g_up = tie(act_o, g_up)
    give, g_down = weight_sum(dy_all, [act_o, act_t])
    dhn_got, g_down, gate_got = tie(dhn_got, g_down, gate_got)
    down_got = to_ctx(give, g_down)

    y_send, dhn_got = tie(added(y_2, swap_core(y_3)), dhn_got)
    y_got = swap_seq(y_send)
    dhn = dhn_0.astype(F32) + swap_core(dhn_1).astype(F32) + dhn_got.astype(F32)
    dhidden = dy_0.astype(F32) + norm_back(hidden, h_scale, gain_f, dhn)
    dhr_0 = dhidden.astype(BF)
    dhr_1 = swap_core(dhr_0)
    do = mm(jnp.concatenate([dhr_0, dhr_1], axis=0), w_out, NT).astype(BF)

    def ordinal(s, c):
        return 2 * s + c

    blocks = jnp.stack([ordinal(seq, core), ordinal(seq, 1 - core), ordinal(1 - seq, core), ordinal(1 - seq, 1 - core)])
    blocks = blocks.astype(jnp.int32)

    out_give, out_keep = weight_sum([dhr_0, dhr_1], [o])
    do, gate_got, out_keep = tie(do, gate_got, out_keep)
    s_gate = scatter(ctx_sum(g_gate, gate_got))
    if n_ctx == 2:
        out_theirs_got = swap_seq(jnp.concatenate([out_give[..., h_out:], out_keep[..., h_out:]], axis=0))
        out_mine = jnp.concatenate([out_give[..., :h_out], out_keep[..., :h_out]], axis=0)
    else:
        out_theirs_got, out_mine = swap_seq(out_keep[..., h_out:]), out_keep[..., :h_out]
    dq, dk, dv = attend_back(ids, q, k, v, o, do, lse, chunk, 1)
    dq, up_got, y_got, out_theirs_got = tie(dq, up_got, y_got, out_theirs_got)
    s_up = scatter(ctx_sum(g_up, up_got))
    g_out = added(out_mine, out_theirs_got)
    out_got = to_ctx(g_out[:n_dp], g_out)
    total = hidden + (y_0.astype(F32) + swap_core(y_1).astype(F32) + y_got.astype(F32))
    total = send_home(total.astype(BF))
    d_theirs, gains_theirs = turn_back(ids, z, dq, dk, dv, cos, sin, gain_q, gain_k, tb, chunk, 1)
    give_theirs, keep_theirs = weight_sum([normed], [d_theirs])
    do, keep_theirs, down_got, s_gate = tie(do, keep_theirs, down_got, s_gate)
    s_down = scatter(ctx_sum(g_down, down_got))
    qkv_got = swap_seq(jnp.concatenate([give_theirs, keep_theirs], axis=0) if n_ctx == 2 else keep_theirs)
    dq, dk, dv = attend_back(ids, q, k, v, o, do, lse, chunk, 0)
    dq, qkv_got, out_got, total = tie(dq, qkv_got, out_got, total)
    s_out = scatter(ctx_sum(g_out[n_dp:] if n_ctx == 2 else g_out, out_got))
    total_core, total_seq = swap_core(total), swap_seq(total)
    d_mine, gains_mine = turn_back(ids, z, dq, dk, dv, cos, sin, gain_q, gain_k, tb, chunk, 0)

    d_mine, s_up, s_down = tie(d_mine, s_up, s_down)
    parity = jnp.reshape(1 - core, (1,)).astype(jnp.int32)
    give = unproject(parity, d_mine, d_theirs, w_all, tb, chunk)
    got = swap_core(give)
    d_mine, give = tie(d_mine, give)
    give, keep = weight_sum([normed], [d_mine])
    d_mine, keep, s_out, got = tie(d_mine, keep, s_out, got)
    where = jnp.stack([core, id_here // 2]).astype(jnp.int32)
    dz = close(where, d_mine, d_theirs, w_all, got, xs, gain_a, dhidden, tb, chunk)
    dz = dz.reshape(n_ctx, chunk, width)

    fold = (gains_mine + gains_theirs)[:2]
    fold = (fold[:, :HD] + fold[:, HD:]).reshape(2, n_dp, h_part)
    fold = jnp.pad(fold, ((0, 0), (0, 0), (0, d_part - h_part))).reshape(2, width)
    fold = jnp.concatenate([fold, jnp.zeros((LANES - 2, width), F32)], axis=0).astype(BF).T
    if n_ctx == 2:
        fold = fold.reshape(n_dp, 2, -1, LANES)
        fold_give, fold_keep = [lax.dynamic_index_in_dim(fold, at, 1, keepdims=False) for at in (1 - ctx, ctx)]
        give = jnp.concatenate([added(give, qkv_got[:n_dp]), fold_give], axis=-1)
        keep = jnp.concatenate([added(keep, qkv_got[n_dp:]), fold_keep], axis=-1)
    else:
        keep = jnp.concatenate([added(keep, qkv_got), fold], axis=-1)
    qkv_got = to_ctx(give, keep)
    if n_ctx == 2:
        dx = swap_ctx(lax.dynamic_index_in_dim(dz, 1 - ctx, 0, keepdims=False))
        dx, qkv_got, total_seq = tie(dx, qkv_got, total_seq)
        dx = added(lax.dynamic_index_in_dim(dz, ctx, 0, keepdims=False), dx)
    else:
        dx = lax.psum_scatter(dz, "ctx", scatter_dimension=0, tiled=False)
    s_qkv = scatter(ctx_sum(keep, qkv_got))
    dx_core, dx_seq = swap_core(dx), swap_seq(dx)
    dx_core, s_qkv = tie(dx_core, s_qkv)

    def join(piece, p_core, p_seq, kind):
        out = put(blocks[:2], piece, p_core, None, kind)
        out = put(blocks[2:], p_seq, swap_core(p_seq), out, kind)
        return out.reshape(2, local_len, width)

    layer_output = join(total, total_core, total_seq, BF)
    input_grad = join(dx, dx_core, dx_seq, F32)

    gate_grad = gather_rows(s_gate).astype(F32)
    up_grad = gather_rows(s_up).astype(F32)
    down_grad = gather_rows(s_down).T.astype(F32)
    out_grad = gather_rows(s_out).T.astype(F32)
    g = gather_rows(s_qkv).astype(F32)
    query_grad, key_grad, value_grad = g[:, :nq], g[:, nq:nq + nk], g[:, nq + nk:n_qkv]

    attn_sum = jnp.sum(query_weight.astype(F32) * query_grad, axis=1) + jnp.sum(key_weight.astype(F32) * key_grad, axis=1)
    attn_sum += jnp.sum(value_weight.astype(F32) * value_grad, axis=1)
    ffn_sum = jnp.sum(gate_weight.astype(F32) * gate_grad, axis=1) + jnp.sum(up_weight.astype(F32) * up_grad, axis=1)
    small = jnp.concatenate([attn_sum / attn_gain.astype(F32), ffn_sum / ffn_gain.astype(F32), g[:h_part, n_qkv], g[:h_part, n_qkv + 1]])
    small = small + swap_core(small)
    small = small + swap_seq(small)
    attn_gain_grad, ffn_gain_grad = small[:d_part], small[d_part:2 * d_part]
    qgain_grad, kgain_grad = small[2 * d_part:2 * d_part + h_part], small[2 * d_part + h_part:]

    return (layer_output, input_grad, attn_gain_grad, query_grad, key_grad, value_grad, qgain_grad, kgain_grad,
            out_grad, ffn_gain_grad, gate_grad, up_grad, down_grad)


def solution(mesh):
    token = P("dp", "ctx", None)
    into, out_of, vector = P("dp", "tensor"), P("tensor", "dp"), P("dp")
    return jax.shard_map(
        on_device,
        mesh=mesh,
        in_specs=(token, token, vector, into, into, into, vector, vector, out_of, vector, into, into, out_of),
        out_specs=(token, token, vector, into, into, into, vector, vector, out_of, vector, into, into, out_of),
        check_vma=False,
    )
```

```python
import functools
import math

import jax
import jax.numpy as jnp
from jax import lax
from jax.experimental import pallas as pl
from jax.experimental.pallas import tpu as pltpu
from jax.sharding import PartitionSpec as P

HD = 64
LANES = 128
EPS = 1e-05
ROPE_BASE = 1000000.0
BF = jnp.bfloat16
F32 = jnp.float32
NT = (((1,), (1,)), ((), ()))
TN = (((0,), (0,)), ((), ()))
NN = (((1,), (0,)), ((), ()))
SCALE = HD ** (-0.5)
SCORE_SCALE = SCALE * math.log2(math.e)
VMEM_LIMIT = 56 * 1024 * 1024
COST_PART = 1000


def cost(flops, bytes_accessed, transcendentals):
    return pl.CostEstimate(flops=flops // COST_PART, bytes_accessed=bytes_accessed // COST_PART,
                           transcendentals=transcendentals // COST_PART)


def mm(a, b, dims=NN):
    return lax.dot_general(a, b, dims, preferred_element_type=F32)


def low_half(shape):
    return lax.broadcasted_iota(jnp.int32, shape, 1) % HD < HD // 2


def left_head(shape):
    return lax.broadcasted_iota(jnp.int32, shape, 1) < HD


def partner(x):
    return jnp.where(low_half(x.shape), pltpu.roll(x, LANES - HD // 2, 1), pltpu.roll(x, HD // 2, 1))


def head_mean(x):
    rows = lax.broadcasted_iota(jnp.int32, (LANES, LANES), 0) // HD
    cols = lax.broadcasted_iota(jnp.int32, (LANES, LANES), 1) // HD
    ones = jnp.where(rows == cols, 1.0 / HD, 0.0).astype(BF)
    high = x.astype(BF)
    rest = (x - high.astype(F32)).astype(BF)
    return mm(high, ones) + mm(rest, ones)


def project_kernel(x_ref, gain_ref, w_ref, cos_ref, sin_ref, qg_ref, kg_ref,
                   normed_ref, z_ref, q_ref, k_ref, v_ref):
    x = x_ref[...].astype(F32)
    scale = lax.rsqrt(jnp.mean(x * x, axis=-1, keepdims=True) + EPS)
    normed = (x * scale * gain_ref[...]).astype(BF)
    normed_ref[...] = normed
    out = mm(normed, w_ref[...])
    cos, sin = cos_ref[...], sin_ref[...]
    for kind, block, at in column_blocks(q_ref.shape[1], k_ref.shape[1]):
        z = out[:, at * LANES:(at + 1) * LANES]
        if kind == "v":
            both(z, v_ref, block)
            continue
        z_ref[:, at * LANES:(at + 1) * LANES] = z
        gain = qg_ref[...] if kind == "q" else kg_ref[...]
        n = z * lax.rsqrt(head_mean(z * z) + EPS) * gain
        turned = n * cos + partner(n) * sin
        if kind == "q":
            q_ref[:, block * LANES:(block + 1) * LANES] = turned.astype(BF)
        else:
            both(turned, k_ref, block)


def column_blocks(n_q, n_k_twice):
    n_q, n_k = n_q // (2 * LANES), n_k_twice // (4 * LANES)
    blocks, at = [], 0
    for shard in range(2):
        for kind, count in (("q", n_q), ("k", n_k), ("v", n_k)):
            for i in range(count):
                blocks.append((kind, shard * count + i, at))
                at += 1
    return blocks


def both(pair, ref, block):
    swapped = pltpu.roll(pair, HD, 1)
    left = left_head(pair.shape)
    at = 2 * block * LANES
    ref[:, at:at + LANES] = jnp.where(left, pair, swapped).astype(BF)
    ref[:, at + LANES:at + 2 * LANES] = jnp.where(left, swapped, pair).astype(BF)


def project(xs, gain, w_all, cos, sin, qgain, kgain, n_qcols, n_kcols, tb):
    tokens, width = xs.shape
    cols = w_all.shape[1]
    row = lambda b: (b, 0)
    fixed = lambda b: (0, 0)
    return pl.pallas_call(
        project_kernel,
        grid=(tokens // tb,),
        in_specs=[
            pl.BlockSpec((tb, width), row),
            pl.BlockSpec((1, width), fixed),
            pl.BlockSpec((width, cols), fixed),
            pl.BlockSpec((tb, LANES), row),
            pl.BlockSpec((tb, LANES), row),
            pl.BlockSpec((1, LANES), fixed),
            pl.BlockSpec((1, LANES), fixed),
        ],
        out_specs=[
            pl.BlockSpec((tb, width), row),
            pl.BlockSpec((tb, cols), row),
            pl.BlockSpec((tb, n_qcols), row),
            pl.BlockSpec((tb, 2 * n_kcols), row),
            pl.BlockSpec((tb, 2 * n_kcols), row),
        ],
        out_shape=[
            jax.ShapeDtypeStruct((tokens, width), BF),
            jax.ShapeDtypeStruct((tokens, cols), F32),
            jax.ShapeDtypeStruct((tokens, n_qcols), BF),
            jax.ShapeDtypeStruct((tokens, 2 * n_kcols), BF),
            jax.ShapeDtypeStruct((tokens, 2 * n_kcols), BF),
        ],
        cost_estimate=cost(flops=2 * tokens * width * cols, bytes_accessed=tokens * 14000, transcendentals=0),
        compiler_params=pltpu.CompilerParams(vmem_limit_bytes=VMEM_LIMIT),
        name="project",
    )(xs, gain, w_all, cos, sin, qgain, kgain)


def attend_kernel(ids, q_ref, k_ref, v_ref, o_ref, lse_ref, acc_a, acc_b):
    chunk = q_ref.shape[0]
    own = ids[pl.program_id(1)]
    left = left_head(q_ref.shape)
    q = q_ref[...]
    zero = jnp.zeros_like(q)
    q_a, q_b = jnp.where(left, q, zero), jnp.where(left, zero, q)
    acc_a[...] = jnp.zeros_like(acc_a)
    acc_b[...] = jnp.zeros_like(acc_b)

    def block(at, masked):
        rows = pl.ds(pl.multiple_of(at * chunk, chunk), chunk)
        k, v = k_ref[rows, :], v_ref[rows, :]
        one = jnp.ones_like(v)
        for q_one, v_one, acc in ((q_a, jnp.where(left, v, one), acc_a), (q_b, jnp.where(left, one, v), acc_b)):
            p = jnp.exp2(mm(q_one, k, NT) * SCORE_SCALE)
            if masked:
                allowed = lax.broadcasted_iota(jnp.int32, p.shape, 1) <= lax.broadcasted_iota(jnp.int32, p.shape, 0)
                p = jnp.where(allowed, p, 0.0)
            acc[...] += mm(p.astype(BF), v_one)

    @pl.loop(0, own)
    def _(at):
        block(at, False)

    block(own, True)
    a, b = acc_a[...], acc_b[...]
    total = pltpu.roll(jnp.where(left, b, a), HD, 1)
    o_ref[...] = (jnp.where(left, a, b) / total).astype(BF)
    rows = jnp.transpose(jnp.log2(total))
    lse_ref[0:1, :] = rows[0:1, :]
    lse_ref[1:2, :] = rows[HD:HD + 1, :]


def attend(ids, q, k, v, chunk):
    tokens, cols = q.shape
    pairs = cols // LANES
    return pl.pallas_call(
        attend_kernel,
        grid_spec=pltpu.PrefetchScalarGridSpec(
            num_scalar_prefetch=1,
            grid=(pairs, 2),
            in_specs=[
                pl.BlockSpec((chunk, LANES), lambda j, c, ids: (ids[c], j)),
                pl.BlockSpec((tokens, LANES), lambda j, c, ids: (0, j)),
                pl.BlockSpec((tokens, LANES), lambda j, c, ids: (0, j)),
            ],
            out_specs=[
                pl.BlockSpec((chunk, LANES), lambda j, c, ids: (c, j)),
                pl.BlockSpec((8, chunk), lambda j, c, ids: (j, c)),
            ],
            scratch_shapes=[pltpu.VMEM((chunk, LANES), F32)] * 2,
        ),
        out_shape=[
            jax.ShapeDtypeStruct((2 * chunk, cols), BF),
            jax.ShapeDtypeStruct((8 * pairs, 2 * chunk), F32),
        ],
        cost_estimate=cost(
            flops=pairs * 2 * 4 * LANES * chunk * (tokens + chunk), bytes_accessed=6 * tokens * cols,
            transcendentals=pairs * 2 * chunk * (tokens + chunk)),
        compiler_params=pltpu.CompilerParams(vmem_limit_bytes=VMEM_LIMIT),
        name="attend",
    )(ids, q, k, v)


def attend_back_kernel(ids, q_ref, k_ref, v_ref, o_ref, do_ref, lse_ref, dq_ref, dk_ref, dv_ref):
    chunk = q_ref.shape[0]
    own = ids[pl.program_id(1)]
    left = left_head(q_ref.shape)
    q, do = q_ref[...], do_ref[...]
    zero = jnp.zeros_like(q)
    q_a, q_b = jnp.where(left, q, zero), jnp.where(left, zero, q)
    do_a, do_b = jnp.where(left, do, zero), jnp.where(left, zero, do)
    prod = jnp.transpose(do.astype(F32) * o_ref[...].astype(F32))
    delta_a = jnp.sum(prod[:HD], axis=0, keepdims=True)
    delta_b = jnp.sum(prod[HD:], axis=0, keepdims=True)
    lse_a, lse_b = lse_ref[0:1, :], lse_ref[1:2, :]
    dq_ref[...] = jnp.zeros_like(dq_ref)

    @pl.when(pl.program_id(1) == 0)
    def _():
        dk_ref[...] = jnp.zeros_like(dk_ref)
        dv_ref[...] = jnp.zeros_like(dv_ref)

    def block(at, masked):
        rows = pl.ds(pl.multiple_of(at * chunk, chunk), chunk)
        k, v = k_ref[rows, :], v_ref[rows, :]
        k_a, k_b = jnp.where(left, k, zero), jnp.where(left, zero, k)
        for q_one, do_one, k_one, lse, delta in ((q_a, do_a, k_a, lse_a, delta_a), (q_b, do_b, k_b, lse_b, delta_b)):
            p = jnp.exp2(mm(k, q_one, NT) * SCORE_SCALE - lse)
            if masked:
                allowed = lax.broadcasted_iota(jnp.int32, p.shape, 0) <= lax.broadcasted_iota(jnp.int32, p.shape, 1)
                p = jnp.where(allowed, p, 0.0)
            ds = (p * (mm(v, do_one, NT) - delta)).astype(BF)
            dv_ref[rows, :] += mm(p.astype(BF), do_one)
            dk_ref[rows, :] += mm(ds, q_one)
            dq_ref[...] += mm(ds, k_one, TN)

    @pl.loop(0, own)
    def _(at):
        block(at, False)

    block(own, True)


def attend_back(ids, q, k, v, o, do, lse, chunk, group):
    tokens, cols = q.shape
    pairs = cols // LANES // 2
    first = group * pairs
    whole = pl.BlockSpec((tokens, LANES), lambda j, c, ids: (0, first + j))
    mine = pl.BlockSpec((chunk, LANES), lambda j, c, ids: (c, first + j))
    natural = pl.BlockSpec((chunk, LANES), lambda j, c, ids: (ids[c], first + j))
    total = pl.BlockSpec((tokens, LANES), lambda j, c, ids: (0, j))
    return pl.pallas_call(
        attend_back_kernel,
        grid_spec=pltpu.PrefetchScalarGridSpec(
            num_scalar_prefetch=1,
            grid=(pairs, 2),
            in_specs=[natural, whole, whole, mine, mine, pl.BlockSpec((8, chunk), lambda j, c, ids: (first + j, c))],
            out_specs=[pl.BlockSpec((chunk, LANES), lambda j, c, ids: (ids[c], j)), total, total],
        ),
        out_shape=[jax.ShapeDtypeStruct((tokens, cols // 2), F32)] * 3,
        cost_estimate=cost(
            flops=pairs * 2 * 10 * LANES * chunk * (tokens + chunk), bytes_accessed=9 * tokens * cols,
            transcendentals=pairs * 2 * chunk * (tokens + chunk)),
        compiler_params=pltpu.CompilerParams(vmem_limit_bytes=VMEM_LIMIT),
        name="attend_back",
    )(ids, q, k, v, o, do, lse)


def turn_back_kernel(ids, z_ref, dq_ref, dk_ref, dv_ref, cos_ref, sin_ref, qg_ref, kg_ref, out_ref, gain_ref, *, per_chunk):
    step = pl.program_id(0)
    blocks = column_blocks(2 * dq_ref.shape[1], 2 * dk_ref.shape[1])
    blocks = blocks[:len(blocks) // 2]
    cos, sin = cos_ref[...], sin_ref[...]

    @pl.when(step == 0)
    def _():
        gain_ref[...] = jnp.zeros_like(gain_ref)

    def back(block, d, gain, row):
        z = z_ref[:, block * LANES:(block + 1) * LANES]
        scale = lax.rsqrt(head_mean(z * z) + EPS)
        d = d * SCALE
        dn = d * cos - partner(d) * sin
        zr = z * scale
        gain_ref[row:row + 1, :] += jnp.sum(dn * zr, axis=0, keepdims=True)
        gdn = gain * dn
        out_ref[:, block * LANES:(block + 1) * LANES] = (scale * (gdn - zr * head_mean(zr * gdn))).astype(BF)

    own = jnp.logical_or(step // per_chunk == ids[0], step // per_chunk == ids[1])

    @pl.when(own)
    def _():
        for kind, block, at in blocks:
            if kind == "q":
                back(at, dq_ref[:, block * LANES:(block + 1) * LANES], qg_ref[...], 0)

    @pl.when(jnp.logical_not(own))
    def _():
        for kind, _, at in blocks:
            if kind == "q":
                out_ref[:, at * LANES:(at + 1) * LANES] = jnp.zeros((out_ref.shape[0], LANES), BF)

    def folded(ref, block):
        at = 2 * block * LANES
        one, two = ref[:, at:at + LANES], ref[:, at + LANES:at + 2 * LANES]
        one, two = one + pltpu.roll(one, HD, 1), two + pltpu.roll(two, HD, 1)
        return jnp.where(left_head(one.shape), one, two)

    for kind, block, at in blocks:
        if kind == "k":
            back(at, folded(dk_ref, block), kg_ref[...], 1)
        if kind == "v":
            out_ref[:, at * LANES:(at + 1) * LANES] = folded(dv_ref, block).astype(BF)


def turn_back(ids, z, dq, dk, dv, cos, sin, qgain, kgain, tb, chunk, group):
    tokens = z.shape[0]
    n_q, n_k = dq.shape[1], dk.shape[1] // 2
    row = lambda b, ids: (b, 0)
    fixed = lambda b, ids: (0, 0)
    return pl.pallas_call(
        functools.partial(turn_back_kernel, per_chunk=chunk // tb),
        grid_spec=pltpu.PrefetchScalarGridSpec(
            num_scalar_prefetch=1,
            grid=(tokens // tb,),
            in_specs=[
                pl.BlockSpec((tb, n_q + 2 * n_k), lambda b, ids: (b, group)),
                pl.BlockSpec((tb, n_q), row),
                pl.BlockSpec((tb, 2 * n_k), row),
                pl.BlockSpec((tb, 2 * n_k), row),
                pl.BlockSpec((tb, LANES), row),
                pl.BlockSpec((tb, LANES), row),
                pl.BlockSpec((1, LANES), fixed),
                pl.BlockSpec((1, LANES), fixed),
            ],
            out_specs=[pl.BlockSpec((tb, n_q + 2 * n_k), row), pl.BlockSpec((8, LANES), fixed)],
        ),
        out_shape=[
            jax.ShapeDtypeStruct((tokens, n_q + 2 * n_k), BF),
            jax.ShapeDtypeStruct((8, LANES), F32),
        ],
        cost_estimate=cost(flops=tokens * 200000, bytes_accessed=tokens * 12000, transcendentals=0),
        compiler_params=pltpu.CompilerParams(vmem_limit_bytes=VMEM_LIMIT),
        name="turn_back",
    )(ids, z, dq, dk, dv, cos, sin, qgain, kgain)


def feed_kernel(place, *refs, n_pieces):
    hn_a, hn_b, dy_a, dy_b = refs[:4]
    pieces, rest = [], refs[4:]
    for count in n_pieces:
        pieces.append(rest[:count])
        rest = rest[count:]
    act_ref, dg_ref, du_ref, out_a, out_b, dhn_a, dhn_b, wg_ref, wu_ref, wd_ref, sems = rest
    step, steps = pl.program_id(0), pl.num_programs(0)
    early = step < steps // 2
    n_dp = wd_ref.shape[0]
    part = wd_ref.shape[2]

    def copies(weight):
        made = []
        for half, source in enumerate(pieces[weight]):
            rows = source.shape[1]
            offset = (place[0] if half == 0 else 1 - place[0]) * rows if n_pieces[weight] == 2 else 0
            for i in range(n_dp):
                if weight < 2:
                    target = (wg_ref, wu_ref)[weight]
                    window = target.at[pl.ds(pl.multiple_of(i * n_pieces[weight] * rows + offset, rows), rows), :]
                else:
                    window = wd_ref.at[i, pl.ds(pl.multiple_of(offset, rows), rows), :]
                made.append(pltpu.make_async_copy(source.at[i], window, sems.at[weight, half, i]))
        return made

    @pl.when(step == 0)
    def _():
        for weight in range(3):
            for copy in copies(weight):
                copy.start()
        for weight in range(3):
            for copy in copies(weight):
                copy.wait()

    hn = jnp.where(early, hn_a[...], hn_b[...])
    dy = jnp.where(early, dy_a[...], dy_b[...])
    gate = mm(hn, wg_ref[...])
    up = mm(hn, wu_ref[...])
    dact = mm(dy[:, :part], wd_ref[0], NT)
    for i in range(1, n_dp):
        dact += mm(dy[:, i * part:(i + 1) * part], wd_ref[i], NT)
    sig = 1.0 / (1.0 + jnp.exp(-gate))
    silu = gate * sig
    act = (silu * up).astype(BF)
    dg = (dact * up * (sig + silu * (1.0 - sig))).astype(BF)
    du = (dact * silu).astype(BF)
    act_ref[...] = act
    dg_ref[...] = dg
    du_ref[...] = du
    dhn = (mm(dg, wg_ref[...], NT) + mm(du, wu_ref[...], NT)).astype(BF)
    out = [mm(act, wd_ref[i]).astype(BF) for i in range(n_dp)]

    def store(dhn_ref, out_ref):
        dhn_ref[...] = dhn
        for i in range(n_dp):
            out_ref[:, i * part:(i + 1) * part] = out[i]

    @pl.when(early)
    def _():
        store(dhn_a, out_a)

    @pl.when(jnp.logical_not(early))
    def _():
        store(dhn_b, out_b)


def feed(place, hn, dy, gate, up, down, tb):
    chunk, width = hn[0].shape
    n_dp, _, units = gate[0].shape
    n_pieces = (len(gate), len(up), len(down))
    steps = 2 * chunk // tb
    row = lambda b, p: (b, 0)
    a = pl.BlockSpec((tb, width), lambda b, p: (jnp.minimum(b, steps // 2 - 1), 0))
    b = pl.BlockSpec((tb, width), lambda b, p: (jnp.maximum(b - steps // 2, 0), 0))
    anywhere = pl.BlockSpec(memory_space=pl.ANY)
    return pl.pallas_call(
        functools.partial(feed_kernel, n_pieces=n_pieces),
        grid_spec=pltpu.PrefetchScalarGridSpec(
            num_scalar_prefetch=1,
            grid=(steps,),
            in_specs=[a, b, a, b] + [anywhere] * sum(n_pieces),
            out_specs=[pl.BlockSpec((tb, units), row)] * 3 + [a, b, a, b],
            scratch_shapes=[
                pltpu.VMEM((width, units), BF),
                pltpu.VMEM((width, units), BF),
                pltpu.VMEM((n_dp, units, width // n_dp), BF),
                pltpu.SemaphoreType.DMA((3, 2, n_dp)),
            ],
        ),
        out_shape=[jax.ShapeDtypeStruct((2 * chunk, units), BF)] * 3 + [jax.ShapeDtypeStruct((chunk, width), BF)] * 4,
        cost_estimate=cost(flops=24 * chunk * width * units, bytes_accessed=6 * width * units + chunk * 30000,
                           transcendentals=2 * chunk * units),
        compiler_params=pltpu.CompilerParams(vmem_limit_bytes=VMEM_LIMIT),
        name="feed",
    )(place, *hn, *dy, *gate, *up, *down)


def weight_grad_kernel(place, *refs, n_left, n_right, n_dp):
    lefts, rights, give_ref, keep_ref = refs[:n_left * n_dp], refs[n_left * n_dp:-2], refs[-2], refs[-1]
    total, right, at = None, 0, 0
    for i in range(n_left):
        tall = jnp.concatenate([lefts[i * n_dp + j][...] for j in range(n_dp)], axis=1)
        tokens = tall.shape[0]
        term = mm(tall, rights[right][at:at + tokens, :], TN)
        total = term if total is None else total + term
        at += tokens
        if at == rights[right].shape[0]:
            right, at = right + 1, 0
    total = total.astype(BF).reshape(give_ref.shape)

    @pl.when(pl.program_id(0) == 0)
    def _():
        give_ref[...] = total

    @pl.when(pl.program_id(0) == 1)
    def _():
        keep_ref[...] = total


def weight_grad(place, lefts, rights, n_dp):
    width, units = lefts[0].shape[1], rights[0].shape[1]
    rows = width // (2 * n_dp)
    tokens = sum(left.shape[0] for left in lefts)

    def column(left, i):
        return pl.BlockSpec((left.shape[0], rows), lambda h, p: (0, 2 * i + jnp.where(h == 0, 1 - p[0], p[0])))

    return pl.pallas_call(
        functools.partial(weight_grad_kernel, n_left=len(lefts), n_right=len(rights), n_dp=n_dp),
        grid_spec=pltpu.PrefetchScalarGridSpec(
            num_scalar_prefetch=1,
            grid=(2,),
            in_specs=[column(left, i) for left in lefts for i in range(n_dp)]
            + [pl.BlockSpec(right.shape, lambda h, p: (0, 0), pipeline_mode=pl.Buffered(1)) for right in rights],
            out_specs=[pl.BlockSpec((n_dp, rows, units), lambda h, p: (0, 0, 0))] * 2,
        ),
        out_shape=[jax.ShapeDtypeStruct((n_dp, rows, units), BF)] * 2,
        cost_estimate=cost(flops=2 * tokens * width * units, bytes_accessed=2 * tokens * (width + units), transcendentals=0),
        compiler_params=pltpu.CompilerParams(vmem_limit_bytes=VMEM_LIMIT),
        name="weight_grad",
    )(place, *[left for left in lefts for _ in range(n_dp)], *rights)


def put_kernel(where, a_ref, b_ref, *refs):
    out_ref = refs[-1]

    @pl.when(pl.program_id(0) == 0)
    def _():
        out_ref[...] = a_ref[...].astype(out_ref.dtype)

    @pl.when(pl.program_id(0) == 1)
    def _():
        out_ref[...] = b_ref[...].astype(out_ref.dtype)


def put(where, a, b, into, kind):
    chunk, width = a.shape
    tb = min(256, chunk)
    per = chunk // tb
    more = () if into is None else (into,)
    return pl.pallas_call(
        put_kernel,
        grid_spec=pltpu.PrefetchScalarGridSpec(
            num_scalar_prefetch=1,
            grid=(2, per),
            in_specs=[
                pl.BlockSpec((tb, width), lambda i, r, w: (jnp.where(i == 0, r, per - 1), 0)),
                pl.BlockSpec((tb, width), lambda i, r, w: (jnp.where(i == 1, r, 0), 0)),
            ] + [pl.BlockSpec(memory_space=pl.ANY)] * len(more),
            out_specs=pl.BlockSpec((tb, width), lambda i, r, w: (jnp.where(i == 0, w[0], w[1]) * per + r, 0)),
        ),
        out_shape=jax.ShapeDtypeStruct((4 * chunk, width), kind),
        input_output_aliases={3: 0} if more else {},
        cost_estimate=cost(flops=chunk, bytes_accessed=12 * chunk * width, transcendentals=0),
        compiler_params=pltpu.CompilerParams(vmem_limit_bytes=VMEM_LIMIT),
        name="put",
    )(where, a, b, *more)


def unproject_kernel(parity, a_ref, b_ref, w_ref, out_ref):
    half = a_ref.shape[1]
    out = mm(a_ref[...], w_ref[:, :half], NT) + mm(b_ref[...], w_ref[:, half:], NT)
    out_ref[...] = out.astype(BF)


def unproject(parity, a, b, w, tb, chunk):
    tokens, half = a.shape
    width = w.shape[0]
    per = chunk // tb
    natural = lambda r, p: ((2 * (r // per) + p[0]) * per + r % per, 0)
    return pl.pallas_call(
        unproject_kernel,
        grid_spec=pltpu.PrefetchScalarGridSpec(
            num_scalar_prefetch=1,
            grid=(tokens // 2 // tb,),
            in_specs=[pl.BlockSpec((tb, half), natural), pl.BlockSpec((tb, half), natural),
                      pl.BlockSpec(w.shape, lambda r, p: (0, 0))],
            out_specs=pl.BlockSpec((tb, width), lambda r, p: (r, 0)),
        ),
        out_shape=jax.ShapeDtypeStruct((tokens // 2, width), BF),
        cost_estimate=cost(flops=2 * tokens * width * half, bytes_accessed=4 * tokens * width, transcendentals=0),
        compiler_params=pltpu.CompilerParams(vmem_limit_bytes=VMEM_LIMIT),
        name="unproject",
    )(parity, a, b, w)


def close_kernel(where, a_ref, b_ref, w_ref, got_ref, x_ref, gain_ref, dhidden_ref, dz_ref, *, per):
    step = pl.program_id(0)
    half = a_ref.shape[1]
    dn = mm(a_ref[...], w_ref[:, :half], NT) + mm(b_ref[...], w_ref[:, half:], NT) + got_ref[...].astype(F32)
    x = x_ref[...].astype(F32)
    scale = lax.rsqrt(jnp.mean(x * x, axis=-1, keepdims=True) + EPS)
    zr = x * scale
    gdn = gain_ref[...] * dn
    dz = scale * (gdn - zr * jnp.mean(zr * gdn, axis=-1, keepdims=True))
    dz += jnp.where(step // per == where[1], dhidden_ref[...], 0.0)
    dz_ref[...] = dz.astype(BF)


def close(where, a, b, w, got, xs, gain, dhidden, tb, chunk):
    tokens, width = got.shape
    half = a.shape[1]
    per = chunk // tb
    row = lambda r, p: (r, 0)
    fixed = lambda r, p: (0, 0)
    natural = lambda r, p: ((2 * (r // per) + p[0]) * per + r % per, 0)
    return pl.pallas_call(
        functools.partial(close_kernel, per=per),
        grid_spec=pltpu.PrefetchScalarGridSpec(
            num_scalar_prefetch=1,
            grid=(tokens // tb,),
            in_specs=[
                pl.BlockSpec((tb, half), natural),
                pl.BlockSpec((tb, half), natural),
                pl.BlockSpec(w.shape, fixed),
                pl.BlockSpec((tb, width), row),
                pl.BlockSpec((tb, width), natural),
                pl.BlockSpec((1, width), fixed),
                pl.BlockSpec((tb, width), lambda r, p: (r % per, 0)),
            ],
            out_specs=pl.BlockSpec((tb, width), row),
        ),
        out_shape=jax.ShapeDtypeStruct((tokens, width), BF),
        cost_estimate=cost(flops=4 * tokens * width * half, bytes_accessed=10 * tokens * width, transcendentals=0),
        compiler_params=pltpu.CompilerParams(vmem_limit_bytes=VMEM_LIMIT),
        name="close",
    )(where, a, b, w, got, xs, gain, dhidden)


def rope_tables(length):
    positions = lax.optimization_barrier(jnp.arange(length, dtype=jnp.int32))
    frequency = ROPE_BASE ** (-jnp.arange(0, HD, 2).astype(F32) / HD)
    angles = positions.astype(F32)[:, None] * frequency[None, :]
    cos, sin = jnp.cos(angles), jnp.sin(angles)
    return jnp.concatenate([cos] * 4, axis=1), jnp.concatenate([-sin, sin] * 2, axis=1)


def tie(*values):
    return lax.optimization_barrier(values)


def rms(z):
    return lax.rsqrt(jnp.mean(z * z, axis=-1, keepdims=True) + EPS)


def norm_back(z, scale, gain, dn):
    zr = z * scale
    gdn = gain * dn
    return scale * (gdn - zr * jnp.mean(zr * gdn, axis=-1, keepdims=True))


def on_device(layer_input, cotangent, attn_gain, query_weight, key_weight, value_weight, query_gain, key_gain,
              out_weight, ffn_gain, gate_weight, up_weight, down_weight):
    n_dp, n_ctx, n_tensor = (lax.axis_size(a) for a in ("dp", "ctx", "tensor"))
    seqs, local_len, width = layer_input.shape
    assert seqs == 2 and n_tensor == 4
    chunk = local_len // 2
    length = local_len * n_ctx
    t = lax.axis_index("tensor")
    seq, core = t // 2, t % 2
    ctx = lax.axis_index("ctx")

    def own_chunk(place, which):
        return jnp.where(place % 2 == which, place, 2 * n_ctx - 1 - place)

    id_here, id_there = own_chunk(ctx, core), own_chunk(ctx, 1 - core)
    ids = jnp.stack([id_here, id_there]).astype(jnp.int32)

    def swap_core(x):
        return lax.ppermute(x, "tensor", [(i, i ^ 1) for i in range(n_tensor)])

    def swap_seq(x):
        return lax.ppermute(x, "tensor", [(i, i ^ 2) for i in range(n_tensor)])

    def swap_ctx(x):
        return lax.ppermute(x, "ctx", [(0, 1), (1, 0)])

    homes = []
    for place in range(n_ctx):
        for i in range(n_tensor):
            which = place if place % 2 == i % 2 else 2 * n_ctx - 1 - place
            homes.append((place * n_tensor + i, (which // 2) * n_tensor + i))

    def send_home(x):
        return lax.ppermute(x, ("ctx", "tensor"), homes)

    def fetch_from_home(x):
        return lax.ppermute(x, ("ctx", "tensor"), [(b, a) for a, b in homes])

    def ctx_pair(x, axis):
        if n_ctx != 2:
            return lax.all_gather(x, "ctx", axis=axis, tiled=False)
        other = swap_ctx(x)
        return jnp.where(ctx == 0, jnp.stack([x, other], axis), jnp.stack([other, x], axis))

    x_here = lax.dynamic_index_in_dim(layer_input, seq, 0, keepdims=False)
    if n_ctx == 2:
        first = swap_ctx(lax.dynamic_slice(layer_input, (seq, core * chunk, 0), (1, chunk, width))[0])
        second = swap_core(first)
        xs = jnp.zeros((length, width), BF)
        xs = lax.dynamic_update_slice(xs, x_here, (ctx * local_len, 0))
        xs = lax.dynamic_update_slice(xs, first, ((1 - ctx) * local_len + core * chunk, 0))
        xs = lax.dynamic_update_slice(xs, second, ((1 - ctx) * local_len + (1 - core) * chunk, 0))
    else:
        xs = lax.all_gather(x_here, "ctx", axis=0, tiled=True)

    d_part, h_part = attn_gain.shape[0], query_gain.shape[0]
    nq, nk = query_weight.shape[1], key_weight.shape[1]
    n_qkv = nq + 2 * nk
    gains = jnp.concatenate([attn_gain, ffn_gain, query_gain, key_gain])
    gain_rows = -(-gains.shape[0] // LANES)
    gains = jnp.pad(gains, (0, gain_rows * LANES - gains.shape[0])).reshape(gain_rows, LANES)
    gains = jnp.pad(gains, ((0, d_part - gain_rows), (0, 0)))
    piece = jnp.concatenate([query_weight, key_weight, value_weight, gains], axis=1)
    dp = lax.axis_index("dp")
    w_all = jnp.zeros((width, 2 * n_qkv), BF)
    gains = jnp.zeros((n_dp, gain_rows, LANES), BF)
    for hop in range(n_dp):
        owner = (dp + n_dp - hop) % n_dp
        w_all = lax.dynamic_update_slice(w_all, piece[:, :n_qkv], (owner * d_part, 0))
        w_all = lax.dynamic_update_slice(w_all, swap_seq(piece[:, :n_qkv]), (owner * d_part, n_qkv))
        gains = lax.dynamic_update_slice(gains, piece[None, :gain_rows, n_qkv:], (owner, 0, 0))
        if hop < n_dp - 1:
            piece = lax.ppermute(piece, "dp", [(i, (i + 1) % n_dp) for i in range(n_dp)])
    gains = gains.reshape(n_dp, gain_rows * LANES)
    gain_a = gains[:, :d_part].reshape(1, width).astype(F32)
    gain_f = gains[:, d_part:2 * d_part].reshape(1, width).astype(F32)
    gain_q = jnp.tile(gains[:, 2 * d_part:2 * d_part + h_part].reshape(1, HD).astype(F32), (1, 2))
    gain_k = jnp.tile(gains[:, 2 * d_part + h_part:2 * d_part + 2 * h_part].reshape(1, HD).astype(F32), (1, 2))

    def half_rows(w):
        rows = w.shape[0] // 2
        return lax.dynamic_slice_in_dim(w, ctx * rows, rows, 0) if n_ctx == 2 else w

    def gather_dp(w):
        return lax.all_gather(w, "dp", axis=0, tiled=False)

    h_out = out_weight.shape[0]
    got = gather_dp(jnp.concatenate([out_weight, half_rows(down_weight)], axis=0))
    out_mine = got[:, :h_out].transpose(1, 0, 2).reshape(h_out, width)
    out_theirs = swap_seq(out_mine)
    down = [got[:, h_out:]]
    gate = [gather_dp(half_rows(gate_weight))]
    up = [gather_dp(up_weight)]
    if n_ctx == 2:
        down.append(swap_ctx(down[0]))

    cot_home = lax.dynamic_slice(cotangent, (seq, core * chunk, 0), (1, chunk, width))[0]
    dy_0 = fetch_from_home(cot_home)
    dy_2 = swap_seq(dy_0)
    dy_02 = jnp.stack([dy_0, dy_2])
    dy_13 = swap_core(dy_02)
    dy_own, dy_other = [dy_0, dy_13[0]], [dy_2, dy_13[1]]

    tb, big = min(256, chunk), min(512, chunk)
    cos, sin = rope_tables(length)
    normed, z, q, k, v = project(xs, gain_a, w_all, cos, sin, gain_q, gain_k, 2 * nq, 2 * nk, big)
    if n_ctx == 2:
        q, down[1], gate[0] = tie(q, down[1], gate[0])
        gate.append(swap_ctx(gate[0]))
    o, lse = attend(ids, q, k, v, chunk)
    if n_ctx == 2:
        o, gate[1] = tie(o, gate[1])
    w_out = jnp.concatenate([out_mine, out_theirs], axis=0)
    attn = mm(o, w_out)
    got = swap_core(attn[chunk:].astype(BF))
    x_0 = lax.dynamic_slice_in_dim(xs, id_here * chunk, chunk, 0).astype(F32)
    hidden = x_0 + (attn[:chunk] + got.astype(F32))
    h_scale = rms(hidden)
    hn_0 = (hidden * h_scale * gain_f).astype(BF)
    hn_1 = swap_core(hn_0)
    hn_2 = swap_seq(hn_0)

    place = jnp.reshape(ctx, (1,)).astype(jnp.int32)

    def added(a, b):
        return (a.astype(F32) + b.astype(F32)).astype(BF)

    act_o, dg_o, du_o, y_0, y_1, dhn_0, dhn_1 = feed(place, [hn_0, hn_1], dy_own, gate, up, down, tb)
    act_o, hn_2 = tie(act_o, hn_2)
    hn_3 = swap_core(hn_2)
    act_t, dg_t, du_t, y_2, y_3, dhn_2, dhn_3 = feed(place, [hn_2, hn_3], dy_other, gate, up, down, tb)
    dhn_send = added(dhn_2, swap_core(dhn_3))
    dhn_got = swap_seq(dhn_send)

    def weight_sum(lefts, rights):
        if n_ctx == 2:
            return weight_grad(place, lefts, rights, n_dp)
        return None, mm(jnp.concatenate(lefts, axis=0), jnp.concatenate(rights, axis=0), TN).astype(BF)

    def to_ctx(give, keep):
        return swap_ctx(give) if n_ctx == 2 else keep[:1]

    def ctx_sum(keep, got):
        return added(keep, got) if n_ctx == 2 else keep

    def scatter(half):
        if n_ctx == 2:
            return lax.psum_scatter(half, "dp", scatter_dimension=0, tiled=False)
        return lax.psum_scatter(half, ("dp", "ctx"), scatter_dimension=0, tiled=True)

    def gather_rows(mine):
        return ctx_pair(mine, 0).reshape(width // n_dp, mine.shape[1])

    hn_all, dy_all = [hn_0, hn_1, hn_2, hn_3], dy_own + dy_other
    act_t, dg_t, du_t, dhn_send = tie(act_t, dg_t, du_t, dhn_send)
    give, g_gate = weight_sum(hn_all, [dg_o, dg_t])
    gate_got = to_ctx(give, g_gate)
    du_o, g_gate = tie(du_o, g_gate)
    give, g_up = weight_sum(hn_all, [du_o, du_t])
    up_got = to_ctx(give, g_up)
    act_o, g_up = tie(act_o, g_up)
    give, g_down = weight_sum(dy_all, [act_o, act_t])
    dhn_got, g_down, gate_got = tie(dhn_got, g_down, gate_got)
    down_got = to_ctx(give, g_down)

    y_send, dhn_got = tie(added(y_2, swap_core(y_3)), dhn_got)
    y_got = swap_seq(y_send)
    dhn = dhn_0.astype(F32) + swap_core(dhn_1).astype(F32) + dhn_got.astype(F32)
    dhidden = dy_0.astype(F32) + norm_back(hidden, h_scale, gain_f, dhn)
    dhr_0 = dhidden.astype(BF)
    dhr_1 = swap_core(dhr_0)
    dhr = jnp.concatenate([dhr_0, dhr_1], axis=0)
    do = mm(dhr, w_out, NT).astype(BF)

    def ordinal(s, c):
        return 2 * s + c

    blocks = jnp.stack([ordinal(seq, core), ordinal(seq, 1 - core), ordinal(1 - seq, core), ordinal(1 - seq, 1 - core)])
    blocks = blocks.astype(jnp.int32)

    do, gate_got = tie(do, gate_got)
    s_gate = scatter(ctx_sum(g_gate, gate_got))
    dq, dk, dv = attend_back(ids, q, k, v, o, do, lse, chunk, 1)
    dq, up_got, y_got = tie(dq, up_got, y_got)
    s_up = scatter(ctx_sum(g_up, up_got))
    total = hidden + (y_0.astype(F32) + swap_core(y_1).astype(F32) + y_got.astype(F32))
    total = send_home(total.astype(BF))
    d_theirs, gains_theirs = turn_back(ids, z, dq, dk, dv, cos, sin, gain_q, gain_k, big, chunk, 1)
    give_theirs, keep_theirs = weight_sum([normed], [d_theirs])
    dhr_0, keep_theirs = tie(dhr_0, keep_theirs)
    out_give, out_keep = weight_sum([dhr_0, dhr_1], [o])
    do, out_keep, down_got, s_gate = tie(do, out_keep, down_got, s_gate)
    out_both = jnp.concatenate([out_give, out_keep], axis=0) if n_ctx == 2 else out_keep
    out_got = swap_seq(out_both[..., h_out:])
    s_down = scatter(ctx_sum(g_down, down_got))
    qkv_got = swap_seq(jnp.concatenate([give_theirs, keep_theirs], axis=0) if n_ctx == 2 else keep_theirs)
    dq, dk, dv = attend_back(ids, q, k, v, o, do, lse, chunk, 0)
    dq, out_got, total = tie(dq, out_got, total)
    g_out = added(out_both[..., :h_out], out_got)
    out_got = to_ctx(g_out[:n_dp], g_out)
    total_core, total_seq = swap_core(total), swap_seq(total)
    d_mine, gains_mine = turn_back(ids, z, dq, dk, dv, cos, sin, gain_q, gain_k, big, chunk, 0)

    d_mine, s_up, s_down, out_got, qkv_got = tie(d_mine, s_up, s_down, out_got, qkv_got)
    s_out = scatter(ctx_sum(g_out[n_dp:], out_got) if n_ctx == 2 else g_out)
    parity = jnp.reshape(1 - core, (1,)).astype(jnp.int32)
    give = unproject(parity, d_mine, d_theirs, w_all, big, chunk)
    got = swap_core(give)
    d_mine, give = tie(d_mine, give)
    give, keep = weight_sum([normed], [d_mine])
    fold = (gains_mine + gains_theirs)[:2]
    fold = (fold[:, :HD] + fold[:, HD:]).reshape(2, n_dp, h_part)
    fold = jnp.pad(fold, ((0, 0), (0, 0), (0, d_part - h_part))).reshape(2, width)
    fold = jnp.concatenate([fold, jnp.zeros((LANES - 2, width), F32)], axis=0).astype(BF).T
    if n_ctx == 2:
        fold = fold.reshape(n_dp, 2, -1, LANES)
        fold_give, fold_keep = [lax.dynamic_index_in_dim(fold, at, 1, keepdims=False) for at in (1 - ctx, ctx)]
        give = jnp.concatenate([added(give, qkv_got[:n_dp]), fold_give], axis=-1)
        keep = jnp.concatenate([added(keep, qkv_got[n_dp:]), fold_keep], axis=-1)
    else:
        keep = jnp.concatenate([added(keep, qkv_got), fold], axis=-1)
    d_mine, give, got = tie(d_mine, give, got)
    qkv_got = to_ctx(give, keep)
    where = jnp.stack([core, id_here // 2]).astype(jnp.int32)
    dz = close(where, d_mine, d_theirs, w_all, got, xs, gain_a, dhidden, tb, chunk)
    _, qkv_got = tie(dz, qkv_got)
    s_qkv = scatter(ctx_sum(keep, qkv_got))
    dz = dz.reshape(n_ctx, chunk, width)
    if n_ctx == 2:
        dx_got = swap_ctx(lax.dynamic_index_in_dim(dz, 1 - ctx, 0, keepdims=False))
        dx_kept = lax.dynamic_index_in_dim(dz, ctx, 0, keepdims=False)
    else:
        dx_got = lax.psum_scatter(dz, "ctx", scatter_dimension=0, tiled=False)

    total, total_seq, _ = tie(total, total_seq, dz)
    total_both = swap_core(total_seq)
    out_low = put(blocks[:2], total, total_core, None, BF)
    dx_got, s_qkv, s_out, out_low, total_both = tie(dx_got, s_qkv, s_out, out_low, total_both)
    dx = added(dx_kept, dx_got) if n_ctx == 2 else dx_got
    dx_core, dx_seq = swap_core(dx), swap_seq(dx)
    s_gate, s_up, s_down, s_qkv, s_out, dx = tie(s_gate, s_up, s_down, s_qkv, s_out, dx)
    in_low = put(blocks[:2], dx, dx_core, None, F32)
    layer_output = put(blocks[2:], total_seq, total_both, out_low, BF).reshape(2, local_len, width)
    gate_grad = gather_rows(s_gate).astype(F32)
    up_grad = gather_rows(s_up).astype(F32)
    down_grad = gather_rows(s_down).T.astype(F32)
    g = gather_rows(s_qkv).astype(F32)
    dx_seq, in_low, layer_output, gate_grad, up_grad, down_grad = tie(dx_seq, in_low, layer_output, gate_grad, up_grad, down_grad)
    input_grad = put(blocks[2:], dx_seq, swap_core(dx_seq), in_low, F32).reshape(2, local_len, width)
    out_grad = gather_rows(s_out).T.astype(F32)
    query_grad, key_grad, value_grad = g[:, :nq], g[:, nq:nq + nk], g[:, nq + nk:n_qkv]

    attn_sum = jnp.sum(query_weight.astype(F32) * query_grad, axis=1) + jnp.sum(key_weight.astype(F32) * key_grad, axis=1)
    attn_sum += jnp.sum(value_weight.astype(F32) * value_grad, axis=1)
    ffn_sum = jnp.sum(gate_weight.astype(F32) * gate_grad, axis=1) + jnp.sum(up_weight.astype(F32) * up_grad, axis=1)
    small = jnp.concatenate([attn_sum / attn_gain.astype(F32), ffn_sum / ffn_gain.astype(F32), g[:h_part, n_qkv], g[:h_part, n_qkv + 1]])
    small = small + swap_core(small)
    small = small + swap_seq(small)
    attn_gain_grad, ffn_gain_grad = small[:d_part], small[d_part:2 * d_part]
    qgain_grad, kgain_grad = small[2 * d_part:2 * d_part + h_part], small[2 * d_part + h_part:]

    return (layer_output, input_grad, attn_gain_grad, query_grad, key_grad, value_grad, qgain_grad, kgain_grad,
            out_grad, ffn_gain_grad, gate_grad, up_grad, down_grad)


def solution(mesh):
    token = P("dp", "ctx", None)
    into, out_of, vector = P("dp", "tensor"), P("tensor", "dp"), P("dp")
    return jax.shard_map(
        on_device,
        mesh=mesh,
        in_specs=(token, token, vector, into, into, into, vector, vector, out_of, vector, into, into, out_of),
        out_specs=(token, token, vector, into, into, into, vector, vector, out_of, vector, into, into, out_of),
        check_vma=False,
    )
```

```python
import functools
import math

import jax
import jax.numpy as jnp
from jax import lax
from jax.experimental import pallas as pl
from jax.experimental.pallas import tpu as pltpu
from jax.sharding import PartitionSpec as P

HD = 64
LANES = 128
EPS = 1e-05
ROPE_BASE = 1000000.0
BF = jnp.bfloat16
F32 = jnp.float32
NT = (((1,), (1,)), ((), ()))
TN = (((0,), (0,)), ((), ()))
NN = (((1,), (0,)), ((), ()))
SCALE = HD ** (-0.5)
SCORE_SCALE = SCALE * math.log2(math.e)
VMEM_LIMIT = 30 * 1024 * 1024
VMEM_ALL = 56 * 1024 * 1024
COST_PART = 1000


def cost(flops, bytes_accessed, transcendentals):
    return pl.CostEstimate(flops=flops // COST_PART, bytes_accessed=bytes_accessed // COST_PART,
                           transcendentals=transcendentals // COST_PART)


def mm(a, b, dims=NN):
    return lax.dot_general(a, b, dims, preferred_element_type=F32)


def low_half(shape):
    return lax.broadcasted_iota(jnp.int32, shape, 1) % HD < HD // 2


def left_head(shape):
    return lax.broadcasted_iota(jnp.int32, shape, 1) < HD


def partner(x):
    return jnp.where(low_half(x.shape), pltpu.roll(x, LANES - HD // 2, 1), pltpu.roll(x, HD // 2, 1))


def head_mean(x):
    rows = lax.broadcasted_iota(jnp.int32, (LANES, LANES), 0) // HD
    cols = lax.broadcasted_iota(jnp.int32, (LANES, LANES), 1) // HD
    ones = jnp.where(rows == cols, 1.0 / HD, 0.0).astype(BF)
    high = x.astype(BF)
    rest = (x - high.astype(F32)).astype(BF)
    return mm(high, ones) + mm(rest, ones)


def project_kernel(x_ref, gain_ref, w_ref, cos_ref, sin_ref, qg_ref, kg_ref,
                   normed_ref, z_ref, q_ref, k_ref, v_ref):
    x = x_ref[...].astype(F32)
    scale = lax.rsqrt(jnp.mean(x * x, axis=-1, keepdims=True) + EPS)
    normed = (x * scale * gain_ref[...]).astype(BF)
    normed_ref[...] = normed
    out = mm(normed, w_ref[...])
    cos, sin = cos_ref[...], sin_ref[...]
    for kind, block, at in column_blocks(q_ref.shape[1], k_ref.shape[1]):
        z = out[:, at * LANES:(at + 1) * LANES]
        if kind == "v":
            both(z, v_ref, block)
            continue
        z_ref[:, at * LANES:(at + 1) * LANES] = z
        gain = qg_ref[...] if kind == "q" else kg_ref[...]
        n = z * lax.rsqrt(head_mean(z * z) + EPS) * gain
        turned = n * cos + partner(n) * sin
        if kind == "q":
            q_ref[:, block * LANES:(block + 1) * LANES] = turned.astype(BF)
        else:
            both(turned, k_ref, block)


def column_blocks(n_q, n_k_twice):
    n_q, n_k = n_q // (2 * LANES), n_k_twice // (4 * LANES)
    blocks, at = [], 0
    for shard in range(2):
        for kind, count in (("q", n_q), ("k", n_k), ("v", n_k)):
            for i in range(count):
                blocks.append((kind, shard * count + i, at))
                at += 1
    return blocks


def both(pair, ref, block):
    swapped = pltpu.roll(pair, HD, 1)
    left = left_head(pair.shape)
    at = 2 * block * LANES
    ref[:, at:at + LANES] = jnp.where(left, pair, swapped).astype(BF)
    ref[:, at + LANES:at + 2 * LANES] = jnp.where(left, swapped, pair).astype(BF)


def project(xs, gain, w_all, cos, sin, qgain, kgain, n_qcols, n_kcols, tb):
    tokens, width = xs.shape
    cols = w_all.shape[1]
    row = lambda b: (b, 0)
    fixed = lambda b: (0, 0)
    return pl.pallas_call(
        project_kernel,
        grid=(tokens // tb,),
        in_specs=[
            pl.BlockSpec((tb, width), row),
            pl.BlockSpec((1, width), fixed),
            pl.BlockSpec((width, cols), fixed),
            pl.BlockSpec((tb, LANES), row),
            pl.BlockSpec((tb, LANES), row),
            pl.BlockSpec((1, LANES), fixed),
            pl.BlockSpec((1, LANES), fixed),
        ],
        out_specs=[
            pl.BlockSpec((tb, width), row),
            pl.BlockSpec((tb, cols), row),
            pl.BlockSpec((tb, n_qcols), row),
            pl.BlockSpec((tb, 2 * n_kcols), row),
            pl.BlockSpec((tb, 2 * n_kcols), row),
        ],
        out_shape=[
            jax.ShapeDtypeStruct((tokens, width), BF),
            jax.ShapeDtypeStruct((tokens, cols), F32),
            jax.ShapeDtypeStruct((tokens, n_qcols), BF),
            jax.ShapeDtypeStruct((tokens, 2 * n_kcols), BF),
            jax.ShapeDtypeStruct((tokens, 2 * n_kcols), BF),
        ],
        cost_estimate=cost(flops=2 * tokens * width * cols, bytes_accessed=tokens * 14000, transcendentals=0),
        compiler_params=pltpu.CompilerParams(vmem_limit_bytes=VMEM_ALL),
        name="project",
    )(xs, gain, w_all, cos, sin, qgain, kgain)


def attend_kernel(ids, q_ref, k_ref, v_ref, o_ref, lse_ref, acc_a, acc_b):
    chunk = q_ref.shape[0]
    own = ids[pl.program_id(1)]
    left = left_head(q_ref.shape)
    q = q_ref[...]
    zero = jnp.zeros_like(q)
    q_a, q_b = jnp.where(left, q, zero), jnp.where(left, zero, q)
    acc_a[...] = jnp.zeros_like(acc_a)
    acc_b[...] = jnp.zeros_like(acc_b)

    def block(at, masked):
        rows = pl.ds(pl.multiple_of(at * chunk, chunk), chunk)
        k, v = k_ref[rows, :], v_ref[rows, :]
        one = jnp.ones_like(v)
        for q_one, v_one, acc in ((q_a, jnp.where(left, v, one), acc_a), (q_b, jnp.where(left, one, v), acc_b)):
            p = jnp.exp2(mm(q_one, k, NT) * SCORE_SCALE)
            if masked:
                allowed = lax.broadcasted_iota(jnp.int32, p.shape, 1) <= lax.broadcasted_iota(jnp.int32, p.shape, 0)
                p = jnp.where(allowed, p, 0.0)
            acc[...] += mm(p.astype(BF), v_one)

    @pl.loop(0, own)
    def _(at):
        block(at, False)

    block(own, True)
    a, b = acc_a[...], acc_b[...]
    total = pltpu.roll(jnp.where(left, b, a), HD, 1)
    o_ref[...] = (jnp.where(left, a, b) / total).astype(BF)
    rows = jnp.transpose(jnp.log2(total))
    lse_ref[0:1, :] = rows[0:1, :]
    lse_ref[1:2, :] = rows[HD:HD + 1, :]


def attend(ids, q, k, v, chunk):
    tokens, cols = q.shape
    pairs = cols // LANES
    return pl.pallas_call(
        attend_kernel,
        grid_spec=pltpu.PrefetchScalarGridSpec(
            num_scalar_prefetch=1,
            grid=(pairs, 2),
            in_specs=[
                pl.BlockSpec((chunk, LANES), lambda j, c, ids: (ids[c], j)),
                pl.BlockSpec((tokens, LANES), lambda j, c, ids: (0, j)),
                pl.BlockSpec((tokens, LANES), lambda j, c, ids: (0, j)),
            ],
            out_specs=[
                pl.BlockSpec((chunk, LANES), lambda j, c, ids: (c, j)),
                pl.BlockSpec((8, chunk), lambda j, c, ids: (j, c)),
            ],
            scratch_shapes=[pltpu.VMEM((chunk, LANES), F32)] * 2,
        ),
        out_shape=[
            jax.ShapeDtypeStruct((2 * chunk, cols), BF),
            jax.ShapeDtypeStruct((8 * pairs, 2 * chunk), F32),
        ],
        cost_estimate=cost(
            flops=pairs * 2 * 4 * LANES * chunk * (tokens + chunk), bytes_accessed=6 * tokens * cols,
            transcendentals=pairs * 2 * chunk * (tokens + chunk)),
        compiler_params=pltpu.CompilerParams(vmem_limit_bytes=VMEM_ALL),
        name="attend",
    )(ids, q, k, v)


def attend_back_kernel(ids, q_ref, k_ref, v_ref, o_ref, do_ref, lse_ref, dq_ref, dk_ref, dv_ref):
    chunk = q_ref.shape[0]
    own = ids[pl.program_id(1)]
    left = left_head(q_ref.shape)
    q, do = q_ref[...], do_ref[...]
    zero = jnp.zeros_like(q)
    q_a, q_b = jnp.where(left, q, zero), jnp.where(left, zero, q)
    do_a, do_b = jnp.where(left, do, zero), jnp.where(left, zero, do)
    prod = jnp.transpose(do.astype(F32) * o_ref[...].astype(F32))
    delta_a = jnp.sum(prod[:HD], axis=0, keepdims=True)
    delta_b = jnp.sum(prod[HD:], axis=0, keepdims=True)
    lse_a, lse_b = lse_ref[0:1, :], lse_ref[1:2, :]
    dq_ref[...] = jnp.zeros_like(dq_ref)

    @pl.when(pl.program_id(1) == 0)
    def _():
        dk_ref[...] = jnp.zeros_like(dk_ref)
        dv_ref[...] = jnp.zeros_like(dv_ref)

    def block(at, masked):
        rows = pl.ds(pl.multiple_of(at * chunk, chunk), chunk)
        k, v = k_ref[rows, :], v_ref[rows, :]
        k_a, k_b = jnp.where(left, k, zero), jnp.where(left, zero, k)
        for q_one, do_one, k_one, lse, delta in ((q_a, do_a, k_a, lse_a, delta_a), (q_b, do_b, k_b, lse_b, delta_b)):
            p = jnp.exp2(mm(k, q_one, NT) * SCORE_SCALE - lse)
            if masked:
                allowed = lax.broadcasted_iota(jnp.int32, p.shape, 0) <= lax.broadcasted_iota(jnp.int32, p.shape, 1)
                p = jnp.where(allowed, p, 0.0)
            ds = (p * (mm(v, do_one, NT) - delta)).astype(BF)
            dv_ref[rows, :] += mm(p.astype(BF), do_one)
            dk_ref[rows, :] += mm(ds, q_one)
            dq_ref[...] += mm(ds, k_one, TN)

    @pl.loop(0, own)
    def _(at):
        block(at, False)

    block(own, True)


def attend_back(ids, q, k, v, o, do, lse, chunk, group):
    tokens, cols = q.shape
    pairs = cols // LANES // 2
    first = group * pairs
    whole = pl.BlockSpec((tokens, LANES), lambda j, c, ids: (0, first + j))
    mine = pl.BlockSpec((chunk, LANES), lambda j, c, ids: (c, first + j))
    natural = pl.BlockSpec((chunk, LANES), lambda j, c, ids: (ids[c], first + j))
    total = pl.BlockSpec((tokens, LANES), lambda j, c, ids: (0, j))
    return pl.pallas_call(
        attend_back_kernel,
        grid_spec=pltpu.PrefetchScalarGridSpec(
            num_scalar_prefetch=1,
            grid=(pairs, 2),
            in_specs=[natural, whole, whole, mine, mine, pl.BlockSpec((8, chunk), lambda j, c, ids: (first + j, c))],
            out_specs=[pl.BlockSpec((chunk, LANES), lambda j, c, ids: (ids[c], j)), total, total],
        ),
        out_shape=[jax.ShapeDtypeStruct((tokens, cols // 2), F32)] * 3,
        cost_estimate=cost(
            flops=pairs * 2 * 10 * LANES * chunk * (tokens + chunk), bytes_accessed=9 * tokens * cols,
            transcendentals=pairs * 2 * chunk * (tokens + chunk)),
        compiler_params=pltpu.CompilerParams(vmem_limit_bytes=VMEM_ALL),
        name="attend_back",
    )(ids, q, k, v, o, do, lse)


def out_project_kernel(place, o_ref, mine_ref, theirs_ref, x_ref, give_ref, keep_ref):
    half = mine_ref.shape[0]
    out = mm(o_ref[:, :half], mine_ref[...]) + mm(o_ref[:, half:], theirs_ref[...])

    @pl.when(pl.program_id(0) == 0)
    def _():
        give_ref[...] = out.astype(BF)

    @pl.when(pl.program_id(0) == 1)
    def _():
        keep_ref[...] = out + x_ref[...].astype(F32)


def out_project(place, o, mine, theirs, xs, chunk):
    cols, width = o.shape[1], xs.shape[1]
    fixed = lambda s, p: (0, 0)
    return pl.pallas_call(
        out_project_kernel,
        grid_spec=pltpu.PrefetchScalarGridSpec(
            num_scalar_prefetch=1,
            grid=(2,),
            in_specs=[
                pl.BlockSpec((chunk, cols), lambda s, p: (1 - s, 0)),
                pl.BlockSpec(mine.shape, fixed),
                pl.BlockSpec(theirs.shape, fixed),
                pl.BlockSpec((chunk, width), lambda s, p: (p[0], 0)),
            ],
            out_specs=[pl.BlockSpec((chunk, width), fixed)] * 2,
        ),
        out_shape=[jax.ShapeDtypeStruct((chunk, width), BF), jax.ShapeDtypeStruct((chunk, width), F32)],
        cost_estimate=cost(flops=4 * chunk * cols * width, bytes_accessed=12 * chunk * width, transcendentals=0),
        compiler_params=pltpu.CompilerParams(vmem_limit_bytes=VMEM_LIMIT),
        name="out_project",
    )(place, o, mine, theirs, xs)


def out_back_kernel(a_ref, b_ref, mine_ref, theirs_ref, do_ref):
    half = mine_ref.shape[0]
    d = jnp.where(pl.program_id(0) == 0, a_ref[...], b_ref[...])
    do_ref[:, :half] = mm(d, mine_ref[...], NT).astype(BF)
    do_ref[:, half:] = mm(d, theirs_ref[...], NT).astype(BF)


def out_back(a, b, mine, theirs):
    chunk, width = a.shape
    cols = 2 * mine.shape[0]
    fixed = lambda s: (0, 0)
    return pl.pallas_call(
        out_back_kernel,
        grid=(2,),
        in_specs=[pl.BlockSpec((chunk, width), fixed)] * 2 + [pl.BlockSpec(mine.shape, fixed)] * 2,
        out_specs=pl.BlockSpec((chunk, cols), lambda s: (s, 0)),
        out_shape=jax.ShapeDtypeStruct((2 * chunk, cols), BF),
        cost_estimate=cost(flops=4 * chunk * cols * width, bytes_accessed=8 * chunk * width, transcendentals=0),
        compiler_params=pltpu.CompilerParams(vmem_limit_bytes=VMEM_LIMIT),
        name="out_back",
    )(a, b, mine, theirs)


def turn_back_kernel(ids, z_ref, dq_ref, dk_ref, dv_ref, cos_ref, sin_ref, qg_ref, kg_ref, out_ref, gain_ref, *, per_chunk):
    step = pl.program_id(0)
    blocks = column_blocks(2 * dq_ref.shape[1], 2 * dk_ref.shape[1])
    blocks = blocks[:len(blocks) // 2]
    cos, sin = cos_ref[...], sin_ref[...]

    @pl.when(step == 0)
    def _():
        gain_ref[...] = jnp.zeros_like(gain_ref)

    def back(block, d, gain, row):
        z = z_ref[:, block * LANES:(block + 1) * LANES]
        scale = lax.rsqrt(head_mean(z * z) + EPS)
        d = d * SCALE
        dn = d * cos - partner(d) * sin
        zr = z * scale
        gain_ref[row:row + 1, :] += jnp.sum(dn * zr, axis=0, keepdims=True)
        gdn = gain * dn
        out_ref[:, block * LANES:(block + 1) * LANES] = (scale * (gdn - zr * head_mean(zr * gdn))).astype(BF)

    own = jnp.logical_or(step // per_chunk == ids[0], step // per_chunk == ids[1])

    @pl.when(own)
    def _():
        for kind, block, at in blocks:
            if kind == "q":
                back(at, dq_ref[:, block * LANES:(block + 1) * LANES], qg_ref[...], 0)

    @pl.when(jnp.logical_not(own))
    def _():
        for kind, _, at in blocks:
            if kind == "q":
                out_ref[:, at * LANES:(at + 1) * LANES] = jnp.zeros((out_ref.shape[0], LANES), BF)

    def folded(ref, block):
        at = 2 * block * LANES
        one, two = ref[:, at:at + LANES], ref[:, at + LANES:at + 2 * LANES]
        one, two = one + pltpu.roll(one, HD, 1), two + pltpu.roll(two, HD, 1)
        return jnp.where(left_head(one.shape), one, two)

    for kind, block, at in blocks:
        if kind == "k":
            back(at, folded(dk_ref, block), kg_ref[...], 1)
        if kind == "v":
            out_ref[:, at * LANES:(at + 1) * LANES] = folded(dv_ref, block).astype(BF)


def turn_back(ids, z, dq, dk, dv, cos, sin, qgain, kgain, tb, chunk, group):
    tokens = z.shape[0]
    n_q, n_k = dq.shape[1], dk.shape[1] // 2
    row = lambda b, ids: (b, 0)
    fixed = lambda b, ids: (0, 0)
    return pl.pallas_call(
        functools.partial(turn_back_kernel, per_chunk=chunk // tb),
        grid_spec=pltpu.PrefetchScalarGridSpec(
            num_scalar_prefetch=1,
            grid=(tokens // tb,),
            in_specs=[
                pl.BlockSpec((tb, n_q + 2 * n_k), lambda b, ids: (b, group)),
                pl.BlockSpec((tb, n_q), row),
                pl.BlockSpec((tb, 2 * n_k), row),
                pl.BlockSpec((tb, 2 * n_k), row),
                pl.BlockSpec((tb, LANES), row),
                pl.BlockSpec((tb, LANES), row),
                pl.BlockSpec((1, LANES), fixed),
                pl.BlockSpec((1, LANES), fixed),
            ],
            out_specs=[pl.BlockSpec((tb, n_q + 2 * n_k), row), pl.BlockSpec((8, LANES), fixed)],
        ),
        out_shape=[
            jax.ShapeDtypeStruct((tokens, n_q + 2 * n_k), BF),
            jax.ShapeDtypeStruct((8, LANES), F32),
        ],
        cost_estimate=cost(flops=tokens * 200000, bytes_accessed=tokens * 12000, transcendentals=0),
        compiler_params=pltpu.CompilerParams(vmem_limit_bytes=VMEM_ALL),
        name="turn_back",
    )(ids, z, dq, dk, dv, cos, sin, qgain, kgain)


def feed_kernel(place, *refs, n_pieces):
    hn_a, hn_b, dy_a, dy_b = refs[:4]
    pieces, rest = [], refs[4:]
    for count in n_pieces:
        pieces.append(rest[:count])
        rest = rest[count:]
    act_ref, dg_ref, du_ref, out_a, out_b, dhn_a, dhn_b, wg_ref, wu_ref, wd_ref, sems = rest
    step, steps = pl.program_id(0), pl.num_programs(0)
    early = step < steps // 2
    n_dp = wd_ref.shape[0]
    part = wd_ref.shape[2]

    def copies(weight):
        made = []
        for half, source in enumerate(pieces[weight]):
            rows = source.shape[1]
            offset = (place[0] if half == 0 else 1 - place[0]) * rows if n_pieces[weight] == 2 else 0
            for i in range(n_dp):
                if weight < 2:
                    target = (wg_ref, wu_ref)[weight]
                    window = target.at[pl.ds(pl.multiple_of(i * n_pieces[weight] * rows + offset, rows), rows), :]
                else:
                    window = wd_ref.at[i, pl.ds(pl.multiple_of(offset, rows), rows), :]
                made.append(pltpu.make_async_copy(source.at[i], window, sems.at[weight, half, i]))
        return made

    @pl.when(step == 0)
    def _():
        for weight in range(3):
            for copy in copies(weight):
                copy.start()
        for weight in range(3):
            for copy in copies(weight):
                copy.wait()

    hn = jnp.where(early, hn_a[...], hn_b[...])
    dy = jnp.where(early, dy_a[...], dy_b[...])
    gate = mm(hn, wg_ref[...])
    up = mm(hn, wu_ref[...])
    dact = mm(dy[:, :part], wd_ref[0], NT)
    for i in range(1, n_dp):
        dact += mm(dy[:, i * part:(i + 1) * part], wd_ref[i], NT)
    sig = 1.0 / (1.0 + jnp.exp(-gate))
    silu = gate * sig
    act = (silu * up).astype(BF)
    dg = (dact * up * (sig + silu * (1.0 - sig))).astype(BF)
    du = (dact * silu).astype(BF)
    act_ref[...] = act
    dg_ref[...] = dg
    du_ref[...] = du
    dhn = (mm(dg, wg_ref[...], NT) + mm(du, wu_ref[...], NT)).astype(BF)
    out = [mm(act, wd_ref[i]).astype(BF) for i in range(n_dp)]

    def store(dhn_ref, out_ref):
        dhn_ref[...] = dhn
        for i in range(n_dp):
            out_ref[:, i * part:(i + 1) * part] = out[i]

    @pl.when(early)
    def _():
        store(dhn_a, out_a)

    @pl.when(jnp.logical_not(early))
    def _():
        store(dhn_b, out_b)


def feed(place, hn, dy, gate, up, down, tb):
    chunk, width = hn[0].shape
    n_dp, _, units = gate[0].shape
    n_pieces = (len(gate), len(up), len(down))
    steps = 2 * chunk // tb
    row = lambda b, p: (b, 0)
    a = pl.BlockSpec((tb, width), lambda b, p: (jnp.minimum(b, steps // 2 - 1), 0))
    b = pl.BlockSpec((tb, width), lambda b, p: (jnp.maximum(b - steps // 2, 0), 0))
    anywhere = pl.BlockSpec(memory_space=pl.ANY)
    return pl.pallas_call(
        functools.partial(feed_kernel, n_pieces=n_pieces),
        grid_spec=pltpu.PrefetchScalarGridSpec(
            num_scalar_prefetch=1,
            grid=(steps,),
            in_specs=[a, b, a, b] + [anywhere] * sum(n_pieces),
            out_specs=[pl.BlockSpec((tb, units), row)] * 3 + [a, b, a, b],
            scratch_shapes=[
                pltpu.VMEM((width, units), BF),
                pltpu.VMEM((width, units), BF),
                pltpu.VMEM((n_dp, units, width // n_dp), BF),
                pltpu.SemaphoreType.DMA((3, 2, n_dp)),
            ],
        ),
        out_shape=[jax.ShapeDtypeStruct((2 * chunk, units), BF)] * 3 + [jax.ShapeDtypeStruct((chunk, width), BF)] * 4,
        cost_estimate=cost(flops=24 * chunk * width * units, bytes_accessed=6 * width * units + chunk * 30000,
                           transcendentals=2 * chunk * units),
        compiler_params=pltpu.CompilerParams(vmem_limit_bytes=VMEM_LIMIT),
        name="feed",
    )(place, *hn, *dy, *gate, *up, *down)


def weight_grad_kernel(place, *refs, n_left, n_right, n_dp):
    lefts, rights, give_ref, keep_ref = refs[:n_left * n_dp], refs[n_left * n_dp:-2], refs[-2], refs[-1]
    total, right, at = None, 0, 0
    for i in range(n_left):
        tall = jnp.concatenate([lefts[i * n_dp + j][...] for j in range(n_dp)], axis=1)
        tokens = tall.shape[0]
        term = mm(tall, rights[right][at:at + tokens, :], TN)
        total = term if total is None else total + term
        at += tokens
        if at == rights[right].shape[0]:
            right, at = right + 1, 0
    total = total.astype(BF).reshape(give_ref.shape)

    @pl.when(pl.program_id(0) == 0)
    def _():
        give_ref[...] = total

    @pl.when(pl.program_id(0) == 1)
    def _():
        keep_ref[...] = total


def weight_grad(place, lefts, rights, n_dp):
    width, units = lefts[0].shape[1], rights[0].shape[1]
    rows = width // (2 * n_dp)
    tokens = sum(left.shape[0] for left in lefts)

    def column(left, i):
        return pl.BlockSpec((left.shape[0], rows), lambda h, p: (0, 2 * i + jnp.where(h == 0, 1 - p[0], p[0])))

    return pl.pallas_call(
        functools.partial(weight_grad_kernel, n_left=len(lefts), n_right=len(rights), n_dp=n_dp),
        grid_spec=pltpu.PrefetchScalarGridSpec(
            num_scalar_prefetch=1,
            grid=(2,),
            in_specs=[column(left, i) for left in lefts for i in range(n_dp)]
            + [pl.BlockSpec(right.shape, lambda h, p: (0, 0), pipeline_mode=pl.Buffered(1)) for right in rights],
            out_specs=[pl.BlockSpec((n_dp, rows, units), lambda h, p: (0, 0, 0))] * 2,
        ),
        out_shape=[jax.ShapeDtypeStruct((n_dp, rows, units), BF)] * 2,
        cost_estimate=cost(flops=2 * tokens * width * units, bytes_accessed=2 * tokens * (width + units), transcendentals=0),
        compiler_params=pltpu.CompilerParams(vmem_limit_bytes=VMEM_LIMIT),
        name="weight_grad",
    )(place, *[left for left in lefts for _ in range(n_dp)], *rights)


def put_kernel(where, a_ref, b_ref, *refs):
    out_ref = refs[-1]

    @pl.when(pl.program_id(0) == 0)
    def _():
        out_ref[...] = a_ref[...].astype(out_ref.dtype)

    @pl.when(pl.program_id(0) == 1)
    def _():
        out_ref[...] = b_ref[...].astype(out_ref.dtype)


def put(where, a, b, into, kind):
    chunk, width = a.shape
    tb = min(256, chunk)
    per = chunk // tb
    more = () if into is None else (into,)
    return pl.pallas_call(
        put_kernel,
        grid_spec=pltpu.PrefetchScalarGridSpec(
            num_scalar_prefetch=1,
            grid=(2, per),
            in_specs=[
                pl.BlockSpec((tb, width), lambda i, r, w: (jnp.where(i == 0, r, per - 1), 0)),
                pl.BlockSpec((tb, width), lambda i, r, w: (jnp.where(i == 1, r, 0), 0)),
            ] + [pl.BlockSpec(memory_space=pl.ANY)] * len(more),
            out_specs=pl.BlockSpec((tb, width), lambda i, r, w: (jnp.where(i == 0, w[0], w[1]) * per + r, 0)),
        ),
        out_shape=jax.ShapeDtypeStruct((4 * chunk, width), kind),
        input_output_aliases={3: 0} if more else {},
        cost_estimate=cost(flops=chunk, bytes_accessed=12 * chunk * width, transcendentals=0),
        compiler_params=pltpu.CompilerParams(vmem_limit_bytes=VMEM_LIMIT),
        name="put",
    )(where, a, b, *more)


def unproject_kernel(parity, a_ref, b_ref, w_ref, out_ref):
    half = a_ref.shape[1]
    out = mm(a_ref[...], w_ref[:, :half], NT) + mm(b_ref[...], w_ref[:, half:], NT)
    out_ref[...] = out.astype(BF)


def unproject(parity, a, b, w, tb, chunk):
    tokens, half = a.shape
    width = w.shape[0]
    per = chunk // tb
    natural = lambda r, p: ((2 * (r // per) + p[0]) * per + r % per, 0)
    return pl.pallas_call(
        unproject_kernel,
        grid_spec=pltpu.PrefetchScalarGridSpec(
            num_scalar_prefetch=1,
            grid=(tokens // 2 // tb,),
            in_specs=[pl.BlockSpec((tb, half), natural), pl.BlockSpec((tb, half), natural),
                      pl.BlockSpec(w.shape, lambda r, p: (0, 0))],
            out_specs=pl.BlockSpec((tb, width), lambda r, p: (r, 0)),
        ),
        out_shape=jax.ShapeDtypeStruct((tokens // 2, width), BF),
        cost_estimate=cost(flops=2 * tokens * width * half, bytes_accessed=4 * tokens * width, transcendentals=0),
        compiler_params=pltpu.CompilerParams(vmem_limit_bytes=VMEM_LIMIT),
        name="unproject",
    )(parity, a, b, w)


def close_kernel(where, a_ref, b_ref, w_ref, got_ref, x_ref, gain_ref, dhidden_ref, dz_ref, *, per):
    step = pl.program_id(0)
    half = a_ref.shape[1]
    dn = mm(a_ref[...], w_ref[:, :half], NT) + mm(b_ref[...], w_ref[:, half:], NT) + got_ref[...].astype(F32)
    x = x_ref[...].astype(F32)
    scale = lax.rsqrt(jnp.mean(x * x, axis=-1, keepdims=True) + EPS)
    zr = x * scale
    gdn = gain_ref[...] * dn
    dz = scale * (gdn - zr * jnp.mean(zr * gdn, axis=-1, keepdims=True))
    dz += jnp.where(step // per == where[1], dhidden_ref[...], 0.0)
    dz_ref[...] = dz.astype(BF)


def close(where, a, b, w, got, xs, gain, dhidden, tb, chunk):
    tokens, width = got.shape
    half = a.shape[1]
    per = chunk // tb
    row = lambda r, p: (r, 0)
    fixed = lambda r, p: (0, 0)
    natural = lambda r, p: ((2 * (r // per) + p[0]) * per + r % per, 0)
    return pl.pallas_call(
        functools.partial(close_kernel, per=per),
        grid_spec=pltpu.PrefetchScalarGridSpec(
            num_scalar_prefetch=1,
            grid=(tokens // tb,),
            in_specs=[
                pl.BlockSpec((tb, half), natural),
                pl.BlockSpec((tb, half), natural),
                pl.BlockSpec(w.shape, fixed),
                pl.BlockSpec((tb, width), row),
                pl.BlockSpec((tb, width), natural),
                pl.BlockSpec((1, width), fixed),
                pl.BlockSpec((tb, width), lambda r, p: (r % per, 0)),
            ],
            out_specs=pl.BlockSpec((tb, width), row),
        ),
        out_shape=jax.ShapeDtypeStruct((tokens, width), BF),
        cost_estimate=cost(flops=4 * tokens * width * half, bytes_accessed=10 * tokens * width, transcendentals=0),
        compiler_params=pltpu.CompilerParams(vmem_limit_bytes=VMEM_LIMIT),
        name="close",
    )(where, a, b, w, got, xs, gain, dhidden)


def rope_tables(length):
    positions = lax.optimization_barrier(jnp.arange(length, dtype=jnp.int32))
    frequency = ROPE_BASE ** (-jnp.arange(0, HD, 2).astype(F32) / HD)
    angles = positions.astype(F32)[:, None] * frequency[None, :]
    cos, sin = jnp.cos(angles), jnp.sin(angles)
    return jnp.concatenate([cos] * 4, axis=1), jnp.concatenate([-sin, sin] * 2, axis=1)


def tie(*values):
    return lax.optimization_barrier(values)


def rms(z):
    return lax.rsqrt(jnp.mean(z * z, axis=-1, keepdims=True) + EPS)


def norm_back(z, scale, gain, dn):
    zr = z * scale
    gdn = gain * dn
    return scale * (gdn - zr * jnp.mean(zr * gdn, axis=-1, keepdims=True))


def on_device(layer_input, cotangent, attn_gain, query_weight, key_weight, value_weight, query_gain, key_gain,
              out_weight, ffn_gain, gate_weight, up_weight, down_weight):
    n_dp, n_ctx, n_tensor = (lax.axis_size(a) for a in ("dp", "ctx", "tensor"))
    seqs, local_len, width = layer_input.shape
    assert seqs == 2 and n_tensor == 4
    chunk = local_len // 2
    length = local_len * n_ctx
    t = lax.axis_index("tensor")
    seq, core = t // 2, t % 2
    ctx = lax.axis_index("ctx")

    def own_chunk(place, which):
        return jnp.where(place % 2 == which, place, 2 * n_ctx - 1 - place)

    id_here, id_there = own_chunk(ctx, core), own_chunk(ctx, 1 - core)
    ids = jnp.stack([id_here, id_there]).astype(jnp.int32)

    def swap_core(x):
        return lax.ppermute(x, "tensor", [(i, i ^ 1) for i in range(n_tensor)])

    def swap_seq(x):
        return lax.ppermute(x, "tensor", [(i, i ^ 2) for i in range(n_tensor)])

    def swap_ctx(x):
        return lax.ppermute(x, "ctx", [(0, 1), (1, 0)])

    homes = []
    for place in range(n_ctx):
        for i in range(n_tensor):
            which = place if place % 2 == i % 2 else 2 * n_ctx - 1 - place
            homes.append((place * n_tensor + i, (which // 2) * n_tensor + i))

    def send_home(x):
        return lax.ppermute(x, ("ctx", "tensor"), homes)

    def fetch_from_home(x):
        return lax.ppermute(x, ("ctx", "tensor"), [(b, a) for a, b in homes])

    x_here = lax.dynamic_index_in_dim(layer_input, seq, 0, keepdims=False)
    if n_ctx == 2:
        first = swap_ctx(lax.dynamic_slice(layer_input, (seq, core * chunk, 0), (1, chunk, width))[0])
        second = swap_core(first)
        xs = jnp.zeros((length, width), BF)
        xs = lax.dynamic_update_slice(xs, x_here, (ctx * local_len, 0))
        xs = lax.dynamic_update_slice(xs, first, ((1 - ctx) * local_len + core * chunk, 0))
        xs = lax.dynamic_update_slice(xs, second, ((1 - ctx) * local_len + (1 - core) * chunk, 0))
    else:
        xs = lax.all_gather(x_here, "ctx", axis=0, tiled=True)

    d_part, h_part = attn_gain.shape[0], query_gain.shape[0]
    nq, nk = query_weight.shape[1], key_weight.shape[1]
    n_qkv = nq + 2 * nk
    gains = jnp.concatenate([attn_gain, ffn_gain, query_gain, key_gain])
    gain_rows = -(-gains.shape[0] // LANES)
    gains = jnp.pad(gains, (0, gain_rows * LANES - gains.shape[0])).reshape(gain_rows, LANES)
    gains = jnp.pad(gains, ((0, d_part - gain_rows), (0, 0)))
    piece = jnp.concatenate([query_weight, key_weight, value_weight, gains], axis=1)
    dp = lax.axis_index("dp")
    w_all = jnp.zeros((width, 2 * n_qkv), BF)
    gains = jnp.zeros((n_dp, gain_rows, LANES), BF)
    for hop in range(n_dp):
        owner = (dp + n_dp - hop) % n_dp
        w_all = lax.dynamic_update_slice(w_all, piece[:, :n_qkv], (owner * d_part, 0))
        theirs = swap_seq(piece[:, :n_qkv])
        w_all = lax.dynamic_update_slice(w_all, theirs, (owner * d_part, n_qkv))
        gains = lax.dynamic_update_slice(gains, piece[None, :gain_rows, n_qkv:], (owner, 0, 0))
        if hop < n_dp - 1:
            piece = lax.ppermute(piece, "dp", [(i, (i + 1) % n_dp) for i in range(n_dp)])
    gains = gains.reshape(n_dp, gain_rows * LANES)
    gain_a = gains[:, :d_part].reshape(1, width).astype(F32)
    gain_f = gains[:, d_part:2 * d_part].reshape(1, width).astype(F32)
    gain_q = jnp.tile(gains[:, 2 * d_part:2 * d_part + h_part].reshape(1, HD).astype(F32), (1, 2))
    gain_k = jnp.tile(gains[:, 2 * d_part + h_part:2 * d_part + 2 * h_part].reshape(1, HD).astype(F32), (1, 2))

    def half_rows(w):
        rows = w.shape[0] // 2
        return lax.dynamic_slice_in_dim(w, ctx * rows, rows, 0) if n_ctx == 2 else w

    def gather_dp(w):
        return lax.all_gather(w, "dp", axis=0, tiled=False)

    h_out = out_weight.shape[0]
    got = gather_dp(jnp.concatenate([out_weight, half_rows(down_weight)], axis=0))
    out_mine = got[:, :h_out].transpose(1, 0, 2).reshape(h_out, width)
    out_theirs = swap_seq(out_mine)
    down = [got[:, h_out:]]
    gate = [gather_dp(half_rows(gate_weight))]
    up = [gather_dp(up_weight)]
    if n_ctx == 2:
        down.append(swap_ctx(down[0]))

    cot_home = lax.dynamic_slice(cotangent, (seq, core * chunk, 0), (1, chunk, width))[0]
    dy_0 = fetch_from_home(cot_home)
    dy_2 = swap_seq(dy_0)
    dy_02 = jnp.stack([dy_0, dy_2])
    dy_13 = swap_core(dy_02)
    dy_own, dy_other = [dy_0, dy_13[0]], [dy_2, dy_13[1]]

    tb, big = min(256, chunk), min(512, chunk)
    cos, sin = rope_tables(length)
    normed, z, q, k, v = project(xs, gain_a, w_all, cos, sin, gain_q, gain_k, 2 * nq, 2 * nk, big)
    if n_ctx == 2:
        q, down[1], gate[0] = tie(q, down[1], gate[0])
        gate.append(swap_ctx(gate[0]))
    o, lse = attend(ids, q, k, v, chunk)
    if n_ctx == 2:
        o, gate[1], out_theirs = tie(o, gate[1], out_theirs)
    attn_give, attn_keep = out_project(jnp.reshape(id_here, (1,)), o, out_mine, out_theirs, xs, chunk)
    got = swap_core(attn_give)
    hidden = attn_keep + got.astype(F32)
    h_scale = rms(hidden)
    hn_0 = (hidden * h_scale * gain_f).astype(BF)
    hn_1 = swap_core(hn_0)
    hn_2 = swap_seq(hn_0)

    place = jnp.reshape(ctx, (1,)).astype(jnp.int32)

    def added(a, b):
        return (a.astype(F32) + b.astype(F32)).astype(BF)

    act_o, dg_o, du_o, y_0, y_1, dhn_0, dhn_1 = feed(place, [hn_0, hn_1], dy_own, gate, up, down, tb)
    act_o, hn_2 = tie(act_o, hn_2)
    hn_3 = swap_core(hn_2)
    act_t, dg_t, du_t, y_2, y_3, dhn_2, dhn_3 = feed(place, [hn_2, hn_3], dy_other, gate, up, down, tb)
    dhn_send = added(dhn_2, swap_core(dhn_3))
    dhn_got = swap_seq(dhn_send)

    def weight_sum(lefts, rights):
        if n_ctx == 2:
            return weight_grad(place, lefts, rights, n_dp)
        return None, mm(jnp.concatenate(lefts, axis=0), jnp.concatenate(rights, axis=0), TN).astype(BF)

    def to_ctx(give, keep):
        return swap_ctx(give) if n_ctx == 2 else keep[:1]

    def ctx_sum(keep, got):
        return added(keep, got) if n_ctx == 2 else keep

    def scatter(half):
        if n_ctx == 2:
            return lax.psum_scatter(half, "dp", scatter_dimension=0, tiled=False)
        return lax.psum_scatter(half, ("dp", "ctx"), scatter_dimension=0, tiled=True)

    def across(mine):
        return swap_ctx(mine) if n_ctx == 2 else None

    def gather_rows(mine, other):
        if n_ctx != 2:
            return lax.all_gather(mine, "ctx", axis=0, tiled=False).reshape(width // n_dp, mine.shape[-1])
        mine, other = mine.reshape(-1, mine.shape[-1]), other.reshape(-1, mine.shape[-1])
        return jnp.where(ctx == 0, jnp.concatenate([mine, other]), jnp.concatenate([other, mine]))

    hn_all, dy_all = [hn_0, hn_1, hn_2, hn_3], dy_own + dy_other
    act_t, dg_t, du_t, dhn_send = tie(act_t, dg_t, du_t, dhn_send)
    give, g_gate = weight_sum(hn_all, [dg_o, dg_t])
    gate_got = to_ctx(give, g_gate)
    du_o, g_gate = tie(du_o, g_gate)
    give, g_up = weight_sum(hn_all, [du_o, du_t])
    up_got = to_ctx(give, g_up)
    act_o, g_up = tie(act_o, g_up)
    give, g_down = weight_sum(dy_all, [act_o, act_t])
    dhn_got, g_down, gate_got = tie(dhn_got, g_down, gate_got)
    down_got = to_ctx(give, g_down)

    y_send, dhn_got = tie(added(y_2, swap_core(y_3)), dhn_got)
    y_got = swap_seq(y_send)
    dhn = dhn_0.astype(F32) + swap_core(dhn_1).astype(F32) + dhn_got.astype(F32)
    dhidden = dy_0.astype(F32) + norm_back(hidden, h_scale, gain_f, dhn)
    dhr_0 = dhidden.astype(BF)
    dhr_1 = swap_core(dhr_0)
    do = out_back(dhr_0, dhr_1, out_mine, out_theirs)

    def ordinal(s, c):
        return 2 * s + c

    blocks = jnp.stack([ordinal(seq, core), ordinal(seq, 1 - core), ordinal(1 - seq, core), ordinal(1 - seq, 1 - core)])
    blocks = blocks.astype(jnp.int32)

    do, gate_got = tie(do, gate_got)
    s_gate = scatter(ctx_sum(g_gate, gate_got))
    dq, dk, dv = attend_back(ids, q, k, v, o, do, lse, chunk, 1)
    dq, up_got, y_got = tie(dq, up_got, y_got)
    s_up = scatter(ctx_sum(g_up, up_got))
    total = hidden + (y_0.astype(F32) + swap_core(y_1).astype(F32) + y_got.astype(F32))
    total = send_home(total.astype(BF))
    d_theirs, gains_theirs = turn_back(ids, z, dq, dk, dv, cos, sin, gain_q, gain_k, big, chunk, 1)
    give_theirs, keep_theirs = weight_sum([normed], [d_theirs])
    dhr_0, keep_theirs = tie(dhr_0, keep_theirs)
    out_give, out_keep = weight_sum([dhr_0, dhr_1], [o])
    do, out_keep, down_got, s_gate = tie(do, out_keep, down_got, s_gate)
    gate_other = across(s_gate)
    out_both = jnp.concatenate([out_give, out_keep], axis=0) if n_ctx == 2 else out_keep
    out_got = swap_seq(out_both[..., h_out:])
    s_down = scatter(ctx_sum(g_down, down_got))
    qkv_got = swap_seq(jnp.concatenate([give_theirs, keep_theirs], axis=0) if n_ctx == 2 else keep_theirs)
    dq, dk, dv = attend_back(ids, q, k, v, o, do, lse, chunk, 0)
    dq, out_got, total, gate_other, s_up = tie(dq, out_got, total, gate_other, s_up)
    up_other = across(s_up)
    g_out = added(out_both[..., :h_out], out_got)
    out_got = to_ctx(g_out[:n_dp], g_out)
    total_core, total_seq = swap_core(total), swap_seq(total)
    d_mine, gains_mine = turn_back(ids, z, dq, dk, dv, cos, sin, gain_q, gain_k, big, chunk, 0)

    d_mine, up_other, s_down, out_got, qkv_got = tie(d_mine, up_other, s_down, out_got, qkv_got)
    s_out = scatter(ctx_sum(g_out[n_dp:], out_got) if n_ctx == 2 else g_out)
    give, keep = weight_sum([normed], [d_mine])
    fold = (gains_mine + gains_theirs)[:2]
    fold = (fold[:, :HD] + fold[:, HD:]).reshape(2, n_dp, h_part)
    fold = jnp.pad(fold, ((0, 0), (0, 0), (0, d_part - h_part))).reshape(2, width)
    fold = jnp.concatenate([fold, jnp.zeros((LANES - 2, width), F32)], axis=0).astype(BF).T
    if n_ctx == 2:
        fold = fold.reshape(n_dp, 2, -1, LANES)
        fold_give, fold_keep = [lax.dynamic_index_in_dim(fold, at, 1, keepdims=False) for at in (1 - ctx, ctx)]
        give = jnp.concatenate([added(give, qkv_got[:n_dp]), fold_give], axis=-1)
        keep = jnp.concatenate([added(keep, qkv_got[n_dp:]), fold_keep], axis=-1)
    else:
        keep = jnp.concatenate([added(keep, qkv_got), fold], axis=-1)
    d_mine, give, keep = tie(d_mine, give, keep)
    qkv_got = to_ctx(give, keep)
    parity = jnp.reshape(1 - core, (1,)).astype(jnp.int32)
    partial = unproject(parity, d_mine, d_theirs, w_all, big, chunk)
    got = swap_core(partial)
    total, _ = tie(total, partial)
    out_low = put(blocks[:2], total, total_core, None, BF)
    d_mine, got, out_low = tie(d_mine, got, out_low)
    where = jnp.stack([core, id_here // 2]).astype(jnp.int32)
    dz = close(where, d_mine, d_theirs, w_all, got, xs, gain_a, dhidden, tb, chunk)
    dz = dz.reshape(n_ctx, chunk, width)
    if n_ctx == 2:
        dx_got = swap_ctx(lax.dynamic_index_in_dim(dz, 1 - ctx, 0, keepdims=False))
        dx_kept = lax.dynamic_index_in_dim(dz, ctx, 0, keepdims=False)
    else:
        dx_got = lax.psum_scatter(dz, "ctx", scatter_dimension=0, tiled=False)

    qkv_got, gate_other, up_other, _ = tie(qkv_got, gate_other, up_other, dz)
    s_qkv = scatter(ctx_sum(keep, qkv_got))
    gate_grad, up_grad = gather_rows(s_gate, gate_other).astype(F32), gather_rows(s_up, up_other).astype(F32)
    ffn_sum = jnp.sum(gate_weight.astype(F32) * gate_grad, axis=1) + jnp.sum(up_weight.astype(F32) * up_grad, axis=1)
    dx_got, s_qkv, s_out, total_seq, gate_grad, up_grad, ffn_sum = tie(dx_got, s_qkv, s_out, total_seq, gate_grad, up_grad, ffn_sum)
    total_both = swap_core(total_seq)
    dx = added(dx_kept, dx_got) if n_ctx == 2 else dx_got
    dx_core, dx_seq = swap_core(dx), swap_seq(dx)
    s_down, s_qkv, s_out, dx = tie(s_down, s_qkv, s_out, dx)
    in_low = put(blocks[:2], dx, dx_core, None, F32)
    layer_output = put(blocks[2:], total_seq, total_both, out_low, BF).reshape(2, local_len, width)
    qkv_other, down_other, out_other = across(s_qkv), across(s_down), across(s_out)
    qkv_other, in_low, layer_output = tie(qkv_other, in_low, layer_output)
    g = gather_rows(s_qkv, qkv_other).astype(F32)
    query_grad, key_grad, value_grad = g[:, :nq], g[:, nq:nq + nk], g[:, nq + nk:n_qkv]

    attn_sum = jnp.sum(query_weight.astype(F32) * query_grad, axis=1) + jnp.sum(key_weight.astype(F32) * key_grad, axis=1)
    attn_sum += jnp.sum(value_weight.astype(F32) * value_grad, axis=1)
    small = jnp.concatenate([attn_sum / attn_gain.astype(F32), ffn_sum / ffn_gain.astype(F32), g[:h_part, n_qkv], g[:h_part, n_qkv + 1]])
    small = small + swap_core(small)
    small, down_other, out_other = tie(small, down_other, out_other)
    small = small + swap_seq(small)
    down_grad = gather_rows(s_down, down_other).T.astype(F32)
    out_grad = gather_rows(s_out, out_other).T.astype(F32)
    dx_seq, in_low, layer_output, down_grad, out_grad = tie(dx_seq, in_low, layer_output, down_grad, out_grad)
    input_grad = put(blocks[2:], dx_seq, swap_core(dx_seq), in_low, F32).reshape(2, local_len, width)
    attn_gain_grad, ffn_gain_grad = small[:d_part], small[d_part:2 * d_part]
    qgain_grad, kgain_grad = small[2 * d_part:2 * d_part + h_part], small[2 * d_part + h_part:]

    return (layer_output, input_grad, attn_gain_grad, query_grad, key_grad, value_grad, qgain_grad, kgain_grad,
            out_grad, ffn_gain_grad, gate_grad, up_grad, down_grad)


def solution(mesh):
    token = P("dp", "ctx", None)
    into, out_of, vector = P("dp", "tensor"), P("tensor", "dp"), P("dp")
    return jax.shard_map(
        on_device,
        mesh=mesh,
        in_specs=(token, token, vector, into, into, into, vector, vector, out_of, vector, into, into, out_of),
        out_specs=(token, token, vector, into, into, into, vector, vector, out_of, vector, into, into, out_of),
        check_vma=False,
    )
```

```python
import functools
import math

import jax
import jax.numpy as jnp
from jax import lax
from jax.experimental import pallas as pl
from jax.experimental.pallas import tpu as pltpu
from jax.sharding import PartitionSpec as P

HD = 64
LANES = 128
EPS = 1e-05
ROPE_BASE = 1000000.0
BF = jnp.bfloat16
F32 = jnp.float32
NT = (((1,), (1,)), ((), ()))
TN = (((0,), (0,)), ((), ()))
NN = (((1,), (0,)), ((), ()))
SCALE = HD ** (-0.5)
SCORE_SCALE = SCALE * math.log2(math.e)
VMEM_LIMIT = 30 * 1024 * 1024
VMEM_ALL = 56 * 1024 * 1024
COST_PART = 1000


def cost(flops, bytes_accessed, transcendentals):
    return pl.CostEstimate(flops=flops // COST_PART, bytes_accessed=bytes_accessed // COST_PART,
                           transcendentals=transcendentals // COST_PART)


def mm(a, b, dims=NN):
    return lax.dot_general(a, b, dims, preferred_element_type=F32)


def low_half(shape):
    return lax.broadcasted_iota(jnp.int32, shape, 1) % HD < HD // 2


def left_head(shape):
    return lax.broadcasted_iota(jnp.int32, shape, 1) < HD


def partner(x):
    return jnp.where(low_half(x.shape), pltpu.roll(x, LANES - HD // 2, 1), pltpu.roll(x, HD // 2, 1))


def head_mean(x):
    rows = lax.broadcasted_iota(jnp.int32, (LANES, LANES), 0) // HD
    cols = lax.broadcasted_iota(jnp.int32, (LANES, LANES), 1) // HD
    ones = jnp.where(rows == cols, 1.0 / HD, 0.0).astype(BF)
    high = x.astype(BF)
    rest = (x - high.astype(F32)).astype(BF)
    return mm(high, ones) + mm(rest, ones)


def project_kernel(x_ref, gain_ref, w_ref, cos_ref, sin_ref, qg_ref, kg_ref,
                   normed_ref, z_ref, q_ref, k_ref, v_ref):
    x = x_ref[...].astype(F32)
    scale = lax.rsqrt(jnp.mean(x * x, axis=-1, keepdims=True) + EPS)
    normed = (x * scale * gain_ref[...]).astype(BF)
    normed_ref[...] = normed
    out = mm(normed, w_ref[...])
    cos, sin = cos_ref[...], sin_ref[...]
    for kind, block, at in column_blocks(q_ref.shape[1], k_ref.shape[1]):
        z = out[:, at * LANES:(at + 1) * LANES]
        if kind == "v":
            both(z, v_ref, block)
            continue
        z_ref[:, at * LANES:(at + 1) * LANES] = z
        gain = qg_ref[...] if kind == "q" else kg_ref[...]
        n = z * lax.rsqrt(head_mean(z * z) + EPS) * gain
        turned = n * cos + partner(n) * sin
        if kind == "q":
            q_ref[:, block * LANES:(block + 1) * LANES] = turned.astype(BF)
        else:
            both(turned, k_ref, block)


def column_blocks(n_q, n_k_twice):
    n_q, n_k = n_q // (2 * LANES), n_k_twice // (4 * LANES)
    blocks, at = [], 0
    for shard in range(2):
        for kind, count in (("q", n_q), ("k", n_k), ("v", n_k)):
            for i in range(count):
                blocks.append((kind, shard * count + i, at))
                at += 1
    return blocks


def both(pair, ref, block):
    swapped = pltpu.roll(pair, HD, 1)
    left = left_head(pair.shape)
    at = 2 * block * LANES
    ref[:, at:at + LANES] = jnp.where(left, pair, swapped).astype(BF)
    ref[:, at + LANES:at + 2 * LANES] = jnp.where(left, swapped, pair).astype(BF)


def project(xs, gain, w_all, cos, sin, qgain, kgain, n_qcols, n_kcols, tb):
    tokens, width = xs.shape
    cols = w_all.shape[1]
    row = lambda b: (b, 0)
    fixed = lambda b: (0, 0)
    return pl.pallas_call(
        project_kernel,
        grid=(tokens // tb,),
        in_specs=[
            pl.BlockSpec((tb, width), row),
            pl.BlockSpec((1, width), fixed),
            pl.BlockSpec((width, cols), fixed),
            pl.BlockSpec((tb, LANES), row),
            pl.BlockSpec((tb, LANES), row),
            pl.BlockSpec((1, LANES), fixed),
            pl.BlockSpec((1, LANES), fixed),
        ],
        out_specs=[
            pl.BlockSpec((tb, width), row),
            pl.BlockSpec((tb, cols), row),
            pl.BlockSpec((tb, n_qcols), row),
            pl.BlockSpec((tb, 2 * n_kcols), row),
            pl.BlockSpec((tb, 2 * n_kcols), row),
        ],
        out_shape=[
            jax.ShapeDtypeStruct((tokens, width), BF),
            jax.ShapeDtypeStruct((tokens, cols), F32),
            jax.ShapeDtypeStruct((tokens, n_qcols), BF),
            jax.ShapeDtypeStruct((tokens, 2 * n_kcols), BF),
            jax.ShapeDtypeStruct((tokens, 2 * n_kcols), BF),
        ],
        cost_estimate=cost(flops=2 * tokens * width * cols, bytes_accessed=tokens * 14000, transcendentals=0),
        compiler_params=pltpu.CompilerParams(vmem_limit_bytes=VMEM_ALL),
        name="project",
    )(xs, gain, w_all, cos, sin, qgain, kgain)


def attend_kernel(ids, q_ref, k_ref, v_ref, o_ref, lse_ref, acc_a, acc_b):
    chunk = q_ref.shape[0]
    own = ids[pl.program_id(1)]
    left = left_head(q_ref.shape)
    q = q_ref[...]
    zero = jnp.zeros_like(q)
    q_a, q_b = jnp.where(left, q, zero), jnp.where(left, zero, q)
    acc_a[...] = jnp.zeros_like(acc_a)
    acc_b[...] = jnp.zeros_like(acc_b)

    def block(at, masked):
        rows = pl.ds(pl.multiple_of(at * chunk, chunk), chunk)
        k, v = k_ref[rows, :], v_ref[rows, :]
        one = jnp.ones_like(v)
        for q_one, v_one, acc in ((q_a, jnp.where(left, v, one), acc_a), (q_b, jnp.where(left, one, v), acc_b)):
            p = jnp.exp2(mm(q_one, k, NT) * SCORE_SCALE)
            if masked:
                allowed = lax.broadcasted_iota(jnp.int32, p.shape, 1) <= lax.broadcasted_iota(jnp.int32, p.shape, 0)
                p = jnp.where(allowed, p, 0.0)
            acc[...] += mm(p.astype(BF), v_one)

    @pl.loop(0, own)
    def _(at):
        block(at, False)

    block(own, True)
    a, b = acc_a[...], acc_b[...]
    total = pltpu.roll(jnp.where(left, b, a), HD, 1)
    o_ref[...] = (jnp.where(left, a, b) / total).astype(BF)
    rows = jnp.transpose(jnp.log2(total))
    lse_ref[0:1, :] = rows[0:1, :]
    lse_ref[1:2, :] = rows[HD:HD + 1, :]


def attend(ids, q, k, v, chunk):
    tokens, cols = q.shape
    pairs = cols // LANES
    return pl.pallas_call(
        attend_kernel,
        grid_spec=pltpu.PrefetchScalarGridSpec(
            num_scalar_prefetch=1,
            grid=(pairs, 2),
            in_specs=[
                pl.BlockSpec((chunk, LANES), lambda j, c, ids: (ids[c], j)),
                pl.BlockSpec((tokens, LANES), lambda j, c, ids: (0, j)),
                pl.BlockSpec((tokens, LANES), lambda j, c, ids: (0, j)),
            ],
            out_specs=[
                pl.BlockSpec((chunk, LANES), lambda j, c, ids: (c, j)),
                pl.BlockSpec((8, chunk), lambda j, c, ids: (j, c)),
            ],
            scratch_shapes=[pltpu.VMEM((chunk, LANES), F32)] * 2,
        ),
        out_shape=[
            jax.ShapeDtypeStruct((2 * chunk, cols), BF),
            jax.ShapeDtypeStruct((8 * pairs, 2 * chunk), F32),
        ],
        cost_estimate=cost(
            flops=pairs * 2 * 4 * LANES * chunk * (tokens + chunk), bytes_accessed=6 * tokens * cols,
            transcendentals=pairs * 2 * chunk * (tokens + chunk)),
        compiler_params=pltpu.CompilerParams(vmem_limit_bytes=VMEM_ALL),
        name="attend",
    )(ids, q, k, v)


def attend_back_kernel(ids, q_ref, k_ref, v_ref, o_ref, do_ref, lse_ref, dq_ref, dk_ref, dv_ref):
    chunk = q_ref.shape[0]
    own = ids[pl.program_id(1)]
    left = left_head(q_ref.shape)
    q, do = q_ref[...], do_ref[...]
    zero = jnp.zeros_like(q)
    q_a, q_b = jnp.where(left, q, zero), jnp.where(left, zero, q)
    do_a, do_b = jnp.where(left, do, zero), jnp.where(left, zero, do)
    prod = jnp.transpose(do.astype(F32) * o_ref[...].astype(F32))
    delta_a = jnp.sum(prod[:HD], axis=0, keepdims=True)
    delta_b = jnp.sum(prod[HD:], axis=0, keepdims=True)
    lse_a, lse_b = lse_ref[0:1, :], lse_ref[1:2, :]
    dq_ref[...] = jnp.zeros_like(dq_ref)

    @pl.when(pl.program_id(1) == 0)
    def _():
        dk_ref[...] = jnp.zeros_like(dk_ref)
        dv_ref[...] = jnp.zeros_like(dv_ref)

    def block(at, masked):
        rows = pl.ds(pl.multiple_of(at * chunk, chunk), chunk)
        k, v = k_ref[rows, :], v_ref[rows, :]
        k_a, k_b = jnp.where(left, k, zero), jnp.where(left, zero, k)
        for q_one, do_one, k_one, lse, delta in ((q_a, do_a, k_a, lse_a, delta_a), (q_b, do_b, k_b, lse_b, delta_b)):
            p = jnp.exp2(mm(k, q_one, NT) * SCORE_SCALE - lse)
            if masked:
                allowed = lax.broadcasted_iota(jnp.int32, p.shape, 0) <= lax.broadcasted_iota(jnp.int32, p.shape, 1)
                p = jnp.where(allowed, p, 0.0)
            ds = (p * (mm(v, do_one, NT) - delta)).astype(BF)
            dv_ref[rows, :] += mm(p.astype(BF), do_one)
            dk_ref[rows, :] += mm(ds, q_one)
            dq_ref[...] += mm(ds, k_one, TN)

    @pl.loop(0, own)
    def _(at):
        block(at, False)

    block(own, True)


def attend_back(ids, q, k, v, o, do, lse, chunk, group):
    tokens, cols = q.shape
    pairs = cols // LANES // 2
    first = group * pairs
    whole = pl.BlockSpec((tokens, LANES), lambda j, c, ids: (0, first + j))
    mine = pl.BlockSpec((chunk, LANES), lambda j, c, ids: (c, first + j))
    natural = pl.BlockSpec((chunk, LANES), lambda j, c, ids: (ids[c], first + j))
    total = pl.BlockSpec((tokens, LANES), lambda j, c, ids: (0, j))
    return pl.pallas_call(
        attend_back_kernel,
        grid_spec=pltpu.PrefetchScalarGridSpec(
            num_scalar_prefetch=1,
            grid=(pairs, 2),
            in_specs=[natural, whole, whole, mine, mine, pl.BlockSpec((8, chunk), lambda j, c, ids: (first + j, c))],
            out_specs=[pl.BlockSpec((chunk, LANES), lambda j, c, ids: (ids[c], j)), total, total],
        ),
        out_shape=[jax.ShapeDtypeStruct((tokens, cols // 2), F32)] * 3,
        cost_estimate=cost(
            flops=pairs * 2 * 10 * LANES * chunk * (tokens + chunk), bytes_accessed=9 * tokens * cols,
            transcendentals=pairs * 2 * chunk * (tokens + chunk)),
        compiler_params=pltpu.CompilerParams(vmem_limit_bytes=VMEM_ALL),
        name="attend_back",
    )(ids, q, k, v, o, do, lse)


def out_project_kernel(place, o_ref, mine_ref, theirs_ref, x_ref, give_ref, keep_ref):
    half = mine_ref.shape[0]
    out = mm(o_ref[:, :half], mine_ref[...]) + mm(o_ref[:, half:], theirs_ref[...])

    @pl.when(pl.program_id(0) == 0)
    def _():
        give_ref[...] = out.astype(BF)

    @pl.when(pl.program_id(0) == 1)
    def _():
        keep_ref[...] = out + x_ref[...].astype(F32)


def out_project(place, o, mine, theirs, xs, chunk):
    cols, width = o.shape[1], xs.shape[1]
    fixed = lambda s, p: (0, 0)
    return pl.pallas_call(
        out_project_kernel,
        grid_spec=pltpu.PrefetchScalarGridSpec(
            num_scalar_prefetch=1,
            grid=(2,),
            in_specs=[
                pl.BlockSpec((chunk, cols), lambda s, p: (1 - s, 0)),
                pl.BlockSpec(mine.shape, fixed),
                pl.BlockSpec(theirs.shape, fixed),
                pl.BlockSpec((chunk, width), lambda s, p: (p[0], 0)),
            ],
            out_specs=[pl.BlockSpec((chunk, width), fixed)] * 2,
        ),
        out_shape=[jax.ShapeDtypeStruct((chunk, width), BF), jax.ShapeDtypeStruct((chunk, width), F32)],
        cost_estimate=cost(flops=4 * chunk * cols * width, bytes_accessed=12 * chunk * width, transcendentals=0),
        compiler_params=pltpu.CompilerParams(vmem_limit_bytes=VMEM_LIMIT),
        name="out_project",
    )(place, o, mine, theirs, xs)


def out_back_kernel(a_ref, b_ref, mine_ref, theirs_ref, do_ref):
    half = mine_ref.shape[0]
    d = jnp.where(pl.program_id(0) == 0, a_ref[...], b_ref[...])
    do_ref[:, :half] = mm(d, mine_ref[...], NT).astype(BF)
    do_ref[:, half:] = mm(d, theirs_ref[...], NT).astype(BF)


def out_back(a, b, mine, theirs):
    chunk, width = a.shape
    cols = 2 * mine.shape[0]
    fixed = lambda s: (0, 0)
    return pl.pallas_call(
        out_back_kernel,
        grid=(2,),
        in_specs=[pl.BlockSpec((chunk, width), fixed)] * 2 + [pl.BlockSpec(mine.shape, fixed)] * 2,
        out_specs=pl.BlockSpec((chunk, cols), lambda s: (s, 0)),
        out_shape=jax.ShapeDtypeStruct((2 * chunk, cols), BF),
        cost_estimate=cost(flops=4 * chunk * cols * width, bytes_accessed=8 * chunk * width, transcendentals=0),
        compiler_params=pltpu.CompilerParams(vmem_limit_bytes=VMEM_LIMIT),
        name="out_back",
    )(a, b, mine, theirs)


def turn_back_kernel(ids, z_ref, dq_ref, dk_ref, dv_ref, cos_ref, sin_ref, qg_ref, kg_ref, out_ref, gain_ref, *, per_chunk):
    step = pl.program_id(0)
    blocks = column_blocks(2 * dq_ref.shape[1], 2 * dk_ref.shape[1])
    blocks = blocks[:len(blocks) // 2]
    cos, sin = cos_ref[...], sin_ref[...]

    @pl.when(step == 0)
    def _():
        gain_ref[...] = jnp.zeros_like(gain_ref)

    def back(block, d, gain, row):
        z = z_ref[:, block * LANES:(block + 1) * LANES]
        scale = lax.rsqrt(head_mean(z * z) + EPS)
        d = d * SCALE
        dn = d * cos - partner(d) * sin
        zr = z * scale
        gain_ref[row:row + 1, :] += jnp.sum(dn * zr, axis=0, keepdims=True)
        gdn = gain * dn
        out_ref[:, block * LANES:(block + 1) * LANES] = (scale * (gdn - zr * head_mean(zr * gdn))).astype(BF)

    own = jnp.logical_or(step // per_chunk == ids[0], step // per_chunk == ids[1])

    @pl.when(own)
    def _():
        for kind, block, at in blocks:
            if kind == "q":
                back(at, dq_ref[:, block * LANES:(block + 1) * LANES], qg_ref[...], 0)

    @pl.when(jnp.logical_not(own))
    def _():
        for kind, _, at in blocks:
            if kind == "q":
                out_ref[:, at * LANES:(at + 1) * LANES] = jnp.zeros((out_ref.shape[0], LANES), BF)

    def folded(ref, block):
        at = 2 * block * LANES
        one, two = ref[:, at:at + LANES], ref[:, at + LANES:at + 2 * LANES]
        one, two = one + pltpu.roll(one, HD, 1), two + pltpu.roll(two, HD, 1)
        return jnp.where(left_head(one.shape), one, two)

    for kind, block, at in blocks:
        if kind == "k":
            back(at, folded(dk_ref, block), kg_ref[...], 1)
        if kind == "v":
            out_ref[:, at * LANES:(at + 1) * LANES] = folded(dv_ref, block).astype(BF)


def turn_back(ids, z, dq, dk, dv, cos, sin, qgain, kgain, tb, chunk, group):
    tokens = z.shape[0]
    n_q, n_k = dq.shape[1], dk.shape[1] // 2
    row = lambda b, ids: (b, 0)
    fixed = lambda b, ids: (0, 0)
    return pl.pallas_call(
        functools.partial(turn_back_kernel, per_chunk=chunk // tb),
        grid_spec=pltpu.PrefetchScalarGridSpec(
            num_scalar_prefetch=1,
            grid=(tokens // tb,),
            in_specs=[
                pl.BlockSpec((tb, n_q + 2 * n_k), lambda b, ids: (b, group)),
                pl.BlockSpec((tb, n_q), row),
                pl.BlockSpec((tb, 2 * n_k), row),
                pl.BlockSpec((tb, 2 * n_k), row),
                pl.BlockSpec((tb, LANES), row),
                pl.BlockSpec((tb, LANES), row),
                pl.BlockSpec((1, LANES), fixed),
                pl.BlockSpec((1, LANES), fixed),
            ],
            out_specs=[pl.BlockSpec((tb, n_q + 2 * n_k), row), pl.BlockSpec((8, LANES), fixed)],
        ),
        out_shape=[
            jax.ShapeDtypeStruct((tokens, n_q + 2 * n_k), BF),
            jax.ShapeDtypeStruct((8, LANES), F32),
        ],
        cost_estimate=cost(flops=tokens * 200000, bytes_accessed=tokens * 12000, transcendentals=0),
        compiler_params=pltpu.CompilerParams(vmem_limit_bytes=VMEM_ALL),
        name="turn_back",
    )(ids, z, dq, dk, dv, cos, sin, qgain, kgain)


def feed_kernel(place, *refs, n_pieces):
    hn_a, hn_b, dy_a, dy_b = refs[:4]
    pieces, rest = [], refs[4:]
    for count in n_pieces:
        pieces.append(rest[:count])
        rest = rest[count:]
    act_ref, dg_ref, du_ref, out_a, out_b, dhn_a, dhn_b, wg_ref, wu_ref, wd_ref, sems = rest
    step, steps = pl.program_id(0), pl.num_programs(0)
    early = step < steps // 2
    n_dp = wd_ref.shape[0]
    part = wd_ref.shape[2]

    def copies(weight):
        made = []
        for half, source in enumerate(pieces[weight]):
            rows = source.shape[1]
            offset = (place[0] if half == 0 else 1 - place[0]) * rows if n_pieces[weight] == 2 else 0
            for i in range(n_dp):
                if weight < 2:
                    target = (wg_ref, wu_ref)[weight]
                    window = target.at[pl.ds(pl.multiple_of(i * n_pieces[weight] * rows + offset, rows), rows), :]
                else:
                    window = wd_ref.at[i, pl.ds(pl.multiple_of(offset, rows), rows), :]
                made.append(pltpu.make_async_copy(source.at[i], window, sems.at[weight, half, i]))
        return made

    @pl.when(step == 0)
    def _():
        for weight in range(3):
            for copy in copies(weight):
                copy.start()
        for weight in range(3):
            for copy in copies(weight):
                copy.wait()

    hn = jnp.where(early, hn_a[...], hn_b[...])
    dy = jnp.where(early, dy_a[...], dy_b[...])
    gate = mm(hn, wg_ref[...])
    up = mm(hn, wu_ref[...])
    dact = mm(dy[:, :part], wd_ref[0], NT)
    for i in range(1, n_dp):
        dact += mm(dy[:, i * part:(i + 1) * part], wd_ref[i], NT)
    sig = 1.0 / (1.0 + jnp.exp(-gate))
    silu = gate * sig
    act = (silu * up).astype(BF)
    dg = (dact * up * (sig + silu * (1.0 - sig))).astype(BF)
    du = (dact * silu).astype(BF)
    act_ref[...] = act
    dg_ref[...] = dg
    du_ref[...] = du
    dhn = (mm(dg, wg_ref[...], NT) + mm(du, wu_ref[...], NT)).astype(BF)
    out = [mm(act, wd_ref[i]).astype(BF) for i in range(n_dp)]

    def store(dhn_ref, out_ref):
        dhn_ref[...] = dhn
        for i in range(n_dp):
            out_ref[:, i * part:(i + 1) * part] = out[i]

    @pl.when(early)
    def _():
        store(dhn_a, out_a)

    @pl.when(jnp.logical_not(early))
    def _():
        store(dhn_b, out_b)


def feed(place, hn, dy, gate, up, down, tb):
    chunk, width = hn[0].shape
    n_dp, _, units = gate[0].shape
    n_pieces = (len(gate), len(up), len(down))
    steps = 2 * chunk // tb
    row = lambda b, p: (b, 0)
    a = pl.BlockSpec((tb, width), lambda b, p: (jnp.minimum(b, steps // 2 - 1), 0))
    b = pl.BlockSpec((tb, width), lambda b, p: (jnp.maximum(b - steps // 2, 0), 0))
    anywhere = pl.BlockSpec(memory_space=pl.ANY)
    return pl.pallas_call(
        functools.partial(feed_kernel, n_pieces=n_pieces),
        grid_spec=pltpu.PrefetchScalarGridSpec(
            num_scalar_prefetch=1,
            grid=(steps,),
            in_specs=[a, b, a, b] + [anywhere] * sum(n_pieces),
            out_specs=[pl.BlockSpec((tb, units), row)] * 3 + [a, b, a, b],
            scratch_shapes=[
                pltpu.VMEM((width, units), BF),
                pltpu.VMEM((width, units), BF),
                pltpu.VMEM((n_dp, units, width // n_dp), BF),
                pltpu.SemaphoreType.DMA((3, 2, n_dp)),
            ],
        ),
        out_shape=[jax.ShapeDtypeStruct((2 * chunk, units), BF)] * 3 + [jax.ShapeDtypeStruct((chunk, width), BF)] * 4,
        cost_estimate=cost(flops=24 * chunk * width * units, bytes_accessed=6 * width * units + chunk * 30000,
                           transcendentals=2 * chunk * units),
        compiler_params=pltpu.CompilerParams(vmem_limit_bytes=VMEM_LIMIT),
        name="feed",
    )(place, *hn, *dy, *gate, *up, *down)


def weight_grad_kernel(place, *refs, n_left, n_right, n_dp):
    lefts, rights, give_ref, keep_ref = refs[:n_left * n_dp], refs[n_left * n_dp:-2], refs[-2], refs[-1]
    total, right, at = None, 0, 0
    for i in range(n_left):
        tall = jnp.concatenate([lefts[i * n_dp + j][...] for j in range(n_dp)], axis=1)
        tokens = tall.shape[0]
        term = mm(tall, rights[right][at:at + tokens, :], TN)
        total = term if total is None else total + term
        at += tokens
        if at == rights[right].shape[0]:
            right, at = right + 1, 0
    total = total.astype(BF).reshape(give_ref.shape)

    @pl.when(pl.program_id(0) == 0)
    def _():
        give_ref[...] = total

    @pl.when(pl.program_id(0) == 1)
    def _():
        keep_ref[...] = total


def weight_grad(place, lefts, rights, n_dp):
    width, units = lefts[0].shape[1], rights[0].shape[1]
    rows = width // (2 * n_dp)
    tokens = sum(left.shape[0] for left in lefts)

    def column(left, i):
        return pl.BlockSpec((left.shape[0], rows), lambda h, p: (0, 2 * i + jnp.where(h == 0, 1 - p[0], p[0])))

    return pl.pallas_call(
        functools.partial(weight_grad_kernel, n_left=len(lefts), n_right=len(rights), n_dp=n_dp),
        grid_spec=pltpu.PrefetchScalarGridSpec(
            num_scalar_prefetch=1,
            grid=(2,),
            in_specs=[column(left, i) for left in lefts for i in range(n_dp)]
            + [pl.BlockSpec(right.shape, lambda h, p: (0, 0), pipeline_mode=pl.Buffered(1)) for right in rights],
            out_specs=[pl.BlockSpec((n_dp, rows, units), lambda h, p: (0, 0, 0))] * 2,
        ),
        out_shape=[jax.ShapeDtypeStruct((n_dp, rows, units), BF)] * 2,
        cost_estimate=cost(flops=2 * tokens * width * units, bytes_accessed=2 * tokens * (width + units), transcendentals=0),
        compiler_params=pltpu.CompilerParams(vmem_limit_bytes=VMEM_LIMIT),
        name="weight_grad",
    )(place, *[left for left in lefts for _ in range(n_dp)], *rights)


def put_kernel(where, *refs, n_parts):
    out_ref = refs[-1]
    for i in range(n_parts):
        @pl.when(pl.program_id(0) == i)
        def _(i=i):
            out_ref[...] = refs[i][...].astype(out_ref.dtype)


def put(where, parts, into, kind, rows):
    part, width = parts[0].shape
    tb = min(256, part)
    per = part // tb
    more = () if into is None else (into,)
    return pl.pallas_call(
        functools.partial(put_kernel, n_parts=len(parts)),
        grid_spec=pltpu.PrefetchScalarGridSpec(
            num_scalar_prefetch=1,
            grid=(len(parts), per),
            in_specs=[
                pl.BlockSpec((tb, width), lambda i, r, w, n=n: (jnp.where(i == n, r, jnp.where(i < n, 0, per - 1)), 0))
                for n in range(len(parts))
            ] + [pl.BlockSpec(memory_space=pl.ANY)] * len(more),
            out_specs=pl.BlockSpec((tb, width), lambda i, r, w: (w[i] * per + r, 0)),
        ),
        out_shape=jax.ShapeDtypeStruct((rows, width), kind),
        input_output_aliases={1 + len(parts): 0} if more else {},
        cost_estimate=cost(flops=rows, bytes_accessed=6 * len(parts) * part * width, transcendentals=0),
        compiler_params=pltpu.CompilerParams(vmem_limit_bytes=VMEM_LIMIT),
        name="put",
    )(where, *parts, *more)


def unproject_kernel(parity, a_ref, b_ref, w_ref, out_ref):
    half = a_ref.shape[1]
    out = mm(a_ref[...], w_ref[:, :half], NT) + mm(b_ref[...], w_ref[:, half:], NT)
    out_ref[...] = out.astype(BF)


def unproject(parity, a, b, w, tb, chunk):
    tokens, half = a.shape
    width = w.shape[0]
    per = chunk // tb
    natural = lambda r, p: ((2 * (r // per) + p[0]) * per + r % per, 0)
    return pl.pallas_call(
        unproject_kernel,
        grid_spec=pltpu.PrefetchScalarGridSpec(
            num_scalar_prefetch=1,
            grid=(tokens // 2 // tb,),
            in_specs=[pl.BlockSpec((tb, half), natural), pl.BlockSpec((tb, half), natural),
                      pl.BlockSpec(w.shape, lambda r, p: (0, 0))],
            out_specs=pl.BlockSpec((tb, width), lambda r, p: (r, 0)),
        ),
        out_shape=jax.ShapeDtypeStruct((tokens // 2, width), BF),
        cost_estimate=cost(flops=2 * tokens * width * half, bytes_accessed=4 * tokens * width, transcendentals=0),
        compiler_params=pltpu.CompilerParams(vmem_limit_bytes=VMEM_LIMIT),
        name="unproject",
    )(parity, a, b, w)


def close_kernel(where, a_ref, b_ref, w_ref, got_ref, x_ref, gain_ref, dhidden_ref, dz_ref, *, per):
    step = pl.program_id(0)
    half = a_ref.shape[1]
    dn = mm(a_ref[...], w_ref[:, :half], NT) + mm(b_ref[...], w_ref[:, half:], NT) + got_ref[...].astype(F32)
    x = x_ref[...].astype(F32)
    scale = lax.rsqrt(jnp.mean(x * x, axis=-1, keepdims=True) + EPS)
    zr = x * scale
    gdn = gain_ref[...] * dn
    dz = scale * (gdn - zr * jnp.mean(zr * gdn, axis=-1, keepdims=True))
    dz += jnp.where(step // per == where[1], dhidden_ref[...], 0.0)
    dz_ref[...] = dz.astype(BF)


def close(where, a, b, w, got, xs, gain, dhidden, tb, chunk):
    tokens, width = got.shape
    half = a.shape[1]
    per = chunk // tb
    row = lambda r, p: (r, 0)
    fixed = lambda r, p: (0, 0)
    natural = lambda r, p: ((2 * (r // per) + p[0]) * per + r % per, 0)
    return pl.pallas_call(
        functools.partial(close_kernel, per=per),
        grid_spec=pltpu.PrefetchScalarGridSpec(
            num_scalar_prefetch=1,
            grid=(tokens // tb,),
            in_specs=[
                pl.BlockSpec((tb, half), natural),
                pl.BlockSpec((tb, half), natural),
                pl.BlockSpec(w.shape, fixed),
                pl.BlockSpec((tb, width), row),
                pl.BlockSpec((tb, width), natural),
                pl.BlockSpec((1, width), fixed),
                pl.BlockSpec((tb, width), lambda r, p: (r % per, 0)),
            ],
            out_specs=pl.BlockSpec((tb, width), row),
        ),
        out_shape=jax.ShapeDtypeStruct((tokens, width), BF),
        cost_estimate=cost(flops=4 * tokens * width * half, bytes_accessed=10 * tokens * width, transcendentals=0),
        compiler_params=pltpu.CompilerParams(vmem_limit_bytes=VMEM_LIMIT),
        name="close",
    )(where, a, b, w, got, xs, gain, dhidden)


def rope_tables(length):
    positions = lax.optimization_barrier(jnp.arange(length, dtype=jnp.int32))
    frequency = ROPE_BASE ** (-jnp.arange(0, HD, 2).astype(F32) / HD)
    angles = positions.astype(F32)[:, None] * frequency[None, :]
    cos, sin = jnp.cos(angles), jnp.sin(angles)
    return jnp.concatenate([cos] * 4, axis=1), jnp.concatenate([-sin, sin] * 2, axis=1)


def tie(*values):
    return lax.optimization_barrier(values)


def rms(z):
    return lax.rsqrt(jnp.mean(z * z, axis=-1, keepdims=True) + EPS)


def norm_back(z, scale, gain, dn):
    zr = z * scale
    gdn = gain * dn
    return scale * (gdn - zr * jnp.mean(zr * gdn, axis=-1, keepdims=True))


def on_device(layer_input, cotangent, attn_gain, query_weight, key_weight, value_weight, query_gain, key_gain,
              out_weight, ffn_gain, gate_weight, up_weight, down_weight):
    n_dp, n_ctx, n_tensor = (lax.axis_size(a) for a in ("dp", "ctx", "tensor"))
    seqs, local_len, width = layer_input.shape
    assert seqs == 2 and n_tensor == 4
    chunk = local_len // 2
    length = local_len * n_ctx
    t = lax.axis_index("tensor")
    seq, core = t // 2, t % 2
    ctx = lax.axis_index("ctx")

    def own_chunk(place, which):
        return jnp.where(place % 2 == which, place, 2 * n_ctx - 1 - place)

    id_here, id_there = own_chunk(ctx, core), own_chunk(ctx, 1 - core)
    ids = jnp.stack([id_here, id_there]).astype(jnp.int32)

    def swap_core(x):
        return lax.ppermute(x, "tensor", [(i, i ^ 1) for i in range(n_tensor)])

    def swap_seq(x):
        return lax.ppermute(x, "tensor", [(i, i ^ 2) for i in range(n_tensor)])

    def swap_ctx(x):
        return lax.ppermute(x, "ctx", [(0, 1), (1, 0)])

    homes = []
    for place in range(n_ctx):
        for i in range(n_tensor):
            which = place if place % 2 == i % 2 else 2 * n_ctx - 1 - place
            homes.append((place * n_tensor + i, (which // 2) * n_tensor + i))

    def send_home(x):
        return lax.ppermute(x, ("ctx", "tensor"), homes)

    def fetch_from_home(x):
        return lax.ppermute(x, ("ctx", "tensor"), [(b, a) for a, b in homes])

    x_here = lax.dynamic_index_in_dim(layer_input, seq, 0, keepdims=False)
    if n_ctx == 2:
        first = swap_ctx(lax.dynamic_slice(layer_input, (seq, core * chunk, 0), (1, chunk, width))[0])
        second = swap_core(first)
        xs = jnp.zeros((length, width), BF)
        xs = lax.dynamic_update_slice(xs, x_here, (ctx * local_len, 0))
        xs = lax.dynamic_update_slice(xs, first, ((1 - ctx) * local_len + core * chunk, 0))
        xs = lax.dynamic_update_slice(xs, second, ((1 - ctx) * local_len + (1 - core) * chunk, 0))
    else:
        xs = lax.all_gather(x_here, "ctx", axis=0, tiled=True)

    d_part, h_part = attn_gain.shape[0], query_gain.shape[0]
    nq, nk = query_weight.shape[1], key_weight.shape[1]
    n_qkv = nq + 2 * nk
    gains = jnp.concatenate([attn_gain, ffn_gain, query_gain, key_gain])
    gain_rows = -(-gains.shape[0] // LANES)
    gains = jnp.pad(gains, (0, gain_rows * LANES - gains.shape[0])).reshape(gain_rows, LANES)
    gains = jnp.pad(gains, ((0, d_part - gain_rows), (0, 0)))
    piece = jnp.concatenate([query_weight, key_weight, value_weight, gains], axis=1)
    dp = lax.axis_index("dp")
    w_all = jnp.zeros((width, 2 * n_qkv), BF)
    gains = jnp.zeros((n_dp, gain_rows, LANES), BF)
    for hop in range(n_dp):
        owner = (dp + n_dp - hop) % n_dp
        w_all = lax.dynamic_update_slice(w_all, piece[:, :n_qkv], (owner * d_part, 0))
        theirs = swap_seq(piece[:, :n_qkv])
        w_all = lax.dynamic_update_slice(w_all, theirs, (owner * d_part, n_qkv))
        gains = lax.dynamic_update_slice(gains, piece[None, :gain_rows, n_qkv:], (owner, 0, 0))
        if hop < n_dp - 1:
            piece = lax.ppermute(piece, "dp", [(i, (i + 1) % n_dp) for i in range(n_dp)])
    gains = gains.reshape(n_dp, gain_rows * LANES)
    gain_a = gains[:, :d_part].reshape(1, width).astype(F32)
    gain_f = gains[:, d_part:2 * d_part].reshape(1, width).astype(F32)
    gain_q = jnp.tile(gains[:, 2 * d_part:2 * d_part + h_part].reshape(1, HD).astype(F32), (1, 2))
    gain_k = jnp.tile(gains[:, 2 * d_part + h_part:2 * d_part + 2 * h_part].reshape(1, HD).astype(F32), (1, 2))

    def half_rows(w):
        rows = w.shape[0] // 2
        return lax.dynamic_slice_in_dim(w, ctx * rows, rows, 0) if n_ctx == 2 else w

    def gather_dp(w):
        return lax.all_gather(w, "dp", axis=0, tiled=False)

    h_out = out_weight.shape[0]
    got = gather_dp(jnp.concatenate([out_weight, half_rows(down_weight)], axis=0))
    out_mine = got[:, :h_out].transpose(1, 0, 2).reshape(h_out, width)
    out_theirs = swap_seq(out_mine)
    down = [got[:, h_out:]]
    gate = [gather_dp(half_rows(gate_weight))]
    up = [gather_dp(up_weight)]
    if n_ctx == 2:
        down.append(swap_ctx(down[0]))

    cot_home = lax.dynamic_slice(cotangent, (seq, core * chunk, 0), (1, chunk, width))[0]
    dy_0 = fetch_from_home(cot_home)
    dy_2 = swap_seq(dy_0)
    dy_02 = jnp.stack([dy_0, dy_2])
    dy_13 = swap_core(dy_02)
    dy_own, dy_other = [dy_0, dy_13[0]], [dy_2, dy_13[1]]

    tb, big = min(256, chunk), min(512, chunk)
    cos, sin = rope_tables(length)
    normed, z, q, k, v = project(xs, gain_a, w_all, cos, sin, gain_q, gain_k, 2 * nq, 2 * nk, big)
    if n_ctx == 2:
        q, down[1], gate[0] = tie(q, down[1], gate[0])
        gate.append(swap_ctx(gate[0]))
    o, lse = attend(ids, q, k, v, chunk)
    if n_ctx == 2:
        o, gate[1], out_theirs = tie(o, gate[1], out_theirs)
    attn_give, attn_keep = out_project(jnp.reshape(id_here, (1,)), o, out_mine, out_theirs, xs, chunk)
    got = swap_core(attn_give)
    hidden = attn_keep + got.astype(F32)
    h_scale = rms(hidden)
    hn_0 = (hidden * h_scale * gain_f).astype(BF)
    hn_1 = swap_core(hn_0)
    hn_2 = swap_seq(hn_0)

    place = jnp.reshape(ctx, (1,)).astype(jnp.int32)

    def added(a, b):
        return (a.astype(F32) + b.astype(F32)).astype(BF)

    act_o, dg_o, du_o, y_0, y_1, dhn_0, dhn_1 = feed(place, [hn_0, hn_1], dy_own, gate, up, down, tb)
    act_o, hn_2 = tie(act_o, hn_2)
    hn_3 = swap_core(hn_2)
    act_t, dg_t, du_t, y_2, y_3, dhn_2, dhn_3 = feed(place, [hn_2, hn_3], dy_other, gate, up, down, tb)
    dhn_send = added(dhn_2, swap_core(dhn_3))
    dhn_got = swap_seq(dhn_send)

    def weight_sum(lefts, rights):
        if n_ctx == 2:
            return weight_grad(place, lefts, rights, n_dp)
        return None, mm(jnp.concatenate(lefts, axis=0), jnp.concatenate(rights, axis=0), TN).astype(BF)

    def to_ctx(give, keep):
        return swap_ctx(give) if n_ctx == 2 else keep[:1]

    def ctx_sum(keep, got):
        return added(keep, got) if n_ctx == 2 else keep

    def scatter(half):
        if n_ctx == 2:
            return lax.psum_scatter(half, "dp", scatter_dimension=0, tiled=False)
        return lax.psum_scatter(half, ("dp", "ctx"), scatter_dimension=0, tiled=True)

    def across(mine):
        return swap_ctx(mine) if n_ctx == 2 else None

    def gather_rows(mine, other):
        if n_ctx != 2:
            return lax.all_gather(mine, "ctx", axis=0, tiled=False).reshape(width // n_dp, mine.shape[-1])
        mine, other = mine.reshape(-1, mine.shape[-1]), other.reshape(-1, mine.shape[-1])
        return jnp.where(ctx == 0, jnp.concatenate([mine, other]), jnp.concatenate([other, mine]))

    hn_all, dy_all = [hn_0, hn_1, hn_2, hn_3], dy_own + dy_other
    act_t, dg_t, du_t, dhn_send = tie(act_t, dg_t, du_t, dhn_send)
    give, g_gate = weight_sum(hn_all, [dg_o, dg_t])
    gate_got = to_ctx(give, g_gate)
    du_o, g_gate = tie(du_o, g_gate)
    give, g_up = weight_sum(hn_all, [du_o, du_t])
    up_got = to_ctx(give, g_up)
    act_o, g_up = tie(act_o, g_up)
    give, g_down = weight_sum(dy_all, [act_o, act_t])
    dhn_got, g_down, gate_got = tie(dhn_got, g_down, gate_got)
    down_got = to_ctx(give, g_down)

    y_send, dhn_got = tie(added(y_2, swap_core(y_3)), dhn_got)
    y_got = swap_seq(y_send)
    dhn = dhn_0.astype(F32) + swap_core(dhn_1).astype(F32) + dhn_got.astype(F32)
    dhidden = dy_0.astype(F32) + norm_back(hidden, h_scale, gain_f, dhn)
    dhr_0 = dhidden.astype(BF)
    dhr_1 = swap_core(dhr_0)
    do = out_back(dhr_0, dhr_1, out_mine, out_theirs)

    def ordinal(s, c):
        return 2 * s + c

    blocks = jnp.stack([ordinal(seq, core), ordinal(seq, 1 - core), ordinal(1 - seq, core), ordinal(1 - seq, 1 - core)])
    blocks = blocks.astype(jnp.int32)

    do, gate_got = tie(do, gate_got)
    s_gate = scatter(ctx_sum(g_gate, gate_got))
    dq, dk, dv = attend_back(ids, q, k, v, o, do, lse, chunk, 1)
    dq, up_got, y_got = tie(dq, up_got, y_got)
    s_up = scatter(ctx_sum(g_up, up_got))
    total = hidden + (y_0.astype(F32) + swap_core(y_1).astype(F32) + y_got.astype(F32))
    total = send_home(total.astype(BF))
    d_theirs, gains_theirs = turn_back(ids, z, dq, dk, dv, cos, sin, gain_q, gain_k, big, chunk, 1)
    give_theirs, keep_theirs = weight_sum([normed], [d_theirs])
    dhr_0, keep_theirs = tie(dhr_0, keep_theirs)
    out_give, out_keep = weight_sum([dhr_0, dhr_1], [o])
    do, out_keep, down_got, s_gate = tie(do, out_keep, down_got, s_gate)
    gate_other = across(s_gate)
    out_both = jnp.concatenate([out_give, out_keep], axis=0) if n_ctx == 2 else out_keep
    out_got = swap_seq(out_both[..., h_out:])
    s_down = scatter(ctx_sum(g_down, down_got))
    qkv_got = swap_seq(jnp.concatenate([give_theirs, keep_theirs], axis=0) if n_ctx == 2 else keep_theirs)
    dq, dk, dv = attend_back(ids, q, k, v, o, do, lse, chunk, 0)
    dq, out_got, total, gate_other, s_up = tie(dq, out_got, total, gate_other, s_up)
    up_other = across(s_up)
    g_out = added(out_both[..., :h_out], out_got)
    out_got = to_ctx(g_out[:n_dp], g_out)
    total_core, total_seq = swap_core(total), swap_seq(total)
    d_mine, gains_mine = turn_back(ids, z, dq, dk, dv, cos, sin, gain_q, gain_k, big, chunk, 0)

    d_mine, up_other, s_down, out_got, qkv_got = tie(d_mine, up_other, s_down, out_got, qkv_got)
    s_out = scatter(ctx_sum(g_out[n_dp:], out_got) if n_ctx == 2 else g_out)
    give, keep = weight_sum([normed], [d_mine])
    fold = (gains_mine + gains_theirs)[:2]
    fold = (fold[:, :HD] + fold[:, HD:]).reshape(2, n_dp, h_part)
    fold = jnp.pad(fold, ((0, 0), (0, 0), (0, d_part - h_part))).reshape(2, width)
    fold = jnp.concatenate([fold, jnp.zeros((LANES - 2, width), F32)], axis=0).astype(BF).T
    if n_ctx == 2:
        fold = fold.reshape(n_dp, 2, -1, LANES)
        fold_give, fold_keep = [lax.dynamic_index_in_dim(fold, at, 1, keepdims=False) for at in (1 - ctx, ctx)]
        give = jnp.concatenate([added(give, qkv_got[:n_dp]), fold_give], axis=-1)
        keep = jnp.concatenate([added(keep, qkv_got[n_dp:]), fold_keep], axis=-1)
    else:
        keep = jnp.concatenate([added(keep, qkv_got), fold], axis=-1)
    d_mine, give, keep = tie(d_mine, give, keep)
    qkv_got = to_ctx(give, keep)
    parity = jnp.reshape(1 - core, (1,)).astype(jnp.int32)
    partial = unproject(parity, d_mine, d_theirs, w_all, big, chunk)
    got = swap_core(partial)
    total, _ = tie(total, partial)
    out_low = put(blocks[:2], [total, total_core], None, BF, 4 * chunk)
    d_mine, got, out_low = tie(d_mine, got, out_low)
    where = jnp.stack([core, id_here // 2]).astype(jnp.int32)
    dz = close(where, d_mine, d_theirs, w_all, got, xs, gain_a, dhidden, tb, chunk)
    dz = dz.reshape(n_ctx, chunk, width)
    if n_ctx == 2:
        rows = chunk // 2
        sent = [lax.dynamic_slice(dz, (1 - ctx, at, 0), (1, rows, width))[0] for at in (0, rows)]
        kept = [lax.dynamic_slice(dz, (ctx, at, 0), (1, rows, width))[0] for at in (0, rows)]
        dx_got = swap_ctx(sent[0])
        dx_last = swap_ctx(sent[1])
    else:
        dx_got = lax.psum_scatter(dz, "ctx", scatter_dimension=0, tiled=False)

    qkv_got, gate_other, up_other, _ = tie(qkv_got, gate_other, up_other, dz)
    s_qkv = scatter(ctx_sum(keep, qkv_got))
    gate_grad, up_grad = gather_rows(s_gate, gate_other).astype(F32), gather_rows(s_up, up_other).astype(F32)
    ffn_sum = jnp.sum(gate_weight.astype(F32) * gate_grad, axis=1) + jnp.sum(up_weight.astype(F32) * up_grad, axis=1)
    dx_got, s_qkv, s_out, total_seq, gate_grad, up_grad, ffn_sum = tie(dx_got, s_qkv, s_out, total_seq, gate_grad, up_grad, ffn_sum)
    total_both = swap_core(total_seq)
    if n_ctx == 2:
        dx_first = added(kept[0], dx_got)
        first_seq = swap_seq(dx_first)
        dx_first, dx_last = tie(dx_first, dx_last)
        dx = [dx_first, added(kept[1], dx_last)]
        dx_seq = [first_seq, swap_seq(dx[1])]
    else:
        dx = [dx_got]
        dx_seq = [swap_seq(dx_got)]
    dx_core = [swap_core(part) for part in dx]
    s_down, s_qkv, s_out, dx[-1] = tie(s_down, s_qkv, s_out, dx[-1])

    def parts_of(pair):
        return jnp.stack([len(dx) * pair[i] + n for i in range(2) for n in range(len(dx))])

    in_low = put(parts_of(blocks[:2]), dx + dx_core, None, F32, 4 * chunk)
    layer_output = put(blocks[2:], [total_seq, total_both], out_low, BF, 4 * chunk).reshape(2, local_len, width)
    qkv_other, down_other, out_other = across(s_qkv), across(s_down), across(s_out)
    qkv_other, in_low, layer_output = tie(qkv_other, in_low, layer_output)
    g = gather_rows(s_qkv, qkv_other).astype(F32)
    query_grad, key_grad, value_grad = g[:, :nq], g[:, nq:nq + nk], g[:, nq + nk:n_qkv]

    attn_sum = jnp.sum(query_weight.astype(F32) * query_grad, axis=1) + jnp.sum(key_weight.astype(F32) * key_grad, axis=1)
    attn_sum += jnp.sum(value_weight.astype(F32) * value_grad, axis=1)
    small = jnp.concatenate([attn_sum / attn_gain.astype(F32), ffn_sum / ffn_gain.astype(F32), g[:h_part, n_qkv], g[:h_part, n_qkv + 1]])
    small = small + swap_core(small)
    small, down_other, out_other = tie(small, down_other, out_other)
    small = small + swap_seq(small)
    down_grad = gather_rows(s_down, down_other).T.astype(F32)
    out_grad = gather_rows(s_out, out_other).T.astype(F32)
    dx_seq[-1], in_low, layer_output, down_grad, out_grad = tie(dx_seq[-1], in_low, layer_output, down_grad, out_grad)
    dx_both = [swap_core(part) for part in dx_seq]
    input_grad = put(parts_of(blocks[2:]), dx_seq + dx_both, in_low, F32, 4 * chunk).reshape(2, local_len, width)
    attn_gain_grad, ffn_gain_grad = small[:d_part], small[d_part:2 * d_part]
    qgain_grad, kgain_grad = small[2 * d_part:2 * d_part + h_part], small[2 * d_part + h_part:]

    return (layer_output, input_grad, attn_gain_grad, query_grad, key_grad, value_grad, qgain_grad, kgain_grad,
            out_grad, ffn_gain_grad, gate_grad, up_grad, down_grad)


def solution(mesh):
    token = P("dp", "ctx", None)
    into, out_of, vector = P("dp", "tensor"), P("tensor", "dp"), P("dp")
    return jax.shard_map(
        on_device,
        mesh=mesh,
        in_specs=(token, token, vector, into, into, into, vector, vector, out_of, vector, into, into, out_of),
        out_specs=(token, token, vector, into, into, into, vector, vector, out_of, vector, into, into, out_of),
        check_vma=False,
    )
```
